128 devices in a mesh: gx: 8 (over z_hi, y), gy: 8 (over x, z_lo), gz: 2 (over core).
Axes of the slice: x: 4, y: 4, z: 4 (z_hi: 2, z_lo: 2; z = z_hi * 2 + z_lo), core: 2. Of those that a mesh axis runs over, the one named last changes fastest.
Arguments:
- diag_blocks: bfloat16 [8, 32, 4, 128, 128], P('gx', 'gy', 'gz'), as said below
- face_blocks: bfloat16 [6, 8, 32, 4, 128, 128], P(None, 'gx', 'gy', 'gz'), may hold values from -1.796875 to 1.796875
- split: int32 [8, 32, 4], P('gx', 'gy', 'gz'), may hold values from 0 to 1, as said below
Outputs:
- interp: bfloat16 [6, 8, 32, 4, 128, 128], P(None, 'gx', 'gy', 'gz')
- coarse: float32 [8, 32, 4, 128, 128], P('gx', 'gy', 'gz')
The draws below stay inside these ranges and needn't reach their ends.
Inputs may be any that keep to these rules, and one draw needn't show every extreme that they name: `diag_blocks`: symmetric positive definite blocks. `split`: along the third dimension no two adjacent elements both have value 0, so every fine element has a coarse face neighbour.
All inputs are finite; a program needn't handle non-finite values.
Results may differ from the reference program's by a relative error of at most 0.00042.
Values may be sent and summed in bfloat16 or wider, within the bound.
No kernel may reach another device: no remote copies, remote signals or barrier semaphores. Data moves between devices by JAX's collectives and lax.ppermute only.
A program may use at most 128 MiB of HBM per device.

```python
import math
import jax
import jax.numpy as jnp
from jax import lax

B = 128
NX = 8
NY = 32
NZ = 4


def draw_diag_blocks(key, part):
    first = jax.random.fold_in(key, 11)
    second = jax.random.fold_in(key, 12)
    base = jax.random.normal(first, (NX, NY, NZ, B, B), jnp.float32)
    gram = jnp.einsum('xyzab,xyzcb->xyzac', base, base, precision=lax.Precision.HIGHEST) / B
    gram = gram + 2.0 * jnp.eye(B, dtype=jnp.float32)
    upper = 0.5 * math.log(10.0)
    scales = jnp.exp(jax.random.uniform(second, (NX, NY, NZ, B), jnp.float32, 0.0, upper))
    matrix = scales[..., :, None] * gram * scales[..., None, :]
    matrix = 0.5 * (matrix + jnp.swapaxes(matrix, -1, -2))
    return matrix.astype(jnp.bfloat16)


def draw_split(key, part):
    first = jax.random.fold_in(key, 21)
    second = jax.random.fold_in(key, 22)
    parity = jax.random.randint(first, (NX, NY, 1), 0, 2)
    depth = lax.broadcasted_iota(jnp.int32, (NX, NY, NZ), 2)
    across = lax.broadcasted_iota(jnp.int32, (NX, NY, NZ), 0)
    level = 1 + 6 * across // NX
    extra = jax.random.randint(second, (NX, NY, NZ), 0, 8) < level
    return jnp.where((depth % 2 == parity) | extra, 1, 0).astype(jnp.int32)


def level_of(key, dims, pieces, low, high):
    loudness, own = 1.0, jax.random.fold_in(key, 6)
    for position, shards_of in pieces:
        draws = jnp.exp(jax.random.uniform(jax.random.fold_in(own, position), (shards_of,), jnp.float32, low / len(pieces), high / len(pieces)))
        loudness = loudness * jnp.repeat(draws, dims[position] // shards_of).reshape([-1 if axis == position else 1 for axis in range(len(dims))])
    return loudness


def bell_draw(key, dims, width, most, cuts=(), kind=jnp.bfloat16):
    values = jax.random.normal(key, dims, jnp.float32) * width
    if len(cuts) > 0:
        values = level_of(key, dims, cuts, -0.22, 0.18) * values
    return jnp.clip(values, min=-most, max=most).astype(kind)


def setup_inputs(seed: int = 0) -> dict:
    splits = jax.random.split(jax.random.key(seed), 4)
    return {
        "diag_blocks": draw_diag_blocks(jax.random.fold_in(splits[3], 71), 0),
        "face_blocks": bell_draw(splits[1], (6, NX, NY, NZ, B, B), 0.3, 1.796875, ((1, 8), (2, 8), (3, 2))),
        "split": draw_split(jax.random.fold_in(splits[3], 71), 0),
    }


def shifted(field, dimension, offset):
    size = field.shape[dimension]
    widths = [(0, 0)] * field.ndim
    widths[dimension] = (1, 1)
    padded = jnp.pad(field, widths)
    return lax.slice_in_dim(padded, 1 + offset, 1 + offset + size, axis=dimension)

def cho_apply(factor, right_side):
    forward = lax.linalg.triangular_solve(factor, right_side, left_side=True, lower=True)
    return lax.linalg.triangular_solve(factor, forward, left_side=True, lower=True, transpose_a=True)

def reference(diag_blocks, face_blocks, split):
    grid = split.shape
    dense = diag_blocks.astype(jnp.float32)
    diag_norm = jnp.sqrt(lax.optimization_barrier(jnp.sum(dense * dense, axis=(-2, -1))))
    is_coarse = split == 1
    total = jnp.zeros(grid, jnp.float32)
    denom = jnp.zeros(grid, jnp.float32)
    links = []
    for direction in range(6):
        dimension = direction // 2
        offset = 1 if direction % 2 else -1
        target = lax.broadcasted_iota(jnp.int32, grid, dimension) + offset
        present = (target >= 0) & (target < grid[dimension])
        face = face_blocks[direction].astype(jnp.float32)
        face_norm = jnp.sqrt(lax.optimization_barrier(jnp.sum(face * face, axis=(-2, -1))))
        other_norm = jnp.where(present, shifted(diag_norm, dimension, offset), 1.0)
        strength = jnp.where(present, face_norm / jnp.sqrt(diag_norm * other_norm), 0.0)
        linked = present & (shifted(split, dimension, offset) == 1)
        total = total + strength
        denom = denom + jnp.where(linked, strength, 0.0)
        links.append(linked)
    ratio = total / jnp.where(is_coarse, 1.0, denom)
    factor = jnp.linalg.cholesky(dense)
    interps = []
    contribs = []
    for direction in range(6):
        face = face_blocks[direction].astype(jnp.float32)
        weight = jnp.where(links[direction] & ~is_coarse, -ratio, 0.0)
        solved = cho_apply(factor, face)
        interp = (weight[..., None, None] * solved).astype(jnp.bfloat16)
        wide_interp = interp.astype(jnp.float32)
        mixed = jnp.einsum('xyzab,xyzbc->xyzac', dense, wide_interp, precision=lax.Precision.HIGHEST) + face
        contrib = jnp.einsum('xyzba,xyzbc->xyzac', wide_interp, mixed, precision=lax.Precision.HIGHEST)
        interps.append(interp)
        contribs.append(contrib.astype(jnp.bfloat16))
    summed = dense
    for direction in range(6):
        dimension = direction // 2
        offset = 1 if direction % 2 else -1
        other = direction ^ 1
        arrive_interp = shifted(interps[other], dimension, offset).astype(jnp.float32)
        arrive_contrib = shifted(contribs[other], dimension, offset).astype(jnp.float32)
        face = face_blocks[direction].astype(jnp.float32)
        summed = summed + arrive_contrib + jnp.einsum('xyzab,xyzbc->xyzac', face, arrive_interp, precision=lax.Precision.HIGHEST)
    coarse = jnp.where(is_coarse[..., None, None], summed, 0.0)
    return (jnp.stack(interps), coarse)
```

```python
import jax
import jax.numpy as jnp
from jax import lax
from jax.experimental import pallas as pl
from jax.experimental.pallas import tpu as pltpu
from jax.sharding import PartitionSpec as P

B = 128
F32 = jnp.float32
BF16 = jnp.bfloat16
VMEM = pl.BlockSpec(memory_space=pltpu.VMEM)
SMEM = pl.BlockSpec(memory_space=pltpu.SMEM)
LIMIT = 24 * 1024 * 1024


def mm(a, b):
    return jnp.dot(a, b, preferred_element_type=F32)


def mm32(a, b):
    return jnp.dot(a, b, preferred_element_type=F32, precision=lax.Precision.HIGHEST)


def mm_t(a, b):
    return lax.dot_general(a, b, (((0,), (0,)), ((), ())), preferred_element_type=F32)


def halves(x):
    hi = x.astype(BF16)
    return hi, (x - hi.astype(F32)).astype(BF16)


def thirds(x):
    hi = x.astype(BF16)
    rest = x - hi.astype(F32)
    mid = rest.astype(BF16)
    return hi, mid, (rest - mid.astype(F32)).astype(BF16)


def wide(x):
    return jnp.concatenate([x, x], axis=0)


def fine_of(split_ref, column):
    return jnp.where(split_ref[2 * column] == 0, 0, 1)


def block_norms(load, rows):
    for e in range(8):
        x = load(e).astype(F32)
        rows[pl.ds(e, 1), :] = jnp.sum(x * x, axis=0, keepdims=True)
    total = jnp.sum(rows[...], axis=1, keepdims=True)
    return jnp.broadcast_to(jnp.sqrt(total), (8, B))


def facts_kernel(split_ref, diag_ref, facts_ref, rows):
    facts_ref[pl.ds(0, 8), :] = block_norms(lambda e: diag_ref[e], rows)
    for e in range(8):
        facts_ref[pl.ds(8 + e, 1), :] = jnp.full((1, B), split_ref[e].astype(F32), F32)


def inverse_kernel(split_ref, diag_ref, face_ref, inv_ref, fnorm_ref, rows, work):
    cols = range(4)
    eye = (
        lax.broadcasted_iota(jnp.int32, (B, B), 0) == lax.broadcasted_iota(jnp.int32, (B, B), 1)
    )
    one = jnp.where(eye, 1.0, 0.0).astype(F32)
    mats = [diag_ref[2 * c + fine_of(split_ref, c)] for c in cols]
    scaled, starts, scales = [], [], []
    for c in cols:
        a = mats[c].astype(F32)
        picked = jnp.where(eye, a, 0.0)
        down = lax.rsqrt(jnp.sum(picked, axis=1, keepdims=True))
        along = lax.rsqrt(jnp.sum(picked, axis=0, keepdims=True))
        a = a * down * along
        bound = jnp.max(jnp.sum(jnp.abs(a), axis=0, keepdims=True), axis=1, keepdims=True)
        scaled.append(a)
        starts.append(1.9 / bound)
        scales.append((down, along))
    powers = [one - starts[c] * scaled[c] for c in cols]
    sums = [one + powers[c] for c in cols]
    powers = [p.astype(BF16) for p in powers]
    for _ in range(4):
        powers = [mm(p, p).astype(BF16) for p in powers]
        sums = [s + mm(s.astype(BF16), p) for s, p in zip(sums, powers)]
    guess = [
        (sums[c] * (starts[c] * scales[c][0]) * scales[c][1]).astype(BF16) for c in cols
    ]
    left = [one - mm(mats[c], guess[c]) for c in cols]
    small = [r.astype(BF16) for r in left]
    left = [r + mm(b, b) for r, b in zip(left, small)]
    better = []
    for c in cols:
        hi, lo = halves(left[c])
        better.append(guess[c].astype(F32) + (mm(guess[c], hi) + mm(guess[c], lo)))
    pairs = [halves(x) for x in better]
    left = [one - (mm(mats[c], pairs[c][0]) + mm(mats[c], pairs[c][1])) for c in cols]
    worst = jnp.zeros((1, B), F32)
    for c in cols:
        hi, lo = pairs[c]
        rhi, rlo = halves(left[c])
        fixed = (hi.astype(F32) + lo.astype(F32)) + (mm(hi, rhi) + (mm(hi, rlo) + mm(lo, rhi)))
        inv_ref[0, c], inv_ref[1, c], inv_ref[2, c] = thirds(fixed)
        worst = worst + jnp.sum(jnp.abs(left[c]), axis=0, keepdims=True)
    reached = jnp.max(worst) <= 1e-3

    @pl.when(jnp.logical_not(reached))
    def _():
        for c in cols:
            a = mats[c].astype(F32)
            picked = jnp.where(eye, a, 0.0)
            down = lax.rsqrt(jnp.sum(picked, axis=1, keepdims=True))
            along = lax.rsqrt(jnp.sum(picked, axis=0, keepdims=True))
            a = a * down * along
            bound = jnp.max(jnp.sum(jnp.abs(a), axis=0, keepdims=True), axis=1, keepdims=True)
            work[0] = a
            work[1] = one * (1.9 / bound)

            @pl.loop(0, 48)
            def _(_):
                x = work[1]
                work[1] = x + mm32(x, one - mm32(work[0], x))

            inv_ref[0, c], inv_ref[1, c], inv_ref[2, c] = thirds(work[1] * down * along)

    for d in range(6):
        fnorm_ref[d] = block_norms(lambda e: face_ref[d, e], rows)


def shifted(own, beyond, step, edge):
    return jnp.where(edge, pltpu.roll(beyond, step, 0), pltpu.roll(own, step, 0))


def weights_of(facts_ref, halo_refs, fnorm_ref, weight_ref):
    gx, gy, gz = lax.axis_index("gx"), lax.axis_index("gy"), lax.axis_index("gz")
    ha, hb, hc, hd, hz = halo_refs
    row = lax.broadcasted_iota(jnp.int32, (8, B), 0)
    depth = row % 2
    even_x, even_y = gx % 2 == 0, gy % 2 == 0

    def pick(test, first, second, part):
        rows = pl.ds(8 * part, 8)
        return jnp.where(test, first[rows, :], second[rows, :])

    def neighbours(part):
        own = facts_ref[pl.ds(8 * part, 8), :]
        z = hz[pl.ds(8 * part, 8), :]
        return (
            pick(even_x, hb, ha, part),
            pick(even_x, ha, hb, part),
            shifted(own, pick(even_y, hd, hc, part), 2, row < 2),
            shifted(own, pick(even_y, hc, hd, part), 6, row >= 6),
            jnp.where(depth == 0, pltpu.roll(z, 7, 0), pltpu.roll(own, 1, 0)),
            jnp.where(depth == 1, pltpu.roll(z, 1, 0), pltpu.roll(own, 7, 0)),
        )

    present = (
        jnp.broadcast_to(gx > 0, (8, B)),
        jnp.broadcast_to(gx < lax.axis_size("gx") - 1, (8, B)),
        (row >= 2) | (gy > 0),
        (row < 6) | (gy < lax.axis_size("gy") - 1),
        (depth == 1) | (gz > 0),
        (depth == 0) | (gz < lax.axis_size("gz") - 1),
    )
    own_norm = facts_ref[pl.ds(0, 8), :]
    fine = facts_ref[pl.ds(8, 8), :] < 0.5
    norms, splits = neighbours(0), neighbours(1)
    total = jnp.zeros((8, B), F32)
    denom = jnp.zeros((8, B), F32)
    links = []
    for d in range(6):
        other = jnp.where(present[d], norms[d], 1.0)
        strength = jnp.where(present[d], fnorm_ref[d] / jnp.sqrt(own_norm * other), 0.0)
        linked = present[d] & (splits[d] > 0.5)
        total = total + strength
        denom = denom + jnp.where(linked, strength, 0.0)
        links.append(linked)
    ratio = total / jnp.where(fine, denom, 1.0)
    for d in range(6):
        weight_ref[d] = jnp.where(links[d] & fine, -ratio, 0.0)


def interp_kernel(
    split_ref, diag_ref, face_ref, inv_ref, fnorm_ref, facts_ref, ha, hb, hc, hd, hz,
    interp_ref, near_ref, code_ref, xa_ref, xb_ref, ya_ref, yb_ref, z_ref, weight_ref,
):
    weights_of(facts_ref, (ha, hb, hc, hd, hz), fnorm_ref, weight_ref)
    gx, gy, gz = lax.axis_index("gx"), lax.axis_index("gy"), lax.axis_index("gz")
    row = lax.broadcasted_iota(jnp.int32, (8, B), 0)
    lane = lax.broadcasted_iota(jnp.int32, (8, B), 1)
    bit = jnp.where((row % 2 == 0) & (lane == 0), 1, 0) * lax.shift_left(1, row // 2)
    code = jnp.zeros((8, B), F32)
    for place, ref in enumerate((ha, hb, hc, hd)):
        code = code + ref[pl.ds(8, 8), :] * (bit * (1 << (4 * place))).astype(F32)
    code_ref[0] = jnp.sum(code).astype(jnp.int32)
    zero = jnp.zeros((B, B), BF16)
    for c in range(4):
        z = fine_of(split_ref, c)
        e = 2 * c + z
        a = diag_ref[e]
        inv = jnp.concatenate([inv_ref[0, c], inv_ref[1, c]], axis=1)
        last = inv_ref[2, c]
        for d in range(6):
            face = face_ref[d, e]
            solved = mm(inv, wide(face)) + mm(last, face)
            interp = (weight_ref[d, pl.ds(e, 1), :] * solved).astype(BF16)
            interp_ref[d, e] = interp
            interp_ref[d, 2 * c + 1 - z] = zero
            hi, lo = halves(mm(a, interp) + face.astype(F32))
            contrib = (mm_t(interp, hi) + mm_t(interp, lo)).astype(BF16)
            if d < 2:
                first = gx % 2 == 1 - d

                @pl.when(first)
                def _():
                    xa_ref[0, c], xa_ref[1, c] = interp, contrib

                @pl.when(jnp.logical_not(first))
                def _():
                    xb_ref[0, c], xb_ref[1, c] = interp, contrib
            elif d < 4:
                if c == (0, 3)[d - 2]:
                    first = gy % 2 == 3 - d

                    @pl.when(first)
                    def _():
                        ya_ref[0, 0], ya_ref[1, 0] = interp, contrib

                    @pl.when(jnp.logical_not(first))
                    def _():
                        yb_ref[0, 0], yb_ref[1, 0] = interp, contrib
                else:
                    near_ref[d - 2, c] = contrib
            else:
                inside = z == 5 - d

                @pl.when(inside)
                def _():
                    near_ref[2, c] = contrib

                @pl.when(jnp.logical_not(inside) & (gz == 5 - d))
                def _():
                    z_ref[0, c], z_ref[1, c] = interp, contrib

        @pl.when(z == gz)
        def _():
            z_ref[0, c], z_ref[1, c] = zero, zero


def coarse_kernel(
    split_ref, code_ref, diag_ref, face_ref, interp_ref, near_ref,
    xa_ref, xb_ref, ya_ref, yb_ref, z_ref, coarse_ref,
):
    gx, gy, gz = lax.axis_index("gx"), lax.axis_index("gy"), lax.axis_index("gz")
    code = code_ref[0]
    for e in range(8):
        coarse_ref[e] = diag_ref[e].astype(F32)

    def add(target, d, interp, contrib):
        coarse_ref[target] = coarse_ref[target] + (
            contrib.astype(F32) + mm(face_ref[d, target], interp)
        )

    def bit_at(place):
        return lax.shift_right_logical(code, place) & 1

    for c in range(4):
        add(2 * c + bit_at(c), jnp.where(gx % 2 == 0, 1, 0), xa_ref[0, c], xa_ref[1, c])
        add(2 * c + bit_at(4 + c), jnp.where(gx % 2 == 0, 0, 1), xb_ref[0, c], xb_ref[1, c])
        if c > 0:
            z = fine_of(split_ref, c - 1)
            add(2 * c + z, 2, interp_ref[3, 2 * (c - 1) + z], near_ref[1, c - 1])
        if c < 3:
            z = fine_of(split_ref, c + 1)
            add(2 * c + z, 3, interp_ref[2, 2 * (c + 1) + z], near_ref[0, c + 1])
        z = fine_of(split_ref, c)
        add(2 * c + 1 - z, 4 + z, interp_ref[5 - z, 2 * c + z], near_ref[2, c])
        add(2 * c + 1 - gz, 5 - gz, z_ref[0, c], z_ref[1, c])
    up = gy % 2 == 0
    code_a = jnp.where(up, bit_at(8), bit_at(11))
    code_b = jnp.where(up, bit_at(15), bit_at(12))
    add(jnp.where(up, 6, 0) + code_a, jnp.where(up, 3, 2), ya_ref[0, 0], ya_ref[1, 0])
    add(jnp.where(up, 0, 6) + code_b, jnp.where(up, 2, 3), yb_ref[0, 0], yb_ref[1, 0])
    for e in range(8):
        coarse_ref[e] = jnp.where(split_ref[e] == 1, coarse_ref[e], 0.0)


def matching(size, start):
    pairs = [(i, i + 1) for i in range(start, size - 1, 2)]
    return pairs + [(b, a) for a, b in pairs]


def swap(x, axis, start):
    return lax.ppermute(x, axis, matching(lax.axis_size(axis), start))


def call(body, out_shape, in_specs, out_specs, scratch, flops, name):
    return pl.pallas_call(
        body,
        out_shape=out_shape,
        in_specs=in_specs,
        out_specs=out_specs,
        scratch_shapes=scratch,
        compiler_params=pltpu.CompilerParams(vmem_limit_bytes=LIMIT),
        cost_estimate=pl.CostEstimate(flops=flops, bytes_accessed=2 << 20, transcendentals=0),
        name=name,
    )


def on_device(diag_blocks, face_blocks, split):
    diag = diag_blocks.reshape(8, B, B)
    face = face_blocks.reshape(6, 8, B, B)
    split = split.reshape(8)
    sds = jax.ShapeDtypeStruct
    facts = call(
        facts_kernel, sds((16, B), F32), [SMEM, VMEM], VMEM,
        [pltpu.VMEM((8, B), F32)], 1 << 20, "facts",
    )(split, diag)
    halo = (
        swap(facts, "gx", 0), swap(facts, "gx", 1),
        swap(facts, "gy", 0), swap(facts, "gy", 1), swap(facts, "gz", 0),
    )
    inv, fnorm = call(
        inverse_kernel, (sds((3, 4, B, B), BF16), sds((6, 8, B), F32)),
        [SMEM, VMEM, VMEM], (VMEM, VMEM),
        [pltpu.VMEM((8, B), F32), pltpu.VMEM((2, B, B), F32)], 1 << 30, "inverse",
    )(split, diag, face)
    blocks = lambda *lead: sds(lead + (B, B), BF16)
    interp, near, code, xa, xb, ya, yb, z = call(
        interp_kernel,
        (
            blocks(6, 8), blocks(3, 4), sds((1,), jnp.int32),
            blocks(2, 4), blocks(2, 4), blocks(2, 1), blocks(2, 1), blocks(2, 4),
        ),
        [SMEM] + [VMEM] * 10,
        (VMEM, VMEM, SMEM) + (VMEM,) * 5,
        [pltpu.VMEM((6, 8, B), F32)], 1 << 30, "interp",
    )(split, diag, face, inv, fnorm, facts, *halo)
    xa, xb = swap(xa, "gx", 0), swap(xb, "gx", 1)
    ya, yb = swap(ya, "gy", 0), swap(yb, "gy", 1)
    z = swap(z, "gz", 0)
    coarse = call(
        coarse_kernel, sds((8, B, B), F32), [SMEM, SMEM] + [VMEM] * 9, VMEM, [], 1 << 30, "coarse",
    )(split, code, diag, face, interp, near, xa, xb, ya, yb, z)
    return interp.reshape(face_blocks.shape), coarse.reshape(diag_blocks.shape)


def solution(mesh):
    in_specs = (
        P("gx", "gy", "gz", None, None),
        P(None, "gx", "gy", "gz", None, None),
        P("gx", "gy", "gz"),
    )
    out_specs = (P(None, "gx", "gy", "gz", None, None), P("gx", "gy", "gz", None, None))
    return jax.shard_map(
        on_device, mesh=mesh, in_specs=in_specs, out_specs=out_specs, check_vma=False
    )
```

```python
import jax
import jax.numpy as jnp
from jax import lax
from jax.experimental import pallas as pl
from jax.experimental.pallas import tpu as pltpu
from jax.sharding import PartitionSpec as P

B = 128
F32 = jnp.float32
BF16 = jnp.bfloat16
VMEM = pl.BlockSpec(memory_space=pltpu.VMEM)
SMEM = pl.BlockSpec(memory_space=pltpu.SMEM)
HBM = pl.BlockSpec(memory_space=pltpu.HBM)
LIMIT = 24 * 1024 * 1024


def mm(a, b):
    return jnp.dot(a, b, preferred_element_type=F32)


def mm32(a, b):
    return jnp.dot(a, b, preferred_element_type=F32, precision=lax.Precision.HIGHEST)


def halves(x):
    hi = x.astype(BF16)
    return hi, (x - hi.astype(F32)).astype(BF16)


def thirds(x):
    hi = x.astype(BF16)
    rest = x - hi.astype(F32)
    mid = rest.astype(BF16)
    return hi, mid, (rest - mid.astype(F32)).astype(BF16)


def wide(x):
    return jnp.concatenate([x, x], axis=0)


def split_at(split_ref, c, z):
    return split_ref[0, z, c]


def fine_of(split_ref, c):
    return jnp.where(split_at(split_ref, c, 0) == 0, 0, 1)


def square_sums(x):
    x = x.astype(F32)
    return jnp.sum(x * x, axis=0, keepdims=True)


def norms_of(rows):
    return jnp.broadcast_to(jnp.sqrt(jnp.sum(rows, axis=1, keepdims=True)), rows.shape)


def facts_kernel(split_ref, diag_ref, facts_ref, rows):
    for e in range(8):
        rows[pl.ds(e, 1), :] = square_sums(diag_ref[e])
        part = split_at(split_ref, e // 2, e % 2).astype(F32)
        facts_ref[pl.ds(8 + e, 1), :] = jnp.full((1, B), part, F32)
    facts_ref[pl.ds(0, 8), :] = norms_of(rows[...])


def scaling(a, eye):
    picked = jnp.where(eye, a, 0.0)
    down = lax.rsqrt(jnp.sum(picked, axis=1, keepdims=True))
    along = lax.rsqrt(jnp.sum(picked, axis=0, keepdims=True))
    a = a * down * along
    bound = jnp.max(jnp.sum(jnp.abs(a), axis=0, keepdims=True), axis=1, keepdims=True)
    return a, down, along, 1.9 / bound


def inverse_kernel(split_ref, diag_ref, face_ref, inv_ref, fnorm_ref, fine_ref, rows, work, sems):
    cols = range(4)
    copies = []
    for c in cols:
        e = 2 * c + fine_of(split_ref, c)
        for d in range(6):
            copies.append(
                pltpu.make_async_copy(face_ref.at[d, e], fine_ref.at[d, c], sems.at[6 * c + d])
            )
            copies[-1].start()
    eye = (
        lax.broadcasted_iota(jnp.int32, (B, B), 0) == lax.broadcasted_iota(jnp.int32, (B, B), 1)
    )
    one = jnp.where(eye, 1.0, 0.0).astype(F32)
    mats = [diag_ref[2 * c + fine_of(split_ref, c)] for c in cols]
    parts = [scaling(m.astype(F32), eye) for m in mats]
    powers = [one - start * a for a, _, _, start in parts]
    sums = [one + p for p in powers]
    powers = [p.astype(BF16) for p in powers]
    for _ in range(4):
        powers = [mm(p, p).astype(BF16) for p in powers]
        sums = [s + mm(s.astype(BF16), p) for s, p in zip(sums, powers)]
    guess = [
        (s * (start * down) * along).astype(BF16) for s, (_, down, along, start) in zip(sums, parts)
    ]
    left = [one - mm(mats[c], guess[c]) for c in cols]
    small = [r.astype(BF16) for r in left]
    left = [r + mm(b, b) for r, b in zip(left, small)]
    better = []
    for c in cols:
        hi, lo = halves(left[c])
        better.append(guess[c].astype(F32) + (mm(guess[c], hi) + mm(guess[c], lo)))
    pairs = [halves(x) for x in better]
    left = [one - (mm(mats[c], pairs[c][0]) + mm(mats[c], pairs[c][1])) for c in cols]
    worst = jnp.zeros((1, B), F32)
    for c in cols:
        hi, lo = pairs[c]
        rhi, rlo = halves(left[c])
        fixed = (hi.astype(F32) + lo.astype(F32)) + (mm(hi, rhi) + (mm(hi, rlo) + mm(lo, rhi)))
        inv_ref[0, c], inv_ref[1, c], inv_ref[2, c] = thirds(fixed)
        worst = worst + jnp.sum(jnp.abs(left[c]), axis=0, keepdims=True)
    for c in cols:
        for d in range(6):
            copies[6 * c + d].wait()
    for d in range(6):
        for c in cols:
            sums = square_sums(fine_ref[d, c])
            rows[pl.ds(8 * d + 2 * c, 1), :] = sums
            rows[pl.ds(8 * d + 2 * c + 1, 1), :] = sums
    fnorm_ref[...] = norms_of(rows[...])
    reached = jnp.max(worst) <= 1e-3

    @pl.when(jnp.logical_not(reached))
    def _():
        for c in cols:
            a, down, along, start = scaling(mats[c].astype(F32), eye)
            work[0] = a
            work[1] = one * start

            @pl.loop(0, 48)
            def _(_):
                x = work[1]
                work[1] = x + mm32(x, one - mm32(work[0], x))

            inv_ref[0, c], inv_ref[1, c], inv_ref[2, c] = thirds(work[1] * down * along)


def shifted(own, beyond, step, edge):
    return jnp.where(edge, pltpu.roll(beyond, step, 0), pltpu.roll(own, step, 0))


def weights_of(facts_ref, halo_refs, fnorm_ref, weight_ref):
    gx, gy, gz = lax.axis_index("gx"), lax.axis_index("gy"), lax.axis_index("gz")
    ha, hb, hc, hd, hz = halo_refs
    row = lax.broadcasted_iota(jnp.int32, (8, B), 0)
    depth = row % 2
    even_x, even_y = gx % 2 == 0, gy % 2 == 0

    def pick(test, first, second, part):
        rows = pl.ds(8 * part, 8)
        return jnp.where(test, first[rows, :], second[rows, :])

    def neighbours(part):
        own = facts_ref[pl.ds(8 * part, 8), :]
        z = hz[pl.ds(8 * part, 8), :]
        return (
            pick(even_x, hb, ha, part),
            pick(even_x, ha, hb, part),
            shifted(own, pick(even_y, hd, hc, part), 2, row < 2),
            shifted(own, pick(even_y, hc, hd, part), 6, row >= 6),
            jnp.where(depth == 0, pltpu.roll(z, 7, 0), pltpu.roll(own, 1, 0)),
            jnp.where(depth == 1, pltpu.roll(z, 1, 0), pltpu.roll(own, 7, 0)),
        )

    present = (
        jnp.broadcast_to(gx > 0, (8, B)),
        jnp.broadcast_to(gx < lax.axis_size("gx") - 1, (8, B)),
        (row >= 2) | (gy > 0),
        (row < 6) | (gy < lax.axis_size("gy") - 1),
        (depth == 1) | (gz > 0),
        (depth == 0) | (gz < lax.axis_size("gz") - 1),
    )
    own_norm = facts_ref[pl.ds(0, 8), :]
    fine = facts_ref[pl.ds(8, 8), :] < 0.5
    norms, splits = neighbours(0), neighbours(1)
    total = jnp.zeros((8, B), F32)
    denom = jnp.zeros((8, B), F32)
    links = []
    for d in range(6):
        other = jnp.where(present[d], norms[d], 1.0)
        strength = jnp.where(present[d], fnorm_ref[pl.ds(8 * d, 8), :] / jnp.sqrt(own_norm * other), 0.0)
        linked = present[d] & (splits[d] > 0.5)
        total = total + strength
        denom = denom + jnp.where(linked, strength, 0.0)
        links.append(linked)
    ratio = total / jnp.where(fine, denom, 1.0)
    for d in range(6):
        weight_ref[d] = jnp.where(links[d] & fine, -ratio, 0.0)


def interp_kernel(
    split_ref, diag_ref, fine_ref, inv_ref, fnorm_ref, facts_ref, ha, hb, hc, hd, hz,
    interp_ref, code_ref, xa_ref, xb_ref, ya_ref, yb_ref, z_ref, near_ref, inside_ref,
    weight_ref, mixed_ref, zero_ref, sems,
):
    zero_ref[...] = jnp.zeros((B, B), BF16)
    gx, gy = lax.axis_index("gx"), lax.axis_index("gy")
    fines = [fine_of(split_ref, c) for c in range(4)]
    weights_of(facts_ref, (ha, hb, hc, hd, hz), fnorm_ref, weight_ref)
    copies = []

    def send(block, d, e):
        copies.append(pltpu.make_async_copy(block, interp_ref.at[d, e], sems.at[len(copies)]))
        copies[-1].start()

    def slots(c):
        return (
            (1 - gx % 2, xa_ref.at[0, c], xa_ref.at[1, c]),
            (gx % 2, xb_ref.at[0, c], xb_ref.at[1, c]),
            (2, near_ref.at[0, 0, c], near_ref.at[0, 1, c]),
            (3, near_ref.at[1, 0, c], near_ref.at[1, 1, c]),
            (5 - fines[c], inside_ref.at[0, c], inside_ref.at[1, c]),
            (4 + fines[c], z_ref.at[0, c], z_ref.at[1, c]),
        )

    def send_column(c):
        for d, interp, _ in slots(c):
            send(interp, d, 2 * c + fines[c])

    for c in range(4):
        e = 2 * c + fines[c]
        inv = jnp.concatenate([inv_ref[0, c], inv_ref[1, c]], axis=1)
        last = inv_ref[2, c]
        here = slots(c)
        for s in (0, 2, 4):
            two = [here[s], here[s + 1]]
            face = jnp.concatenate([fine_ref[d, c] for d, _, _ in two], axis=1)
            weight = jnp.concatenate([weight_ref[d, pl.ds(e, 1), :] for d, _, _ in two], axis=1)
            interp = (weight * (mm(inv, wide(face)) + mm(last, face))).astype(BF16)
            two[0][1][...] = interp[:, :B]
            two[1][1][...] = interp[:, B:]
        for d in range(6):
            send(zero_ref, d, 2 * c + 1 - fines[c])
        if c > 0:
            send_column(c - 1)
    row = lax.broadcasted_iota(jnp.int32, (8, B), 0)
    lane = lax.broadcasted_iota(jnp.int32, (8, B), 1)
    bit = jnp.where((row % 2 == 0) & (lane == 0), 1, 0) * lax.shift_left(1, row // 2)
    code = jnp.zeros((8, B), F32)
    for place, ref in enumerate((ha, hb, hc, hd)):
        code = code + ref[pl.ds(8, 8), :] * (bit * (1 << (4 * place))).astype(F32)
    code_ref[0] = jnp.sum(code).astype(jnp.int32)
    for c in range(4):
        a = diag_ref[2 * c + fines[c]]
        here = slots(c)
        for s in (0, 2, 4):
            two = [here[s], here[s + 1]]
            face = jnp.concatenate([fine_ref[d, c] for d, _, _ in two], axis=1)
            interp = jnp.concatenate([block[...] for _, block, _ in two], axis=1)
            hi, lo = halves(mm(a, interp) + face.astype(F32))
            for t in range(2):
                lanes = slice(B * t, B * t + B)
                mixed_ref[c, s + t, pl.ds(0, B), :] = hi[:, lanes]
                mixed_ref[c, s + t, pl.ds(B, B), :] = lo[:, lanes]
        if c == 1:
            send_column(3)
    for c in range(4):
        for s, (_, interp, contrib) in enumerate(slots(c)):
            turned = jnp.transpose(interp[...])
            both = jnp.concatenate([turned, turned], axis=1)
            contrib[...] = mm(both, mixed_ref[c, s]).astype(BF16)
    up = gy % 2 == 0
    for k in range(2):
        low, high = near_ref[0, k, 0], near_ref[1, k, 3]
        ya_ref[k, 0] = jnp.where(up, high, low)
        yb_ref[k, 0] = jnp.where(up, low, high)
    for copy in copies:
        copy.wait()


def near_kernel(
    split_ref, code_ref, diag_ref, face_ref, near_ref, inside_ref,
    sum_ref, far_ref, held_ref, sems,
):
    gx, gy, gz = lax.axis_index("gx"), lax.axis_index("gy"), lax.axis_index("gz")
    fines = [fine_of(split_ref, c) for c in range(4)]
    local = []
    for c in range(4):
        if c > 0:
            local.append((2 * c + fines[c - 1], 2, near_ref.at[1, 0, c - 1], near_ref.at[1, 1, c - 1]))
        if c < 3:
            local.append((2 * c + fines[c + 1], 3, near_ref.at[0, 0, c + 1], near_ref.at[0, 1, c + 1]))
        local.append((2 * c + 1 - fines[c], 4 + fines[c], inside_ref.at[0, c], inside_ref.at[1, c]))
    copies = []

    def fetch(target, d, into):
        copies.append(pltpu.make_async_copy(face_ref.at[d, target], into, sems.at[len(copies)]))
        copies[-1].start()

    for k, (target, d, _, _) in enumerate(local):
        fetch(target, d, held_ref.at[k])
    for k, (target, d) in enumerate(far_targets(code_ref[0], gx, gy, gz)):
        fetch(target, d, far_ref.at[k])
    for e in range(8):
        sum_ref[e] = diag_ref[e].astype(F32)
    for copy in copies:
        copy.wait()
    for k, (target, _, interp, contrib) in enumerate(local):
        sum_ref[target] = sum_ref[target] + (contrib[...].astype(F32) + mm(held_ref[k], interp[...]))


def far_targets(code, gx, gy, gz):
    def bit_at(place):
        return lax.shift_right_logical(code, place) & 1

    up = gy % 2 == 0
    found = [(2 * c + bit_at(c), 1 - gx % 2) for c in range(4)]
    found += [(2 * c + bit_at(4 + c), gx % 2) for c in range(4)]
    code_a = jnp.where(up, bit_at(8), bit_at(11))
    code_b = jnp.where(up, bit_at(15), bit_at(12))
    found.append((jnp.where(up, 6, 0) + code_a, jnp.where(up, 3, 2)))
    found.append((jnp.where(up, 0, 6) + code_b, jnp.where(up, 2, 3)))
    return found + [(2 * c + 1 - gz, 5 - gz) for c in range(4)]


def coarse_kernel(
    split_ref, code_ref, sum_ref, far_ref, xa_ref, xb_ref, ya_ref, yb_ref, z_ref, coarse_ref
):
    gx, gy, gz = lax.axis_index("gx"), lax.axis_index("gy"), lax.axis_index("gz")
    arrived = [(ref, c) for ref in (xa_ref, xb_ref) for c in range(4)]
    arrived += [(ya_ref, 0), (yb_ref, 0)] + [(z_ref, c) for c in range(4)]
    for e in range(8):
        coarse_ref[e] = sum_ref[e]
    targets = far_targets(code_ref[0], gx, gy, gz)
    for k, ((target, _), (ref, c)) in enumerate(zip(targets, arrived)):
        coarse_ref[target] = coarse_ref[target] + (
            ref[1, c].astype(F32) + mm(far_ref[k], ref[0, c])
        )
    for e in range(8):
        keep = split_at(split_ref, e // 2, e % 2) == 1
        coarse_ref[e] = jnp.where(keep, coarse_ref[e], 0.0)


def matching(size, start):
    pairs = [(i, i + 1) for i in range(start, size - 1, 2)]
    return pairs + [(b, a) for a, b in pairs]


def swap(x, axis, start):
    return lax.ppermute(x, axis, matching(lax.axis_size(axis), start))


def call(body, out_shape, in_specs, out_specs, scratch, flops, name):
    return pl.pallas_call(
        body,
        out_shape=out_shape,
        in_specs=in_specs,
        out_specs=out_specs,
        scratch_shapes=scratch,
        compiler_params=pltpu.CompilerParams(vmem_limit_bytes=LIMIT),
        cost_estimate=pl.CostEstimate(flops=flops, bytes_accessed=2 << 20, transcendentals=0),
        name=name,
    )


def on_device(diag_blocks, face_blocks, split):
    diag = diag_blocks.reshape(8, B, B)
    face = face_blocks.reshape(6, 8, B, B)
    split = jnp.transpose(split, (0, 2, 1))
    sds = jax.ShapeDtypeStruct
    dma = pltpu.SemaphoreType.DMA
    facts = call(
        facts_kernel, sds((16, B), F32), [SMEM, VMEM], VMEM,
        [pltpu.VMEM((8, B), F32)], 1 << 20, "facts",
    )(split, diag)
    halo = (
        swap(facts, "gx", 0), swap(facts, "gx", 1),
        swap(facts, "gy", 0), swap(facts, "gy", 1), swap(facts, "gz", 0),
    )
    blocks = lambda *lead: sds(lead + (B, B), BF16)
    inv, fnorm, fine = call(
        inverse_kernel, (blocks(3, 4), sds((48, B), F32), blocks(6, 4)),
        [SMEM, VMEM, HBM], (VMEM, VMEM, VMEM),
        [pltpu.VMEM((48, B), F32), pltpu.VMEM((2, B, B), F32), dma((24,))], 1 << 30, "inverse",
    )(split, diag, face)
    interp, code, xa, xb, ya, yb, z, near, inside = call(
        interp_kernel,
        (
            blocks(6, 8), sds((1,), jnp.int32), blocks(2, 4), blocks(2, 4), blocks(2, 1),
            blocks(2, 1), blocks(2, 4), blocks(2, 2, 4), blocks(2, 4),
        ),
        [SMEM] + [VMEM] * 10,
        (HBM, SMEM) + (VMEM,) * 7,
        [
            pltpu.VMEM((6, 8, B), F32), pltpu.VMEM((4, 6, 2 * B, B), BF16),
            pltpu.VMEM((B, B), BF16), dma((48,)),
        ],
        1 << 30, "interp",
    )(split, diag, fine, inv, fnorm, facts, *halo)
    xa, xb = swap(xa, "gx", 0), swap(xb, "gx", 1)
    ya, yb = swap(ya, "gy", 0), swap(yb, "gy", 1)
    z = swap(z, "gz", 0)
    total, far = call(
        near_kernel, (sds((8, B, B), F32), blocks(14)),
        [SMEM, SMEM, VMEM, HBM, VMEM, VMEM], (VMEM, VMEM),
        [pltpu.VMEM((10, B, B), BF16), dma((24,))], 1 << 30, "near",
    )(split, code, diag, face, near, inside)
    coarse = call(
        coarse_kernel, sds((8, B, B), F32), [SMEM, SMEM] + [VMEM] * 7, VMEM, [], 1 << 30, "coarse",
    )(split, code, total, far, xa, xb, ya, yb, z)
    return interp.reshape(face_blocks.shape), coarse.reshape(diag_blocks.shape)


def solution(mesh):
    in_specs = (
        P("gx", "gy", "gz", None, None),
        P(None, "gx", "gy", "gz", None, None),
        P("gx", "gy", "gz"),
    )
    out_specs = (P(None, "gx", "gy", "gz", None, None), P("gx", "gy", "gz", None, None))
    return jax.shard_map(
        on_device, mesh=mesh, in_specs=in_specs, out_specs=out_specs, check_vma=False
    )
```

```python
import jax
import jax.numpy as jnp
from jax import lax
from jax.experimental import pallas as pl
from jax.experimental.pallas import tpu as pltpu
from jax.sharding import PartitionSpec as P

B = 128
F32 = jnp.float32
BF16 = jnp.bfloat16
VMEM = pl.BlockSpec(memory_space=pltpu.VMEM)
SMEM = pl.BlockSpec(memory_space=pltpu.SMEM)
HBM = pl.BlockSpec(memory_space=pltpu.HBM)
LIMIT = 24 * 1024 * 1024


def mm(a, b):
    return jnp.dot(a, b, preferred_element_type=F32)


def mm32(a, b):
    return jnp.dot(a, b, preferred_element_type=F32, precision=lax.Precision.HIGHEST)


def halves(x):
    hi = x.astype(BF16)
    return hi, (x - hi.astype(F32)).astype(BF16)


def thirds(x):
    hi = x.astype(BF16)
    rest = x - hi.astype(F32)
    mid = rest.astype(BF16)
    return hi, mid, (rest - mid.astype(F32)).astype(BF16)


def wide(x):
    return jnp.concatenate([x, x], axis=0)


def split_at(split_ref, c, z):
    return split_ref[2 * c + z, 0]


def fine_of(split_ref, c):
    return jnp.where(split_at(split_ref, c, 0) == 0, 0, 1)


def square_sums(x):
    x = x.astype(F32)
    return jnp.sum(x * x, axis=0, keepdims=True)


def norms_of(rows):
    return jnp.broadcast_to(jnp.sqrt(jnp.sum(rows, axis=1, keepdims=True)), rows.shape)


def facts_kernel(split_ref, diag_ref, facts_ref, flags_ref, kept_ref, rows, held, sems):
    copies = [
        pltpu.make_async_copy(diag_ref.at[e], kept_ref.at[e], sems.at[e]) for e in range(8)
    ]
    copies.append(pltpu.make_async_copy(split_ref, held, sems.at[8]))
    for copy in copies[::-1]:
        copy.start()
    copies[8].wait()
    for e in range(8):
        part = held[0, e % 2, e // 2]
        flags_ref[pl.ds(e, 1), :] = jnp.full((1, B), part, jnp.int32)
    facts_ref[pl.ds(8, 8), :] = flags_ref[...].astype(F32)
    for e in range(8):
        copies[e].wait()
        rows[pl.ds(e, 1), :] = square_sums(kept_ref[e])
    facts_ref[pl.ds(0, 8), :] = norms_of(rows[...])


def scaling(a, eye):
    picked = jnp.where(eye, a, 0.0)
    down = lax.rsqrt(jnp.sum(picked, axis=1, keepdims=True))
    along = lax.rsqrt(jnp.sum(picked, axis=0, keepdims=True))
    a = a * down * along
    bound = jnp.max(jnp.sum(jnp.abs(a), axis=0, keepdims=True), axis=1, keepdims=True)
    return a, down, along, 1.9 / bound


def inverse_kernel(split_ref, diag_ref, face_ref, inv_ref, fnorm_ref, fine_ref, rows, work, sems):
    cols = range(4)
    copies = []
    for c in cols:
        e = 2 * c + fine_of(split_ref, c)
        for d in range(6):
            copies.append(
                pltpu.make_async_copy(face_ref.at[d, e], fine_ref.at[d, c], sems.at[6 * c + d])
            )
            copies[-1].start()
    eye = (
        lax.broadcasted_iota(jnp.int32, (B, B), 0) == lax.broadcasted_iota(jnp.int32, (B, B), 1)
    )
    one = jnp.where(eye, 1.0, 0.0).astype(F32)
    mats = [diag_ref[2 * c + fine_of(split_ref, c)] for c in cols]
    parts = [scaling(m.astype(F32), eye) for m in mats]
    powers = [one - start * a for a, _, _, start in parts]
    sums = [one + p for p in powers]
    powers = [p.astype(BF16) for p in powers]
    for _ in range(4):
        powers = [mm(p, p).astype(BF16) for p in powers]
        sums = [s + mm(s.astype(BF16), p) for s, p in zip(sums, powers)]
    guess = [
        (s * (start * down) * along).astype(BF16) for s, (_, down, along, start) in zip(sums, parts)
    ]
    left = [one - mm(mats[c], guess[c]) for c in cols]
    small = [r.astype(BF16) for r in left]
    left = [r + mm(b, b) for r, b in zip(left, small)]
    better = []
    for c in cols:
        hi, lo = halves(left[c])
        better.append(guess[c].astype(F32) + (mm(guess[c], hi) + mm(guess[c], lo)))
    pairs = [halves(x) for x in better]
    left = [one - (mm(mats[c], pairs[c][0]) + mm(mats[c], pairs[c][1])) for c in cols]
    worst = jnp.zeros((1, B), F32)
    for c in cols:
        hi, lo = pairs[c]
        rhi, rlo = halves(left[c])
        fixed = (hi.astype(F32) + lo.astype(F32)) + (mm(hi, rhi) + (mm(hi, rlo) + mm(lo, rhi)))
        inv_ref[0, c], inv_ref[1, c], inv_ref[2, c] = thirds(fixed)
        worst = worst + jnp.sum(jnp.abs(left[c]), axis=0, keepdims=True)
    for c in cols:
        for d in range(6):
            copies[6 * c + d].wait()
    for d in range(6):
        for c in cols:
            sums = square_sums(fine_ref[d, c])
            rows[pl.ds(8 * d + 2 * c, 1), :] = sums
            rows[pl.ds(8 * d + 2 * c + 1, 1), :] = sums
    fnorm_ref[...] = norms_of(rows[...])
    reached = jnp.max(worst) <= 1e-3

    @pl.when(jnp.logical_not(reached))
    def _():
        for c in cols:
            a, down, along, start = scaling(mats[c].astype(F32), eye)
            work[0] = a
            work[1] = one * start

            @pl.loop(0, 48)
            def _(_):
                x = work[1]
                work[1] = x + mm32(x, one - mm32(work[0], x))

            inv_ref[0, c], inv_ref[1, c], inv_ref[2, c] = thirds(work[1] * down * along)


def shifted(own, beyond, step, edge):
    return jnp.where(edge, pltpu.roll(beyond, step, 0), pltpu.roll(own, step, 0))


def weights_of(facts_ref, halo_refs, fnorm_ref, weight_ref):
    gx, gy, gz = lax.axis_index("gx"), lax.axis_index("gy"), lax.axis_index("gz")
    ha, hb, hc, hd, hz = halo_refs
    row = lax.broadcasted_iota(jnp.int32, (8, B), 0)
    depth = row % 2
    even_x, even_y = gx % 2 == 0, gy % 2 == 0

    def pick(test, first, second, part):
        rows = pl.ds(8 * part, 8)
        return jnp.where(test, first[rows, :], second[rows, :])

    def neighbours(part):
        own = facts_ref[pl.ds(8 * part, 8), :]
        z = hz[pl.ds(8 * part, 8), :]
        return (
            pick(even_x, hb, ha, part),
            pick(even_x, ha, hb, part),
            shifted(own, pick(even_y, hd, hc, part), 2, row < 2),
            shifted(own, pick(even_y, hc, hd, part), 6, row >= 6),
            jnp.where(depth == 0, pltpu.roll(z, 7, 0), pltpu.roll(own, 1, 0)),
            jnp.where(depth == 1, pltpu.roll(z, 1, 0), pltpu.roll(own, 7, 0)),
        )

    present = (
        jnp.broadcast_to(gx > 0, (8, B)),
        jnp.broadcast_to(gx < lax.axis_size("gx") - 1, (8, B)),
        (row >= 2) | (gy > 0),
        (row < 6) | (gy < lax.axis_size("gy") - 1),
        (depth == 1) | (gz > 0),
        (depth == 0) | (gz < lax.axis_size("gz") - 1),
    )
    own_norm = facts_ref[pl.ds(0, 8), :]
    fine = facts_ref[pl.ds(8, 8), :] < 0.5
    norms, splits = neighbours(0), neighbours(1)
    total = jnp.zeros((8, B), F32)
    denom = jnp.zeros((8, B), F32)
    links = []
    for d in range(6):
        other = jnp.where(present[d], norms[d], 1.0)
        strength = jnp.where(present[d], fnorm_ref[pl.ds(8 * d, 8), :] / jnp.sqrt(own_norm * other), 0.0)
        linked = present[d] & (splits[d] > 0.5)
        total = total + strength
        denom = denom + jnp.where(linked, strength, 0.0)
        links.append(linked)
    ratio = total / jnp.where(fine, denom, 1.0)
    for d in range(6):
        weight_ref[d] = jnp.where(links[d] & fine, -ratio, 0.0)


def interp_kernel(
    split_ref, diag_ref, fine_ref, inv_ref, fnorm_ref, facts_ref, ha, hb, hc, hd, hz,
    interp_ref, code_ref, xa_ref, xb_ref, ya_ref, yb_ref, z_ref, near_ref, inside_ref,
    weight_ref, mixed_ref, zero_ref, sems,
):
    zero_ref[...] = jnp.zeros((B, B), BF16)
    gx, gy = lax.axis_index("gx"), lax.axis_index("gy")
    fines = [fine_of(split_ref, c) for c in range(4)]
    weights_of(facts_ref, (ha, hb, hc, hd, hz), fnorm_ref, weight_ref)
    copies = []

    def send(block, d, e):
        copies.append(pltpu.make_async_copy(block, interp_ref.at[d, e], sems.at[len(copies)]))
        copies[-1].start()

    def slots(c):
        return (
            (1 - gx % 2, xa_ref.at[0, c], xa_ref.at[1, c]),
            (gx % 2, xb_ref.at[0, c], xb_ref.at[1, c]),
            (2, near_ref.at[0, 0, c], near_ref.at[0, 1, c]),
            (3, near_ref.at[1, 0, c], near_ref.at[1, 1, c]),
            (5 - fines[c], inside_ref.at[0, c], inside_ref.at[1, c]),
            (4 + fines[c], z_ref.at[0, c], z_ref.at[1, c]),
        )

    def send_column(c):
        for d, interp, _ in slots(c):
            send(interp, d, 2 * c + fines[c])

    for c in range(4):
        e = 2 * c + fines[c]
        inv = jnp.concatenate([inv_ref[0, c], inv_ref[1, c]], axis=1)
        last = inv_ref[2, c]
        here = slots(c)
        for s in (0, 2, 4):
            two = [here[s], here[s + 1]]
            face = jnp.concatenate([fine_ref[d, c] for d, _, _ in two], axis=1)
            weight = jnp.concatenate([weight_ref[d, pl.ds(e, 1), :] for d, _, _ in two], axis=1)
            interp = (weight * (mm(inv, wide(face)) + mm(last, face))).astype(BF16)
            two[0][1][...] = interp[:, :B]
            two[1][1][...] = interp[:, B:]
        for d in range(6):
            send(zero_ref, d, 2 * c + 1 - fines[c])
        if c > 0:
            send_column(c - 1)
    row = lax.broadcasted_iota(jnp.int32, (8, B), 0)
    lane = lax.broadcasted_iota(jnp.int32, (8, B), 1)
    bit = jnp.where((row % 2 == 0) & (lane == 0), 1, 0) * lax.shift_left(1, row // 2)
    code = jnp.zeros((8, B), F32)
    for place, ref in enumerate((ha, hb, hc, hd)):
        code = code + ref[pl.ds(8, 8), :] * (bit * (1 << (4 * place))).astype(F32)
    code = jnp.sum(jnp.sum(code, axis=0, keepdims=True), axis=1, keepdims=True)
    code_ref[...] = jnp.broadcast_to(code, (8, B)).astype(jnp.int32)
    for c in range(4):
        a = diag_ref[2 * c + fines[c]]
        here = slots(c)
        for s in (0, 2, 4):
            two = [here[s], here[s + 1]]
            face = jnp.concatenate([fine_ref[d, c] for d, _, _ in two], axis=1)
            interp = jnp.concatenate([block[...] for _, block, _ in two], axis=1)
            hi, lo = halves(mm(a, interp) + face.astype(F32))
            for t in range(2):
                lanes = slice(B * t, B * t + B)
                mixed_ref[c, s + t, pl.ds(0, B), :] = hi[:, lanes]
                mixed_ref[c, s + t, pl.ds(B, B), :] = lo[:, lanes]
        if c == 1:
            send_column(3)
    for c in range(4):
        for s, (_, interp, contrib) in enumerate(slots(c)):
            turned = jnp.transpose(interp[...])
            both = jnp.concatenate([turned, turned], axis=1)
            contrib[...] = mm(both, mixed_ref[c, s]).astype(BF16)
    up = gy % 2 == 0
    for k in range(2):
        low, high = near_ref[0, k, 0], near_ref[1, k, 3]
        ya_ref[k, 0] = jnp.where(up, high, low)
        yb_ref[k, 0] = jnp.where(up, low, high)
    for copy in copies:
        copy.wait()


def near_kernel(split_ref, diag_ref, face_ref, near_ref, inside_ref, sum_ref):
    fines = [fine_of(split_ref, c) for c in range(4)]
    for c in range(4):
        arrived = []
        if c > 0:
            arrived.append((fines[c - 1], 2, near_ref.at[1, 0, c - 1], near_ref.at[1, 1, c - 1]))
        if c < 3:
            arrived.append((fines[c + 1], 3, near_ref.at[0, 0, c + 1], near_ref.at[0, 1, c + 1]))
        arrived.append((1 - fines[c], 4 + fines[c], inside_ref.at[0, c], inside_ref.at[1, c]))
        gather(c, arrived, face_ref, lambda e: diag_ref[e].astype(F32), sum_ref)


def gather(c, arrived, face_ref, start, out_ref):
    totals = [start(2 * c), start(2 * c + 1)]
    for z, d, interp, contrib in arrived:
        part = contrib[...].astype(F32) + mm(face_ref[d, 2 * c + z], interp[...])
        totals = [total + jnp.where(z == k, part, 0.0) for k, total in enumerate(totals)]
    for k in range(2):
        out_ref[2 * c + k] = totals[k]


def coarse_kernel(
    split_ref, code_ref, sum_ref, face_ref, xa_ref, xb_ref, ya_ref, yb_ref, z_ref,
    coarse_ref, total_ref, sems,
):
    gx, gy, gz = lax.axis_index("gx"), lax.axis_index("gy"), lax.axis_index("gz")
    code = code_ref[0, 0]
    up = gy % 2 == 0

    def bit_at(place):
        return lax.shift_right_logical(code, place) & 1

    copies = []
    for c in (1, 2, 0, 3):
        arrived = [
            (bit_at(c), 1 - gx % 2, xa_ref.at[0, c], xa_ref.at[1, c]),
            (bit_at(4 + c), gx % 2, xb_ref.at[0, c], xb_ref.at[1, c]),
            (1 - gz, 5 - gz, z_ref.at[0, c], z_ref.at[1, c]),
        ]
        extra = None
        if c in (0, 3):
            first = up if c == 3 else jnp.logical_not(up)
            edge = 0 if c == 3 else 3
            z = jnp.where(first, bit_at(8 + edge), bit_at(12 + edge))
            pair = [jnp.where(first, ya_ref[k, 0], yb_ref[k, 0]) for k in range(2)]
            extra = (z, 3 if c == 3 else 2, pair)
        totals = [sum_ref[2 * c], sum_ref[2 * c + 1]]
        parts = [
            (z, contrib[...].astype(F32) + mm(face_ref[d, 2 * c + z], interp[...]))
            for z, d, interp, contrib in arrived
        ]
        if extra:
            z, d, (interp, contrib) = extra
            parts.append((z, contrib.astype(F32) + mm(face_ref[d, 2 * c + z], interp)))
        for k in range(2):
            e = 2 * c + k
            keep = split_at(split_ref, c, k) == 1
            for z, part in parts:
                totals[k] = totals[k] + jnp.where(z == k, part, 0.0)
            total_ref[e] = jnp.where(keep, totals[k], 0.0)
            copies.append(pltpu.make_async_copy(total_ref.at[e], coarse_ref.at[e], sems.at[e]))
            copies[-1].start()
    for copy in copies:
        copy.wait()


def matching(size, start):
    pairs = [(i, i + 1) for i in range(start, size - 1, 2)]
    return pairs + [(b, a) for a, b in pairs]


def swap(x, axis, start):
    return lax.ppermute(x, axis, matching(lax.axis_size(axis), start))


def call(body, out_shape, in_specs, out_specs, scratch, flops, name):
    return pl.pallas_call(
        body,
        out_shape=out_shape,
        in_specs=in_specs,
        out_specs=out_specs,
        scratch_shapes=scratch,
        compiler_params=pltpu.CompilerParams(vmem_limit_bytes=LIMIT),
        cost_estimate=pl.CostEstimate(flops=flops, bytes_accessed=2 << 20, transcendentals=0),
        name=name,
    )


def on_device(diag_blocks, face_blocks, split):
    diag = diag_blocks.reshape(8, B, B)
    face = face_blocks.reshape(6, 8, B, B)
    split = jnp.transpose(split, (0, 2, 1))
    sds = jax.ShapeDtypeStruct
    dma = pltpu.SemaphoreType.DMA
    in_hbm = lambda x: pltpu.with_memory_space_constraint(x, pltpu.HBM)
    blocks = lambda *lead: sds(lead + (B, B), BF16)
    facts, flags, diag = call(
        facts_kernel, (sds((16, B), F32), sds((8, B), jnp.int32), blocks(8)),
        [HBM, HBM], (VMEM, VMEM, VMEM),
        [pltpu.VMEM((8, B), F32), pltpu.SMEM((1, 2, 4), jnp.int32), dma((9,))], 1 << 20, "facts",
    )(in_hbm(split), in_hbm(diag))
    halo = (
        swap(facts, "gx", 0), swap(facts, "gx", 1),
        swap(facts, "gy", 0), swap(facts, "gy", 1), swap(facts, "gz", 0),
    )
    inv, fnorm, fine = call(
        inverse_kernel, (blocks(3, 4), sds((48, B), F32), blocks(6, 4)),
        [SMEM, VMEM, HBM], (VMEM, VMEM, VMEM),
        [pltpu.VMEM((48, B), F32), pltpu.VMEM((2, B, B), F32), dma((24,))], 1 << 30, "inverse",
    )(flags, diag, in_hbm(face))
    interp, code, xa, xb, ya, yb, z, near, inside = call(
        interp_kernel,
        (
            blocks(6, 8), sds((8, B), jnp.int32), blocks(2, 4), blocks(2, 4), blocks(2, 1),
            blocks(2, 1), blocks(2, 4), blocks(2, 2, 4), blocks(2, 4),
        ),
        [SMEM] + [VMEM] * 10,
        (HBM,) + (VMEM,) * 8,
        [
            pltpu.VMEM((6, 8, B), F32), pltpu.VMEM((4, 6, 2 * B, B), BF16),
            pltpu.VMEM((B, B), BF16), dma((48,)),
        ],
        1 << 30, "interp",
    )(flags, diag, fine, inv, fnorm, facts, *halo)
    xb = swap(xb, "gx", 1)
    xa = swap(xa, "gx", 0)
    yb, ya = swap(yb, "gy", 1), swap(ya, "gy", 0)
    z = swap(z, "gz", 0)
    total = call(
        near_kernel, sds((8, B, B), F32), [SMEM] + [VMEM] * 4, VMEM, [], 1 << 30, "near",
    )(flags, diag, face, near, inside)
    coarse = call(
        coarse_kernel, sds((8, B, B), F32), [SMEM, SMEM] + [VMEM] * 7, HBM,
        [pltpu.VMEM((8, B, B), F32), dma((8,))], 1 << 30, "coarse",
    )(flags, code, total, face, xa, xb, ya, yb, z)
    return interp.reshape(face_blocks.shape), coarse.reshape(diag_blocks.shape)


def solution(mesh):
    in_specs = (
        P("gx", "gy", "gz", None, None),
        P(None, "gx", "gy", "gz", None, None),
        P("gx", "gy", "gz"),
    )
    out_specs = (P(None, "gx", "gy", "gz", None, None), P("gx", "gy", "gz", None, None))
    return jax.shard_map(
        on_device, mesh=mesh, in_specs=in_specs, out_specs=out_specs, check_vma=False
    )
```

```python
import jax
import jax.numpy as jnp
from jax import lax
from jax.experimental import pallas as pl
from jax.experimental.pallas import tpu as pltpu
from jax.sharding import PartitionSpec as P


B = 128
F32 = jnp.float32
BF16 = jnp.bfloat16
VMEM = pl.BlockSpec(memory_space=pltpu.VMEM)
SMEM = pl.BlockSpec(memory_space=pltpu.SMEM)
HBM = pl.BlockSpec(memory_space=pltpu.HBM)
LIMIT = 24 * 1024 * 1024


def mm(a, b):
    return jnp.dot(a, b, preferred_element_type=F32)


def mm32(a, b):
    return jnp.dot(a, b, preferred_element_type=F32, precision=lax.Precision.HIGHEST)


def halves(x):
    hi = x.astype(BF16)
    return hi, (x - hi.astype(F32)).astype(BF16)


def thirds(x):
    hi = x.astype(BF16)
    rest = x - hi.astype(F32)
    mid = rest.astype(BF16)
    return hi, mid, (rest - mid.astype(F32)).astype(BF16)


def wide(x):
    return jnp.concatenate([x, x], axis=0)


def split_at(split_ref, c, z):
    return split_ref[2 * c + z, 0]


def fine_of(split_ref, c):
    return jnp.where(split_at(split_ref, c, 0) == 0, 0, 1)


def square_sums(x):
    x = x.astype(F32)
    return jnp.sum(x * x, axis=0, keepdims=True)


def norms_of(rows):
    return jnp.broadcast_to(jnp.sqrt(jnp.sum(rows, axis=1, keepdims=True)), rows.shape)


def facts_kernel(split_ref, diag_ref, facts_ref, flags_ref, kept_ref, rows, held, sems):
    copies = [
        pltpu.make_async_copy(diag_ref.at[e], kept_ref.at[e], sems.at[e]) for e in range(8)
    ]
    copies.append(pltpu.make_async_copy(split_ref, held, sems.at[8]))
    for copy in copies[::-1]:
        copy.start()
    copies[8].wait()
    for e in range(8):
        part = held[0, e % 2, e // 2]
        flags_ref[pl.ds(e, 1), :] = jnp.full((1, B), part, jnp.int32)
    facts_ref[pl.ds(8, 8), :] = flags_ref[...].astype(F32)
    for e in range(8):
        copies[e].wait()
        rows[pl.ds(e, 1), :] = square_sums(kept_ref[e])
    facts_ref[pl.ds(0, 8), :] = norms_of(rows[...])


def scaling(a, eye):
    picked = jnp.where(eye, a, 0.0)
    down = lax.rsqrt(jnp.sum(picked, axis=1, keepdims=True))
    along = lax.rsqrt(jnp.sum(picked, axis=0, keepdims=True))
    a = a * down * along
    bound = jnp.max(jnp.sum(jnp.abs(a), axis=0, keepdims=True), axis=1, keepdims=True)
    return a, down, along, 1.9 / bound


def inverse_kernel(split_ref, diag_ref, face_ref, inv_ref, fnorm_ref, fine_ref, rows, work, sems):
    cols = range(4)
    copies = []
    for c in cols:
        e = 2 * c + fine_of(split_ref, c)
        for d in range(6):
            copies.append(
                pltpu.make_async_copy(face_ref.at[d, e], fine_ref.at[d, c], sems.at[6 * c + d])
            )
            copies[-1].start()
    eye = (
        lax.broadcasted_iota(jnp.int32, (B, B), 0) == lax.broadcasted_iota(jnp.int32, (B, B), 1)
    )
    one = jnp.where(eye, 1.0, 0.0).astype(F32)
    mats = [diag_ref[2 * c + fine_of(split_ref, c)] for c in cols]
    parts = [scaling(m.astype(F32), eye) for m in mats]
    powers = [one - start * a for a, _, _, start in parts]
    sums = [one + p for p in powers]
    powers = [p.astype(BF16) for p in powers]
    for _ in range(4):
        powers = [mm(p, p).astype(BF16) for p in powers]
        sums = [s + mm(s.astype(BF16), p) for s, p in zip(sums, powers)]
    guess = [
        (s * (start * down) * along).astype(BF16) for s, (_, down, along, start) in zip(sums, parts)
    ]
    left = [one - mm(mats[c], guess[c]) for c in cols]
    small = [r.astype(BF16) for r in left]
    left = [r + mm(b, b) for r, b in zip(left, small)]
    better = []
    for c in cols:
        hi, lo = halves(left[c])
        better.append(guess[c].astype(F32) + (mm(guess[c], hi) + mm(guess[c], lo)))
    pairs = [halves(x) for x in better]
    left = [one - (mm(mats[c], pairs[c][0]) + mm(mats[c], pairs[c][1])) for c in cols]
    worst = jnp.zeros((1, B), F32)
    for c in cols:
        hi, lo = pairs[c]
        rhi, rlo = halves(left[c])
        fixed = (hi.astype(F32) + lo.astype(F32)) + (mm(hi, rhi) + (mm(hi, rlo) + mm(lo, rhi)))
        inv_ref[0, c], inv_ref[1, c], inv_ref[2, c] = thirds(fixed)
        worst = worst + jnp.sum(jnp.abs(left[c]), axis=0, keepdims=True)
    for c in cols:
        for d in range(6):
            copies[6 * c + d].wait()
    for d in range(6):
        for c in cols:
            sums = square_sums(fine_ref[d, c])
            rows[pl.ds(8 * d + 2 * c, 1), :] = sums
            rows[pl.ds(8 * d + 2 * c + 1, 1), :] = sums
    fnorm_ref[...] = norms_of(rows[...])
    reached = jnp.max(worst) <= 1e-3

    @pl.when(jnp.logical_not(reached))
    def _():
        for c in cols:
            a, down, along, start = scaling(mats[c].astype(F32), eye)
            work[0] = a
            work[1] = one * start

            @pl.loop(0, 48)
            def _(_):
                x = work[1]
                work[1] = x + mm32(x, one - mm32(work[0], x))

            inv_ref[0, c], inv_ref[1, c], inv_ref[2, c] = thirds(work[1] * down * along)


def shifted(own, beyond, step, edge):
    return jnp.where(edge, pltpu.roll(beyond, step, 0), pltpu.roll(own, step, 0))


def weights_of(facts_ref, halo_refs, fnorm_ref, weight_ref):
    gx, gy, gz = lax.axis_index("gx"), lax.axis_index("gy"), lax.axis_index("gz")
    ha, hb, hc, hd, hz = halo_refs
    row = lax.broadcasted_iota(jnp.int32, (8, B), 0)
    depth = row % 2
    even_x, even_y = gx % 2 == 0, gy % 2 == 0

    def pick(test, first, second, part):
        rows = pl.ds(8 * part, 8)
        return jnp.where(test, first[rows, :], second[rows, :])

    def neighbours(part):
        own = facts_ref[pl.ds(8 * part, 8), :]
        z = hz[pl.ds(8 * part, 8), :]
        return (
            pick(even_x, hb, ha, part),
            pick(even_x, ha, hb, part),
            shifted(own, pick(even_y, hd, hc, part), 2, row < 2),
            shifted(own, pick(even_y, hc, hd, part), 6, row >= 6),
            jnp.where(depth == 0, pltpu.roll(z, 7, 0), pltpu.roll(own, 1, 0)),
            jnp.where(depth == 1, pltpu.roll(z, 1, 0), pltpu.roll(own, 7, 0)),
        )

    present = (
        jnp.broadcast_to(gx > 0, (8, B)),
        jnp.broadcast_to(gx < lax.axis_size("gx") - 1, (8, B)),
        (row >= 2) | (gy > 0),
        (row < 6) | (gy < lax.axis_size("gy") - 1),
        (depth == 1) | (gz > 0),
        (depth == 0) | (gz < lax.axis_size("gz") - 1),
    )
    own_norm = facts_ref[pl.ds(0, 8), :]
    fine = facts_ref[pl.ds(8, 8), :] < 0.5
    norms, splits = neighbours(0), neighbours(1)
    total = jnp.zeros((8, B), F32)
    denom = jnp.zeros((8, B), F32)
    links = []
    for d in range(6):
        other = jnp.where(present[d], norms[d], 1.0)
        strength = jnp.where(present[d], fnorm_ref[pl.ds(8 * d, 8), :] / jnp.sqrt(own_norm * other), 0.0)
        linked = present[d] & (splits[d] > 0.5)
        total = total + strength
        denom = denom + jnp.where(linked, strength, 0.0)
        links.append(linked)
    ratio = total / jnp.where(fine, denom, 1.0)
    for d in range(6):
        weight_ref[d] = jnp.where(links[d] & fine, -ratio, 0.0)


def interp_kernel(
    split_ref, diag_ref, fine_ref, inv_ref, fnorm_ref, facts_ref, ha, hb, hc, hd, hz,
    interp_ref, code_ref, xa_ref, xb_ref, ya_ref, yb_ref, z_ref, near_ref, inside_ref,
    weight_ref, edge_ref, zero_ref, sems,
):
    zero_ref[...] = jnp.zeros((B, B), BF16)
    gx, gy = lax.axis_index("gx"), lax.axis_index("gy")
    fines = [fine_of(split_ref, c) for c in range(4)]
    weights_of(facts_ref, (ha, hb, hc, hd, hz), fnorm_ref, weight_ref)
    copies = []

    def send(block, d, e):
        copies.append(pltpu.make_async_copy(block, interp_ref.at[d, e], sems.at[len(copies)]))
        copies[-1].start()

    def slots(c):
        return (
            (1 - gx % 2, xa_ref.at[0, c], xa_ref.at[1, c]),
            (gx % 2, xb_ref.at[0, c], xb_ref.at[1, c]),
            (4 + fines[c], z_ref.at[0, c], z_ref.at[1, c]),
            (2, near_ref.at[0, c], edge_ref.at[0] if c == 0 else None),
            (3, near_ref.at[1, c], edge_ref.at[1] if c == 3 else None),
            (5 - fines[c], inside_ref.at[c], None),
        )

    def send_column(c):
        for d, interp, _ in slots(c):
            send(interp, d, 2 * c + fines[c])

    for c in range(4):
        e = 2 * c + fines[c]
        inv = jnp.concatenate([inv_ref[0, c], inv_ref[1, c]], axis=1)
        last = inv_ref[2, c]
        here = slots(c)
        for s in (0, 2, 4):
            two = [here[s], here[s + 1]]
            face = jnp.concatenate([fine_ref[d, c] for d, _, _ in two], axis=1)
            weight = jnp.concatenate([weight_ref[d, pl.ds(e, 1), :] for d, _, _ in two], axis=1)
            interp = (weight * (mm(inv, wide(face)) + mm(last, face))).astype(BF16)
            two[0][1][...] = interp[:, :B]
            two[1][1][...] = interp[:, B:]
        for d in range(6):
            send(zero_ref, d, 2 * c + 1 - fines[c])
        if c > 0:
            send_column(c - 1)
    row = lax.broadcasted_iota(jnp.int32, (8, B), 0)
    lane = lax.broadcasted_iota(jnp.int32, (8, B), 1)
    bit = jnp.where((row % 2 == 0) & (lane == 0), 1, 0) * lax.shift_left(1, row // 2)
    code = jnp.zeros((8, B), F32)
    for place, ref in enumerate((ha, hb, hc, hd)):
        code = code + ref[pl.ds(8, 8), :] * (bit * (1 << (4 * place))).astype(F32)
    code = jnp.sum(jnp.sum(code, axis=0, keepdims=True), axis=1, keepdims=True)
    code_ref[...] = jnp.broadcast_to(code, (8, B)).astype(jnp.int32)
    for c in range(4):
        here = [slot for slot in slots(c) if slot[2] is not None]
        a = diag_ref[2 * c + fines[c]]
        faces = [fine_ref[d, c] for d, _, _ in here]
        found = contribs(a, faces, [block[...] for _, block, _ in here])
        for (_, _, into), contrib in zip(here, found):
            into[...] = contrib
        if c == 0:
            send_column(3)
    up = gy % 2 == 0
    low, high = near_ref[0, 0], near_ref[1, 3]
    ya_ref[0, 0], yb_ref[0, 0] = jnp.where(up, high, low), jnp.where(up, low, high)
    low, high = edge_ref[0], edge_ref[1]
    ya_ref[1, 0], yb_ref[1, 0] = jnp.where(up, high, low), jnp.where(up, low, high)
    for copy in copies:
        copy.wait()


def contribs(a, faces, interps):
    found = []
    for s in range(0, len(faces), 2):
        pair = interps[s:s + 2]
        face = jnp.concatenate(faces[s:s + 2], axis=1)
        hi, lo = halves(mm(a, jnp.concatenate(pair, axis=1)) + face.astype(F32))
        for t, interp in enumerate(pair):
            lanes = slice(B * t, B * t + B)
            turned = jnp.transpose(interp)
            both = jnp.concatenate([turned, turned], axis=1)
            mixed = jnp.concatenate([hi[:, lanes], lo[:, lanes]], axis=0)
            found.append(mm(both, mixed).astype(BF16))
    return found


def near_kernel(split_ref, diag_ref, face_ref, fine_ref, near_ref, inside_ref, sum_ref):
    fines = [fine_of(split_ref, c) for c in range(4)]
    parts = [[] for _ in range(4)]
    for c in range(4):
        z = fines[c]
        here = [(c, 1 - z, 4 + z, 5 - z, inside_ref[c])]
        if c > 0:
            here.append((c - 1, z, 3, 2, near_ref[0, c]))
        if c < 3:
            here.append((c + 1, z, 2, 3, near_ref[1, c]))
        found = contribs(
            diag_ref[2 * c + z], [fine_ref[d, c] for _, _, _, d, _ in here], [p for *_, p in here]
        )
        for (to, depth, back, _, interp), contrib in zip(here, found):
            product = mm(face_ref[back, 2 * to + depth], interp)
            parts[to].append((depth, contrib.astype(F32) + product))
    for c in range(4):
        for k in range(2):
            total = diag_ref[2 * c + k].astype(F32)
            for z, part in parts[c]:
                total = total + jnp.where(z == k, part, 0.0)
            sum_ref[2 * c + k] = total


def coarse_kernel(
    split_ref, code_ref, sum_ref, face_ref, xa_ref, xb_ref, ya_ref, yb_ref, z_ref,
    coarse_ref, total_ref, sems,
):
    gx, gy, gz = lax.axis_index("gx"), lax.axis_index("gy"), lax.axis_index("gz")
    code = code_ref[0, 0]
    up = gy % 2 == 0

    def bit_at(place):
        return lax.shift_right_logical(code, place) & 1

    copies = []
    for c in (1, 2, 0, 3):
        arrived = [
            (bit_at(c), 1 - gx % 2, xa_ref.at[0, c], xa_ref.at[1, c]),
            (bit_at(4 + c), gx % 2, xb_ref.at[0, c], xb_ref.at[1, c]),
            (1 - gz, 5 - gz, z_ref.at[0, c], z_ref.at[1, c]),
        ]
        extra = None
        if c in (0, 3):
            first = up if c == 3 else jnp.logical_not(up)
            edge = 0 if c == 3 else 3
            z = jnp.where(first, bit_at(8 + edge), bit_at(12 + edge))
            pair = [jnp.where(first, ya_ref[k, 0], yb_ref[k, 0]) for k in range(2)]
            extra = (z, 3 if c == 3 else 2, pair)
        totals = [sum_ref[2 * c], sum_ref[2 * c + 1]]
        parts = [
            (z, contrib[...].astype(F32) + mm(face_ref[d, 2 * c + z], interp[...]))
            for z, d, interp, contrib in arrived
        ]
        if extra:
            z, d, (interp, contrib) = extra
            parts.append((z, contrib.astype(F32) + mm(face_ref[d, 2 * c + z], interp)))
        for k in range(2):
            e = 2 * c + k
            keep = split_at(split_ref, c, k) == 1
            for z, part in parts:
                totals[k] = totals[k] + jnp.where(z == k, part, 0.0)
            total_ref[e] = jnp.where(keep, totals[k], 0.0)
            copies.append(pltpu.make_async_copy(total_ref.at[e], coarse_ref.at[e], sems.at[e]))
            copies[-1].start()
    for copy in copies:
        copy.wait()


def matching(size, start):
    pairs = [(i, i + 1) for i in range(start, size - 1, 2)]
    return pairs + [(b, a) for a, b in pairs]


def swap(x, axis, start):
    return lax.ppermute(x, axis, matching(lax.axis_size(axis), start))


def call(body, out_shape, in_specs, out_specs, scratch, flops):
    return pl.pallas_call(
        body,
        out_shape=out_shape,
        in_specs=in_specs,
        out_specs=out_specs,
        scratch_shapes=scratch,
        compiler_params=pltpu.CompilerParams(vmem_limit_bytes=LIMIT),
        cost_estimate=pl.CostEstimate(flops=flops, bytes_accessed=2 << 20, transcendentals=0),
    )


def on_device(diag_blocks, face_blocks, split):
    diag = diag_blocks.reshape(8, B, B)
    face = face_blocks.reshape(6, 8, B, B)
    split = jnp.transpose(split, (0, 2, 1))
    sds = jax.ShapeDtypeStruct
    dma = pltpu.SemaphoreType.DMA
    in_hbm = lambda x: pltpu.with_memory_space_constraint(x, pltpu.HBM)
    blocks = lambda *lead: sds(lead + (B, B), BF16)
    facts, flags, diag = call(
        facts_kernel, (sds((16, B), F32), sds((8, B), jnp.int32), blocks(8)),
        [HBM, HBM], (VMEM, VMEM, VMEM),
        [pltpu.VMEM((8, B), F32), pltpu.SMEM((1, 2, 4), jnp.int32), dma((9,))], 1 << 20,
    )(in_hbm(split), in_hbm(diag))
    halo = (
        swap(facts, "gx", 0), swap(facts, "gx", 1),
        swap(facts, "gy", 0), swap(facts, "gy", 1),
        swap(facts, "gz", 0),
    )
    inv, fnorm, fine = call(
        inverse_kernel, (blocks(3, 4), sds((48, B), F32), blocks(6, 4)),
        [SMEM, VMEM, HBM], (VMEM, VMEM, VMEM),
        [pltpu.VMEM((48, B), F32), pltpu.VMEM((2, B, B), F32), dma((24,))], 1 << 30,
    )(flags, diag, in_hbm(face))
    interp, code, xa, xb, ya, yb, z, near, inside = call(
        interp_kernel,
        (
            blocks(6, 8), sds((8, B), jnp.int32), blocks(2, 4), blocks(2, 4), blocks(2, 1),
            blocks(2, 1), blocks(2, 4), blocks(2, 4), blocks(4),
        ),
        [SMEM] + [VMEM] * 10,
        (HBM,) + (VMEM,) * 8,
        [
            pltpu.VMEM((6, 8, B), F32), pltpu.VMEM((2, B, B), BF16),
            pltpu.VMEM((B, B), BF16), dma((48,)),
        ],
        1 << 30,
    )(flags, diag, fine, inv, fnorm, facts, *halo)
    xa, xb = swap(xa, "gx", 0), swap(xb, "gx", 1)
    ya, yb = swap(ya, "gy", 0), swap(yb, "gy", 1)
    z = swap(z, "gz", 0)
    total = call(
        near_kernel, sds((8, B, B), F32), [SMEM] + [VMEM] * 5, VMEM, [], 1 << 30,
    )(flags, diag, face, fine, near, inside)
    coarse = call(
        coarse_kernel, sds((8, B, B), F32), [SMEM, SMEM] + [VMEM] * 7, HBM,
        [pltpu.VMEM((8, B, B), F32), dma((8,))], 1 << 30,
    )(flags, code, total, face, xa, xb, ya, yb, z)
    return interp.reshape(face_blocks.shape), coarse.reshape(diag_blocks.shape)


def solution(mesh):
    in_specs = (
        P("gx", "gy", "gz", None, None),
        P(None, "gx", "gy", "gz", None, None),
        P("gx", "gy", "gz"),
    )
    out_specs = (P(None, "gx", "gy", "gz", None, None), P("gx", "gy", "gz", None, None))
    return jax.shard_map(
        on_device, mesh=mesh, in_specs=in_specs, out_specs=out_specs, check_vma=False
    )
```

```python
import jax
import jax.numpy as jnp
from jax import lax
from jax.experimental import pallas as pl
from jax.experimental.pallas import tpu as pltpu
from jax.sharding import PartitionSpec as P


B = 128
F32 = jnp.float32
BF16 = jnp.bfloat16
VMEM = pl.BlockSpec(memory_space=pltpu.VMEM)
SMEM = pl.BlockSpec(memory_space=pltpu.SMEM)
HBM = pl.BlockSpec(memory_space=pltpu.HBM)
LIMIT = 24 * 1024 * 1024


def mm(a, b):
    return jnp.dot(a, b, preferred_element_type=F32)


def mm32(a, b):
    return jnp.dot(a, b, preferred_element_type=F32, precision=lax.Precision.HIGHEST)


def halves(x):
    hi = x.astype(BF16)
    return hi, (x - hi.astype(F32)).astype(BF16)


def thirds(x):
    hi = x.astype(BF16)
    rest = x - hi.astype(F32)
    mid = rest.astype(BF16)
    return hi, mid, (rest - mid.astype(F32)).astype(BF16)


def wide(x):
    return jnp.concatenate([x, x], axis=0)


def split_at(split_ref, c, z):
    return split_ref[2 * c + z, 0]


def fine_of(split_ref, c):
    return jnp.where(split_at(split_ref, c, 0) == 0, 0, 1)


def square_sums(x):
    x = x.astype(F32)
    return jnp.sum(x * x, axis=0, keepdims=True)


def norms_of(rows):
    return jnp.broadcast_to(jnp.sqrt(jnp.sum(rows, axis=1, keepdims=True)), rows.shape)


def facts_kernel(
    split_ref, diag_ref, face_ref, facts_ref, flags_ref, kept_ref, xa_ref, xb_ref, rows, held, sems
):
    gx = lax.axis_index("gx")
    first = pltpu.make_async_copy(split_ref, held, sems.at[0])
    first.start()
    copies = [
        pltpu.make_async_copy(diag_ref.at[e], kept_ref.at[e], sems.at[1 + e]) for e in range(8)
    ]
    for copy in copies:
        copy.start()
    first.wait()
    for c in range(4):
        e = 2 * c + jnp.where(held[0, 0, c] == 0, 0, 1)
        for ref, d in ((xa_ref, 1 - gx % 2), (xb_ref, gx % 2)):
            for block, place in ((diag_ref.at[e], c), (face_ref.at[d, e], 4 + c)):
                into = ref.at[pl.ds(B * place, B), :]
                copies.append(pltpu.make_async_copy(block, into, sems.at[1 + len(copies)]))
                copies[-1].start()
    for e in range(8):
        part = held[0, e % 2, e // 2]
        flags_ref[pl.ds(e, 1), :] = jnp.full((1, B), part, jnp.int32)
    flags = flags_ref[...].astype(F32)
    facts_ref[pl.ds(8, 8), :] = flags
    for e in range(8):
        copies[e].wait()
        rows[pl.ds(e, 1), :] = square_sums(kept_ref[e])
    norms = norms_of(rows[...])
    facts_ref[pl.ds(0, 8), :] = norms
    parts = [part.astype(F32) for part in thirds(norms)] + [flags]
    for ref in (xa_ref, xb_ref):
        for k in range(2):
            both = jnp.concatenate(parts[2 * k:2 * k + 2], axis=0)
            ref[pl.ds(8 * B + 16 * k, 16), :] = both.astype(BF16)
    for copy in copies[8:]:
        copy.wait()


def facts_in(ref):
    high, low = ref[pl.ds(8 * B, 16), :].astype(F32), ref[pl.ds(8 * B + 16, 16), :].astype(F32)
    return high[:8] + high[8:] + low[:8], low[8:]


def scaling(a, eye):
    picked = jnp.where(eye, a, 0.0)
    down = lax.rsqrt(jnp.sum(picked, axis=1, keepdims=True))
    along = lax.rsqrt(jnp.sum(picked, axis=0, keepdims=True))
    a = a * down * along
    bound = jnp.max(jnp.sum(jnp.abs(a), axis=0, keepdims=True), axis=1, keepdims=True)
    return a, down, along, 1.9 / bound


def inverse_kernel(
    split_ref, diag_ref, face_ref, solved_ref, fnorm_ref, fine_ref, inv_ref, rows, work, sems
):
    cols = range(4)
    copies = []
    for c in cols:
        e = 2 * c + fine_of(split_ref, c)
        for d in range(6):
            copies.append(
                pltpu.make_async_copy(face_ref.at[d, e], fine_ref.at[d, c], sems.at[6 * c + d])
            )
            copies[-1].start()
    eye = (
        lax.broadcasted_iota(jnp.int32, (B, B), 0) == lax.broadcasted_iota(jnp.int32, (B, B), 1)
    )
    one = jnp.where(eye, 1.0, 0.0).astype(F32)
    mats = [diag_ref[2 * c + fine_of(split_ref, c)] for c in cols]
    parts = [scaling(m.astype(F32), eye) for m in mats]
    powers = [one - start * a for a, _, _, start in parts]
    sums = [one + p for p in powers]
    powers = [p.astype(BF16) for p in powers]
    for _ in range(4):
        powers = [mm(p, p).astype(BF16) for p in powers]
        sums = [s + mm(s.astype(BF16), p) for s, p in zip(sums, powers)]
    guess = [
        (s * (start * down) * along).astype(BF16) for s, (_, down, along, start) in zip(sums, parts)
    ]
    left = [one - mm(mats[c], guess[c]) for c in cols]
    small = [r.astype(BF16) for r in left]
    left = [r + mm(b, b) for r, b in zip(left, small)]
    better = []
    for c in cols:
        hi, lo = halves(left[c])
        better.append(guess[c].astype(F32) + (mm(guess[c], hi) + mm(guess[c], lo)))
    pairs = [halves(x) for x in better]
    left = [one - (mm(mats[c], pairs[c][0]) + mm(mats[c], pairs[c][1])) for c in cols]
    worst = jnp.zeros((1, B), F32)
    for c in cols:
        hi, lo = pairs[c]
        rhi, rlo = halves(left[c])
        fixed = (hi.astype(F32) + lo.astype(F32)) + (mm(hi, rhi) + (mm(hi, rlo) + mm(lo, rhi)))
        inv_ref[0, c], inv_ref[1, c], inv_ref[2, c] = thirds(fixed)
        worst = worst + jnp.sum(jnp.abs(left[c]), axis=0, keepdims=True)
    for c in cols:
        for d in range(6):
            copies[6 * c + d].wait()
    for d in range(6):
        for c in cols:
            sums = square_sums(fine_ref[d, c])
            rows[pl.ds(8 * d + 2 * c, 1), :] = sums
            rows[pl.ds(8 * d + 2 * c + 1, 1), :] = sums
    fnorm_ref[...] = norms_of(rows[...])

    def solve():
        for c in cols:
            inv = jnp.concatenate([inv_ref[0, c], inv_ref[1, c]], axis=1)
            last = inv_ref[2, c]
            for d in (0, 2, 4):
                face = jnp.concatenate([fine_ref[d, c], fine_ref[d + 1, c]], axis=1)
                both = mm(inv, wide(face)) + mm(last, face)
                solved_ref[d, c] = both[:, :B]
                solved_ref[d + 1, c] = both[:, B:]

    solve()
    reached = jnp.max(worst) <= 1e-3

    @pl.when(jnp.logical_not(reached))
    def _():
        for c in cols:
            a, down, along, start = scaling(mats[c].astype(F32), eye)
            work[0] = a
            work[1] = one * start

            @pl.loop(0, 48)
            def _(_):
                x = work[1]
                work[1] = x + mm32(x, one - mm32(work[0], x))

            inv_ref[0, c], inv_ref[1, c], inv_ref[2, c] = thirds(work[1] * down * along)
        solve()


def shifted(own, beyond, step, edge):
    return jnp.where(edge, pltpu.roll(beyond, step, 0), pltpu.roll(own, step, 0))


def weights_of(facts_ref, halo_refs, fnorm_ref, weight_ref):
    gx, gy, gz = lax.axis_index("gx"), lax.axis_index("gy"), lax.axis_index("gz")
    ha, hb, hc, hd, hz = halo_refs
    row = lax.broadcasted_iota(jnp.int32, (8, B), 0)
    depth = row % 2
    even_x, even_y = gx % 2 == 0, gy % 2 == 0

    xa, xb = facts_in(ha), facts_in(hb)

    def pick(test, first, second, part):
        rows = pl.ds(8 * part, 8)
        return jnp.where(test, first[rows, :], second[rows, :])

    def neighbours(part):
        own = facts_ref[pl.ds(8 * part, 8), :]
        z = hz[pl.ds(8 * part, 8), :]
        return (
            jnp.where(even_x, xb[part], xa[part]),
            jnp.where(even_x, xa[part], xb[part]),
            shifted(own, pick(even_y, hd, hc, part), 2, row < 2),
            shifted(own, pick(even_y, hc, hd, part), 6, row >= 6),
            jnp.where(depth == 0, pltpu.roll(z, 7, 0), pltpu.roll(own, 1, 0)),
            jnp.where(depth == 1, pltpu.roll(z, 1, 0), pltpu.roll(own, 7, 0)),
        )

    present = (
        jnp.broadcast_to(gx > 0, (8, B)),
        jnp.broadcast_to(gx < lax.axis_size("gx") - 1, (8, B)),
        (row >= 2) | (gy > 0),
        (row < 6) | (gy < lax.axis_size("gy") - 1),
        (depth == 1) | (gz > 0),
        (depth == 0) | (gz < lax.axis_size("gz") - 1),
    )
    own_norm = facts_ref[pl.ds(0, 8), :]
    fine = facts_ref[pl.ds(8, 8), :] < 0.5
    norms, splits = neighbours(0), neighbours(1)
    total = jnp.zeros((8, B), F32)
    denom = jnp.zeros((8, B), F32)
    links = []
    for d in range(6):
        other = jnp.where(present[d], norms[d], 1.0)
        strength = jnp.where(present[d], fnorm_ref[pl.ds(8 * d, 8), :] / jnp.sqrt(own_norm * other), 0.0)
        linked = present[d] & (splits[d] > 0.5)
        total = total + strength
        denom = denom + jnp.where(linked, strength, 0.0)
        links.append(linked)
    ratio = total / jnp.where(fine, denom, 1.0)
    for d in range(6):
        weight_ref[d] = jnp.where(links[d] & fine, -ratio, 0.0)


def interp_kernel(
    split_ref, diag_ref, fine_ref, solved_ref, fnorm_ref, facts_ref, ha, hb, hc, hd, hz,
    code_ref, xa_ref, xb_ref, ya_ref, yb_ref, z_ref, near_ref, inside_ref, weight_ref,
):
    gx, gy = lax.axis_index("gx"), lax.axis_index("gy")
    fines = [fine_of(split_ref, c) for c in range(4)]
    weights_of(facts_ref, (ha, hb, hc, hd, hz), fnorm_ref, weight_ref)

    def weighted(d, c):
        return (weight_ref[d, pl.ds(2 * c + fines[c], 1), :] * solved_ref[d, c]).astype(BF16)

    for c in range(4):
        xa_ref[c] = weighted(1 - gx % 2, c)
        xb_ref[c] = weighted(gx % 2, c)
        near_ref[0, c] = weighted(2, c)
        near_ref[1, c] = weighted(3, c)
        inside_ref[c] = weighted(5 - fines[c], c)
        z_ref[0, c] = weighted(4 + fines[c], c)
    row = lax.broadcasted_iota(jnp.int32, (8, B), 0)
    lane = lax.broadcasted_iota(jnp.int32, (8, B), 1)
    bit = jnp.where((row % 2 == 0) & (lane == 0), 1, 0) * lax.shift_left(1, row // 2)
    code = jnp.zeros((8, B), F32)
    splits = (facts_in(ha)[1], facts_in(hb)[1], hc[pl.ds(8, 8), :], hd[pl.ds(8, 8), :])
    for place, flags in enumerate(splits):
        code = code + flags * (bit * (1 << (4 * place))).astype(F32)
    code = jnp.sum(jnp.sum(code, axis=0, keepdims=True), axis=1, keepdims=True)
    code_ref[...] = jnp.broadcast_to(code, (8, B)).astype(jnp.int32)
    edges = []
    for c in range(4):
        here = [(4 + fines[c], z_ref[0, c])]
        if c in (0, 3):
            here.append((c // 3 + 2, near_ref[c // 3, c]))
        found = contribs(
            diag_ref[2 * c + fines[c]], [fine_ref[d, c] for d, _ in here], [p for _, p in here]
        )
        z_ref[1, c] = found[0]
        edges += found[1:]
    up = gy % 2 == 0
    low, high = near_ref[0, 0], near_ref[1, 3]
    ya_ref[0, 0], yb_ref[0, 0] = jnp.where(up, high, low), jnp.where(up, low, high)
    low, high = edges
    ya_ref[1, 0], yb_ref[1, 0] = jnp.where(up, high, low), jnp.where(up, low, high)


def contribs(a, faces, interps):
    found = []
    for s in range(0, len(faces), 2):
        pair = interps[s:s + 2]
        face = jnp.concatenate(faces[s:s + 2], axis=1)
        hi, lo = halves(mm(a, jnp.concatenate(pair, axis=1)) + face.astype(F32))
        for t, interp in enumerate(pair):
            lanes = slice(B * t, B * t + B)
            turned = jnp.transpose(interp)
            both = jnp.concatenate([turned, turned], axis=1)
            mixed = jnp.concatenate([hi[:, lanes], lo[:, lanes]], axis=0)
            found.append(mm(both, mixed).astype(BF16))
    return found


def near_kernel(
    split_ref, diag_ref, face_ref, fine_ref, near_ref, inside_ref, xa_ref, xb_ref, z_ref,
    sum_ref, interp_ref, zero_ref, sems,
):
    gx = lax.axis_index("gx")
    fines = [fine_of(split_ref, c) for c in range(4)]
    copies = []

    def send(block, d, e):
        copies.append(pltpu.make_async_copy(block, interp_ref.at[d, e], sems.at[len(copies)]))
        copies[-1].start()

    zero_ref[...] = jnp.zeros((B, B), BF16)
    for c in range(4):
        e = 2 * c + fines[c]
        send(xa_ref.at[c], 1 - gx % 2, e)
        send(xb_ref.at[c], gx % 2, e)
        send(near_ref.at[0, c], 2, e)
        send(near_ref.at[1, c], 3, e)
        send(inside_ref.at[c], 5 - fines[c], e)
        send(z_ref.at[0, c], 4 + fines[c], e)
    for c in range(4):
        for d in range(6):
            send(zero_ref, d, 2 * c + 1 - fines[c])
    parts = [[] for _ in range(4)]
    for c in range(4):
        z = fines[c]
        here = [(c, 1 - z, 4 + z, 5 - z, inside_ref[c])]
        if c > 0:
            here.append((c - 1, z, 3, 2, near_ref[0, c]))
        if c < 3:
            here.append((c + 1, z, 2, 3, near_ref[1, c]))
        found = contribs(
            diag_ref[2 * c + z], [fine_ref[d, c] for _, _, _, d, _ in here], [p for *_, p in here]
        )
        for (to, depth, back, _, interp), contrib in zip(here, found):
            product = mm(face_ref[back, 2 * to + depth], interp)
            parts[to].append((depth, contrib.astype(F32) + product))
    for c in range(4):
        for k in range(2):
            total = diag_ref[2 * c + k].astype(F32)
            for z, part in parts[c]:
                total = total + jnp.where(z == k, part, 0.0)
            sum_ref[2 * c + k] = total
    for copy in copies:
        copy.wait()


def coarse_kernel(
    split_ref, code_ref, sum_ref, face_ref, ha, hb, xa_ref, xb_ref, ya_ref, yb_ref, z_ref,
    coarse_ref, total_ref, sems,
):
    gx, gy, gz = lax.axis_index("gx"), lax.axis_index("gy"), lax.axis_index("gz")
    code = code_ref[0, 0]
    up = gy % 2 == 0

    def bit_at(place):
        return lax.shift_right_logical(code, place) & 1

    copies = []
    for c in (1, 2, 0, 3):
        arrived = [(1 - gz, 5 - gz, z_ref[0, c], z_ref[1, c])]
        for z, d, sent, ref in (
            (bit_at(c), 1 - gx % 2, ha, xa_ref), (bit_at(4 + c), gx % 2, hb, xb_ref)
        ):
            theirs, face = sent[pl.ds(B * c, B), :], sent[pl.ds(B * (4 + c), B), :]
            arrived.append((z, d, ref[c], contribs(theirs, [face], [ref[c]])[0]))
        if c in (0, 3):
            first = up if c == 3 else jnp.logical_not(up)
            edge = 0 if c == 3 else 3
            z = jnp.where(first, bit_at(8 + edge), bit_at(12 + edge))
            pair = [jnp.where(first, ya_ref[k, 0], yb_ref[k, 0]) for k in range(2)]
            arrived.append((z, 3 if c == 3 else 2, *pair))
        totals = [sum_ref[2 * c], sum_ref[2 * c + 1]]
        parts = [
            (z, contrib.astype(F32) + mm(face_ref[d, 2 * c + z], interp))
            for z, d, interp, contrib in arrived
        ]
        for k in range(2):
            e = 2 * c + k
            keep = split_at(split_ref, c, k) == 1
            for z, part in parts:
                totals[k] = totals[k] + jnp.where(z == k, part, 0.0)
            total_ref[e] = jnp.where(keep, totals[k], 0.0)
            copies.append(pltpu.make_async_copy(total_ref.at[e], coarse_ref.at[e], sems.at[e]))
            copies[-1].start()
    for copy in copies:
        copy.wait()


def matching(size, start):
    pairs = [(i, i + 1) for i in range(start, size - 1, 2)]
    return pairs + [(b, a) for a, b in pairs]


def swap(x, axis, start):
    return lax.ppermute(x, axis, matching(lax.axis_size(axis), start))


def call(body, out_shape, in_specs, out_specs, scratch, flops):
    return pl.pallas_call(
        body,
        out_shape=out_shape,
        in_specs=in_specs,
        out_specs=out_specs,
        scratch_shapes=scratch,
        compiler_params=pltpu.CompilerParams(vmem_limit_bytes=LIMIT),
        cost_estimate=pl.CostEstimate(flops=flops, bytes_accessed=2 << 20, transcendentals=0),
    )


def on_device(diag_blocks, face_blocks, split):
    diag = diag_blocks.reshape(8, B, B)
    face = face_blocks.reshape(6, 8, B, B)
    split = jnp.transpose(split, (0, 2, 1))
    sds = jax.ShapeDtypeStruct
    dma = pltpu.SemaphoreType.DMA
    in_hbm = lambda x: pltpu.with_memory_space_constraint(x, pltpu.HBM)
    blocks = lambda *lead: sds(lead + (B, B), BF16)
    packed = sds((8 * B + 32, B), BF16)
    facts, flags, diag, pa, pb = call(
        facts_kernel,
        (sds((16, B), F32), sds((8, B), jnp.int32), blocks(8), packed, packed),
        [HBM] * 3, (VMEM,) * 5,
        [pltpu.VMEM((8, B), F32), pltpu.SMEM((1, 2, 4), jnp.int32), dma((25,))], 1 << 20,
    )(in_hbm(split), in_hbm(diag), in_hbm(face))
    ha, hb = swap(pa, "gx", 0), swap(pb, "gx", 1)
    hc, hd = swap(facts, "gy", 0), swap(facts, "gy", 1)
    hz = swap(facts, "gz", 0)
    solved, fnorm, fine = call(
        inverse_kernel, (sds((6, 4, B, B), F32), sds((48, B), F32), blocks(6, 4)),
        [SMEM, VMEM, HBM], (VMEM, VMEM, VMEM),
        [
            pltpu.VMEM((3, 4, B, B), BF16), pltpu.VMEM((48, B), F32), pltpu.VMEM((2, B, B), F32),
            dma((24,)),
        ],
        1 << 30,
    )(flags, diag, in_hbm(face))
    code, xa, xb, ya, yb, z, near, inside = call(
        interp_kernel,
        (
            sds((8, B), jnp.int32), blocks(4), blocks(4), blocks(2, 1),
            blocks(2, 1), blocks(2, 4), blocks(2, 4), blocks(4),
        ),
        [SMEM] + [VMEM] * 10, (VMEM,) * 8, [pltpu.VMEM((6, 8, B), F32)], 1 << 30,
    )(flags, diag, fine, solved, fnorm, facts, ha, hb, hc, hd, hz)
    sa, sb = swap(xa, "gx", 0), swap(xb, "gx", 1)
    ya, yb = swap(ya, "gy", 0), swap(yb, "gy", 1)
    sz = swap(z, "gz", 0)
    total, interp = call(
        near_kernel, (sds((8, B, B), F32), blocks(6, 8)), [SMEM] + [VMEM] * 8, (VMEM, HBM),
        [pltpu.VMEM((B, B), BF16), dma((48,))], 1 << 30,
    )(flags, diag, face, fine, near, inside, xa, xb, z)
    coarse = call(
        coarse_kernel, sds((8, B, B), F32), [SMEM, SMEM] + [VMEM] * 9, HBM,
        [pltpu.VMEM((8, B, B), F32), dma((8,))], 1 << 30,
    )(flags, code, total, face, ha, hb, sa, sb, ya, yb, sz)
    return interp.reshape(face_blocks.shape), coarse.reshape(diag_blocks.shape)


def solution(mesh):
    in_specs = (
        P("gx", "gy", "gz", None, None),
        P(None, "gx", "gy", "gz", None, None),
        P("gx", "gy", "gz"),
    )
    out_specs = (P(None, "gx", "gy", "gz", None, None), P("gx", "gy", "gz", None, None))
    return jax.shard_map(
        on_device, mesh=mesh, in_specs=in_specs, out_specs=out_specs, check_vma=False
    )
```

```python
import jax
import jax.numpy as jnp
from jax import lax
from jax.experimental import pallas as pl
from jax.experimental.pallas import tpu as pltpu
from jax.sharding import PartitionSpec as P


B = 128
F32 = jnp.float32
BF16 = jnp.bfloat16
VMEM = pl.BlockSpec(memory_space=pltpu.VMEM)
HBM = pl.BlockSpec(memory_space=pltpu.HBM)
LIMIT = 24 * 1024 * 1024


def mm(a, b):
    return jnp.dot(a, b, preferred_element_type=F32)


def mm32(a, b):
    return jnp.dot(a, b, preferred_element_type=F32, precision=lax.Precision.HIGHEST)


def halves(x):
    hi = x.astype(BF16)
    return hi, (x - hi.astype(F32)).astype(BF16)


def thirds(x):
    hi = x.astype(BF16)
    rest = x - hi.astype(F32)
    mid = rest.astype(BF16)
    return hi, mid, (rest - mid.astype(F32)).astype(BF16)


def wide(x):
    return jnp.concatenate([x, x], axis=0)


def split_at(flags, c, z):
    return lax.shift_right_logical(flags, 2 * c + z) & 1


def fine_of(flags, c):
    return split_at(flags, c, 0)


def square_sums(x):
    x = x.astype(F32)
    return jnp.sum(x * x, axis=0, keepdims=True)


def norms_of(rows):
    return jnp.broadcast_to(jnp.sqrt(jnp.sum(rows, axis=1, keepdims=True)), rows.shape)


def facts_kernel(
    split_ref, diag_ref, face_ref, facts_ref, flags_ref, kept_ref, xa_ref, xb_ref, rows, held, faces, sems
):
    gx = lax.axis_index("gx")
    copies = [
        pltpu.make_async_copy(split_ref, held, sems.at[0]),
        pltpu.make_async_copy(diag_ref, kept_ref, sems.at[1]),
        pltpu.make_async_copy(face_ref.at[pl.ds(0, 2)], faces, sems.at[2]),
    ]
    for copy in copies:
        copy.start()
    copies[0].wait()
    row = lax.broadcasted_iota(jnp.int32, (8, B), 0)
    splits = [held[0, e % 2, e // 2] for e in range(8)]
    flags = jnp.zeros((8, B), F32)
    code = 0
    for e, split in enumerate(splits):
        flags = jnp.where(row == e, split.astype(F32), flags)
        code = code + split * (1 << e)
    flags_ref[...] = jnp.full((8, B), code, jnp.int32)
    facts_ref[pl.ds(8, 8), :] = flags
    copies[1].wait()
    for e in range(8):
        rows[pl.ds(e, 1), :] = square_sums(kept_ref[e])
    norms = norms_of(rows[...])
    facts_ref[pl.ds(0, 8), :] = norms
    copies[2].wait()
    for c in range(4):
        e = 2 * c + splits[2 * c]
        block = kept_ref[e]
        for ref, d in ((xa_ref, 1 - gx % 2), (xb_ref, gx % 2)):
            ref[pl.ds(B * c, B), :] = block
            ref[pl.ds(B * (4 + c), B), :] = faces[d, e]
    parts = [part.astype(F32) for part in thirds(norms)] + [flags]
    for ref in (xa_ref, xb_ref):
        for k in range(2):
            both = jnp.concatenate(parts[2 * k:2 * k + 2], axis=0)
            ref[pl.ds(8 * B + 16 * k, 16), :] = both.astype(BF16)


def facts_in(ref):
    high, low = ref[pl.ds(8 * B, 16), :].astype(F32), ref[pl.ds(8 * B + 16, 16), :].astype(F32)
    return high[:8] + high[8:] + low[:8], low[8:]


def scaling(a, eye):
    picked = jnp.where(eye, a, 0.0)
    down = lax.rsqrt(jnp.sum(picked, axis=1, keepdims=True))
    along = lax.rsqrt(jnp.sum(picked, axis=0, keepdims=True))
    a = a * down * along
    bound = jnp.max(jnp.sum(jnp.abs(a), axis=0, keepdims=True), axis=1, keepdims=True)
    return a, down, along, 1.9 / bound


def inverse_kernel(
    split_ref, diag_ref, face_ref, solved_ref, fnorm_ref, fine_ref, inv_ref, rows, work, sems
):
    cols = range(4)
    flags = split_ref[...][0, 0]
    copies = []
    for c in cols:
        e = 2 * c + fine_of(flags, c)
        copies.append(pltpu.make_async_copy(face_ref.at[:, e], fine_ref.at[:, c], sems.at[c]))
        copies[-1].start()
    eye = (
        lax.broadcasted_iota(jnp.int32, (B, B), 0) == lax.broadcasted_iota(jnp.int32, (B, B), 1)
    )
    one = jnp.where(eye, 1.0, 0.0).astype(F32)
    mats = [diag_ref[2 * c + fine_of(flags, c)] for c in cols]
    parts = [scaling(m.astype(F32), eye) for m in mats]
    powers = [one - start * a for a, _, _, start in parts]
    sums = [one + p for p in powers]
    powers = [p.astype(BF16) for p in powers]
    for _ in range(4):
        powers = [mm(p, p).astype(BF16) for p in powers]
        sums = [s + mm(s.astype(BF16), p) for s, p in zip(sums, powers)]
    guess = [
        (s * (start * down) * along).astype(BF16) for s, (_, down, along, start) in zip(sums, parts)
    ]
    left = [one - mm(mats[c], guess[c]) for c in cols]
    small = [r.astype(BF16) for r in left]
    left = [r + mm(b, b) for r, b in zip(left, small)]
    better = []
    for c in cols:
        hi, lo = halves(left[c])
        better.append(guess[c].astype(F32) + (mm(guess[c], hi) + mm(guess[c], lo)))
    pairs = [halves(x) for x in better]
    left = [one - (mm(mats[c], pairs[c][0]) + mm(mats[c], pairs[c][1])) for c in cols]
    worst = jnp.zeros((1, B), F32)
    for c in cols:
        hi, lo = pairs[c]
        rhi, rlo = halves(left[c])
        fixed = (hi.astype(F32) + lo.astype(F32)) + (mm(hi, rhi) + (mm(hi, rlo) + mm(lo, rhi)))
        inv_ref[0, c], inv_ref[1, c], inv_ref[2, c] = thirds(fixed)
        worst = worst + jnp.sum(jnp.abs(left[c]), axis=0, keepdims=True)
    for copy in copies:
        copy.wait()
    for d in range(6):
        for c in cols:
            sums = square_sums(fine_ref[d, c])
            rows[pl.ds(8 * d + 2 * c, 1), :] = sums
            rows[pl.ds(8 * d + 2 * c + 1, 1), :] = sums
    fnorm_ref[...] = norms_of(rows[...])

    def solve():
        for c in cols:
            inv = jnp.concatenate([inv_ref[0, c], inv_ref[1, c]], axis=1)
            last = inv_ref[2, c]
            for d in (0, 2, 4):
                face = jnp.concatenate([fine_ref[d, c], fine_ref[d + 1, c]], axis=1)
                both = mm(inv, wide(face)) + mm(last, face)
                solved_ref[d, c] = both[:, :B]
                solved_ref[d + 1, c] = both[:, B:]

    solve()
    reached = jnp.max(worst) <= 1e-3

    @pl.when(jnp.logical_not(reached))
    def _():
        for c in cols:
            a, down, along, start = scaling(mats[c].astype(F32), eye)
            work[0] = a
            work[1] = one * start

            @pl.loop(0, 48)
            def _(_):
                x = work[1]
                work[1] = x + mm32(x, one - mm32(work[0], x))

            inv_ref[0, c], inv_ref[1, c], inv_ref[2, c] = thirds(work[1] * down * along)
        solve()


def shifted(own, beyond, step, edge):
    return jnp.where(edge, pltpu.roll(beyond, step, 0), pltpu.roll(own, step, 0))


def weights_of(facts_ref, halo_refs, fnorm_ref, weight_ref):
    gx, gy, gz = lax.axis_index("gx"), lax.axis_index("gy"), lax.axis_index("gz")
    ha, hb, hc, hd, hz = halo_refs
    row = lax.broadcasted_iota(jnp.int32, (8, B), 0)
    depth = row % 2
    even_x, even_y = gx % 2 == 0, gy % 2 == 0

    xa, xb = facts_in(ha), facts_in(hb)

    def pick(test, first, second, part):
        rows = pl.ds(8 * part, 8)
        return jnp.where(test, first[rows, :], second[rows, :])

    def neighbours(part):
        own = facts_ref[pl.ds(8 * part, 8), :]
        z = hz[pl.ds(8 * part, 8), :]
        return (
            jnp.where(even_x, xb[part], xa[part]),
            jnp.where(even_x, xa[part], xb[part]),
            shifted(own, pick(even_y, hd, hc, part), 2, row < 2),
            shifted(own, pick(even_y, hc, hd, part), 6, row >= 6),
            jnp.where(depth == 0, pltpu.roll(z, 7, 0), pltpu.roll(own, 1, 0)),
            jnp.where(depth == 1, pltpu.roll(z, 1, 0), pltpu.roll(own, 7, 0)),
        )

    present = (
        jnp.broadcast_to(gx > 0, (8, B)),
        jnp.broadcast_to(gx < lax.axis_size("gx") - 1, (8, B)),
        (row >= 2) | (gy > 0),
        (row < 6) | (gy < lax.axis_size("gy") - 1),
        (depth == 1) | (gz > 0),
        (depth == 0) | (gz < lax.axis_size("gz") - 1),
    )
    own_norm = facts_ref[pl.ds(0, 8), :]
    fine = facts_ref[pl.ds(8, 8), :] < 0.5
    norms, splits = neighbours(0), neighbours(1)
    total = jnp.zeros((8, B), F32)
    denom = jnp.zeros((8, B), F32)
    links = []
    for d in range(6):
        other = jnp.where(present[d], norms[d], 1.0)
        strength = jnp.where(present[d], fnorm_ref[pl.ds(8 * d, 8), :] / jnp.sqrt(own_norm * other), 0.0)
        linked = present[d] & (splits[d] > 0.5)
        total = total + strength
        denom = denom + jnp.where(linked, strength, 0.0)
        links.append(linked)
    ratio = total / jnp.where(fine, denom, 1.0)
    for d in range(6):
        weight_ref[d] = jnp.where(links[d] & fine, -ratio, 0.0)


def interp_kernel(
    split_ref, diag_ref, fine_ref, solved_ref, fnorm_ref, facts_ref, ha, hb, hc, hd, hz,
    code_ref, xa_ref, xb_ref, ya_ref, yb_ref, z_ref, all_ref, weight_ref,
):
    gx, gy = lax.axis_index("gx"), lax.axis_index("gy")
    flags = split_ref[...][0, 0]
    fines = [fine_of(flags, c) for c in range(4)]
    weights_of(facts_ref, (ha, hb, hc, hd, hz), fnorm_ref, weight_ref)

    even_x = gx % 2 == 0
    for c in range(4):
        for d in range(6):
            weight = weight_ref[d, pl.ds(2 * c + fines[c], 1), :]
            all_ref[d, c] = (weight * solved_ref[d, c]).astype(BF16)
        low, high = all_ref[0, c], all_ref[1, c]
        xa_ref[c] = jnp.where(even_x, high, low)
        xb_ref[c] = jnp.where(even_x, low, high)
        z_ref[0, c] = all_ref[4 + fines[c], c]
    row = lax.broadcasted_iota(jnp.int32, (8, B), 0)
    lane = lax.broadcasted_iota(jnp.int32, (8, B), 1)
    bit = jnp.where((row % 2 == 0) & (lane == 0), 1, 0) * lax.shift_left(1, row // 2)
    code = jnp.zeros((8, B), F32)
    splits = (facts_in(ha)[1], facts_in(hb)[1], hc[pl.ds(8, 8), :], hd[pl.ds(8, 8), :])
    for place, theirs in enumerate(splits):
        code = code + theirs * (bit * (1 << (4 * place))).astype(F32)
    code = jnp.sum(jnp.sum(code, axis=0, keepdims=True), axis=1, keepdims=True)
    code_ref[...] = jnp.broadcast_to(code, (8, B)).astype(jnp.int32)
    edges = []
    for c in range(4):
        here = [(4 + fines[c], z_ref[0, c])]
        if c in (0, 3):
            here.append((c // 3 + 2, all_ref[c // 3 + 2, c]))
        found = contribs(
            diag_ref[2 * c + fines[c]], [fine_ref[d, c] for d, _ in here], [p for _, p in here]
        )
        z_ref[1, c] = found[0]
        edges += found[1:]
    up = gy % 2 == 0
    low, high = all_ref[2, 0], all_ref[3, 3]
    ya_ref[0, 0], yb_ref[0, 0] = jnp.where(up, high, low), jnp.where(up, low, high)
    low, high = edges
    ya_ref[1, 0], yb_ref[1, 0] = jnp.where(up, high, low), jnp.where(up, low, high)


def contribs(a, faces, interps):
    found = []
    for s in range(0, len(faces), 2):
        pair = interps[s:s + 2]
        face = jnp.concatenate(faces[s:s + 2], axis=1)
        hi, lo = halves(mm(a, jnp.concatenate(pair, axis=1)) + face.astype(F32))
        for t, interp in enumerate(pair):
            lanes = slice(B * t, B * t + B)
            turned = jnp.transpose(interp)
            both = jnp.concatenate([turned, turned], axis=1)
            mixed = jnp.concatenate([hi[:, lanes], lo[:, lanes]], axis=0)
            found.append(mm(both, mixed).astype(BF16))
    return found


def near_kernel(
    split_ref, diag_ref, face_ref, fine_ref, all_ref, sum_ref, interp_ref, zero_ref, sems
):
    flags = split_ref[...][0, 0]
    fines = [fine_of(flags, c) for c in range(4)]
    zero_ref[...] = jnp.zeros((6, B, B), BF16)
    copies = []
    for c in range(4):
        e = 2 * c + fines[c]
        for block, to in ((all_ref.at[:, c], e), (zero_ref, 4 * c + 1 - e)):
            copies.append(pltpu.make_async_copy(block, interp_ref.at[:, to], sems.at[len(copies)]))
    for copy in copies[::2] + copies[1::2]:
        copy.start()
    parts = [[] for _ in range(4)]
    for c in range(4):
        z = fines[c]
        here = [(c, 1 - z, 4 + z, 5 - z, all_ref[5 - z, c])]
        if c > 0:
            here.append((c - 1, z, 3, 2, all_ref[2, c]))
        if c < 3:
            here.append((c + 1, z, 2, 3, all_ref[3, c]))
        found = contribs(
            diag_ref[2 * c + z], [fine_ref[d, c] for _, _, _, d, _ in here], [p for *_, p in here]
        )
        for (to, depth, back, _, interp), contrib in zip(here, found):
            product = mm(face_ref[back, 2 * to + depth], interp)
            parts[to].append((depth, contrib.astype(F32) + product))
    for c in range(4):
        for k in range(2):
            total = diag_ref[2 * c + k].astype(F32)
            for z, part in parts[c]:
                total = total + jnp.where(z == k, part, 0.0)
            sum_ref[2 * c + k] = total
    for copy in copies:
        copy.wait()


def bit_at(code, place):
    return lax.shift_right_logical(code, place) & 1


def from_x(z, d, sent, interp, c):
    theirs, face = sent[pl.ds(B * c, B), :], sent[pl.ds(B * (4 + c), B), :]
    return z, d, interp[c], contribs(theirs, [face], [interp[c]])[0]


def added(c, arrived, sum_ref, face_ref):
    totals = [sum_ref[2 * c], sum_ref[2 * c + 1]]
    for z, d, interp, contrib in arrived:
        part = contrib.astype(F32) + mm(face_ref[d, 2 * c + z], interp)
        totals = [total + jnp.where(z == k, part, 0.0) for k, total in enumerate(totals)]
    return totals


def middle_kernel(code_ref, sum_ref, face_ref, ha, xa_ref, z_ref, total_ref):
    gx, gz = lax.axis_index("gx"), lax.axis_index("gz")
    code = code_ref[...][0, 0]
    for c in range(4):
        arrived = [
            (1 - gz, 5 - gz, z_ref[0, c], z_ref[1, c]),
            from_x(bit_at(code, c), 1 - gx % 2, ha, xa_ref, c),
        ]
        totals = added(c, arrived, sum_ref, face_ref)
        total_ref[2 * c], total_ref[2 * c + 1] = totals


def coarse_kernel(
    split_ref, code_ref, sum_ref, face_ref, hb, xb_ref, ya_ref, yb_ref,
    coarse_ref, total_ref, sems,
):
    gx, gy = lax.axis_index("gx"), lax.axis_index("gy")
    code = code_ref[...][0, 0]
    up = gy % 2 == 0
    flags = split_ref[...][0, 0]
    copies = []
    for c in (1, 2, 0, 3):
        arrived = [from_x(bit_at(code, 4 + c), gx % 2, hb, xb_ref, c)]
        if c in (0, 3):
            first = up if c == 3 else jnp.logical_not(up)
            edge = 0 if c == 3 else 3
            z = jnp.where(first, bit_at(code, 8 + edge), bit_at(code, 12 + edge))
            pair = [jnp.where(first, ya_ref[k, 0], yb_ref[k, 0]) for k in range(2)]
            arrived.append((z, 3 if c == 3 else 2, *pair))
        totals = added(c, arrived, sum_ref, face_ref)
        for k in range(2):
            e = 2 * c + k
            keep = split_at(flags, c, k) == 1
            total_ref[e] = jnp.where(keep, totals[k], 0.0)
            copies.append(pltpu.make_async_copy(total_ref.at[e], coarse_ref.at[e], sems.at[e]))
            copies[-1].start()
    for copy in copies:
        copy.wait()


def matching(size, start):
    pairs = [(i, i + 1) for i in range(start, size - 1, 2)]
    return pairs + [(b, a) for a, b in pairs]


def swap(x, axis, start):
    return lax.ppermute(x, axis, matching(lax.axis_size(axis), start))


def call(body, out_shape, in_specs, out_specs, scratch, flops):
    return pl.pallas_call(
        body,
        out_shape=out_shape,
        in_specs=in_specs,
        out_specs=out_specs,
        scratch_shapes=scratch,
        compiler_params=pltpu.CompilerParams(vmem_limit_bytes=LIMIT),
        cost_estimate=pl.CostEstimate(flops=flops, bytes_accessed=2 << 20, transcendentals=0),
    )


def on_device(diag_blocks, face_blocks, split):
    diag = diag_blocks.reshape(8, B, B)
    face = face_blocks.reshape(6, 8, B, B)
    split = jnp.transpose(split, (0, 2, 1))
    sds = jax.ShapeDtypeStruct
    dma = pltpu.SemaphoreType.DMA
    in_hbm = lambda x: pltpu.with_memory_space_constraint(x, pltpu.HBM)
    blocks = lambda *lead: sds(lead + (B, B), BF16)
    packed = sds((8 * B + 32, B), BF16)
    facts, flags, diag, pa, pb = call(
        facts_kernel,
        (sds((16, B), F32), sds((8, B), jnp.int32), blocks(8), packed, packed),
        [HBM] * 3, (VMEM,) * 5,
        [
            pltpu.VMEM((8, B), F32), pltpu.SMEM((1, 2, 4), jnp.int32),
            pltpu.VMEM((2, 8, B, B), BF16), dma((3,)),
        ],
        1 << 20,
    )(in_hbm(split), in_hbm(diag), in_hbm(face))
    ha, hb = swap(pa, "gx", 0), swap(pb, "gx", 1)
    hc, hd = swap(facts, "gy", 0), swap(facts, "gy", 1)
    hz = swap(facts, "gz", 0)
    solved, fnorm, fine = call(
        inverse_kernel, (sds((6, 4, B, B), F32), sds((48, B), F32), blocks(6, 4)),
        [VMEM, VMEM, HBM], (VMEM, VMEM, VMEM),
        [
            pltpu.VMEM((3, 4, B, B), BF16), pltpu.VMEM((48, B), F32), pltpu.VMEM((2, B, B), F32),
            dma((4,)),
        ],
        1 << 30,
    )(flags, diag, in_hbm(face))
    code, xa, xb, ya, yb, z, both = call(
        interp_kernel,
        (
            sds((8, B), jnp.int32), blocks(4), blocks(4), blocks(2, 1),
            blocks(2, 1), blocks(2, 4), blocks(6, 4),
        ),
        [VMEM] + [VMEM] * 10, (VMEM,) * 7, [pltpu.VMEM((6, 8, B), F32)], 1 << 30,
    )(flags, diag, fine, solved, fnorm, facts, ha, hb, hc, hd, hz)
    xa, xb = swap(xa, "gx", 0), swap(xb, "gx", 1)
    ya, yb = swap(ya, "gy", 0), swap(yb, "gy", 1)
    z = swap(z, "gz", 0)
    total, interp = call(
        near_kernel, (sds((8, B, B), F32), blocks(6, 8)), [VMEM] + [VMEM] * 4, (VMEM, HBM),
        [pltpu.VMEM((6, B, B), BF16), dma((8,))], 1 << 30,
    )(flags, diag, face, fine, both)
    total = call(
        middle_kernel, sds((8, B, B), F32), [VMEM] + [VMEM] * 5, VMEM, [], 1 << 30,
    )(code, total, face, ha, xa, z)
    coarse = call(
        coarse_kernel, sds((8, B, B), F32), [VMEM] * 8, HBM,
        [pltpu.VMEM((8, B, B), F32), dma((8,))], 1 << 30,
    )(flags, code, total, face, hb, xb, ya, yb)
    return interp.reshape(face_blocks.shape), coarse.reshape(diag_blocks.shape)


def solution(mesh):
    in_specs = (
        P("gx", "gy", "gz", None, None),
        P(None, "gx", "gy", "gz", None, None),
        P("gx", "gy", "gz"),
    )
    out_specs = (P(None, "gx", "gy", "gz", None, None), P("gx", "gy", "gz", None, None))
    return jax.shard_map(
        on_device, mesh=mesh, in_specs=in_specs, out_specs=out_specs, check_vma=False
    )
```

```python
import jax
import jax.numpy as jnp
from jax import lax
from jax.experimental import pallas as pl
from jax.experimental.pallas import tpu as pltpu
from jax.sharding import PartitionSpec as P


B = 128
F32 = jnp.float32
BF16 = jnp.bfloat16
VMEM = pl.BlockSpec(memory_space=pltpu.VMEM)
HBM = pl.BlockSpec(memory_space=pltpu.HBM)
LIMIT = 24 * 1024 * 1024


def mm(a, b):
    return jnp.dot(a, b, preferred_element_type=F32)


def mm32(a, b):
    return jnp.dot(a, b, preferred_element_type=F32, precision=lax.Precision.HIGHEST)


def halves(x):
    hi = x.astype(BF16)
    return hi, (x - hi.astype(F32)).astype(BF16)


def thirds(x):
    hi = x.astype(BF16)
    rest = x - hi.astype(F32)
    mid = rest.astype(BF16)
    return hi, mid, (rest - mid.astype(F32)).astype(BF16)


def wide(x):
    return jnp.concatenate([x, x], axis=0)


def split_at(flags, c, z):
    return lax.shift_right_logical(flags, 2 * c + z) & 1


def fine_of(flags, c):
    return split_at(flags, c, 0)


def square_sums(x):
    x = x.astype(F32)
    return jnp.sum(x * x, axis=0, keepdims=True)


def norms_of(rows):
    return jnp.broadcast_to(jnp.sqrt(jnp.sum(rows, axis=1, keepdims=True)), rows.shape)


def facts_kernel(
    split_ref, diag_ref, face_ref,
    facts_ref, flags_ref, kept_ref, xa_ref, xb_ref, z_ref, rows, held, faces, sems,
):
    gx, gz = lax.axis_index("gx"), lax.axis_index("gz")
    copies = [
        pltpu.make_async_copy(split_ref, held, sems.at[0]),
        pltpu.make_async_copy(diag_ref, kept_ref, sems.at[1]),
        pltpu.make_async_copy(face_ref.at[pl.ds(0, 2)], faces, sems.at[2]),
    ]
    for c in range(4):
        block, into = face_ref.at[5 - gz, 2 * c + 1 - gz], z_ref.at[pl.ds(B * (4 + c), B), :]
        copies.append(pltpu.make_async_copy(block, into, sems.at[3 + c]))
    for copy in copies:
        copy.start()
    copies[0].wait()
    row = lax.broadcasted_iota(jnp.int32, (8, B), 0)
    splits = [held[0, e % 2, e // 2] for e in range(8)]
    flags = jnp.zeros((8, B), F32)
    code = 0
    for e, split in enumerate(splits):
        flags = jnp.where(row == e, split.astype(F32), flags)
        code = code + split * (1 << e)
    flags_ref[...] = jnp.full((8, B), code, jnp.int32)
    facts_ref[pl.ds(8, 8), :] = flags
    copies[1].wait()
    for e in range(8):
        rows[pl.ds(e, 1), :] = square_sums(kept_ref[e])
    norms = norms_of(rows[...])
    facts_ref[pl.ds(0, 8), :] = norms
    parts = [part.astype(F32) for part in thirds(norms)] + [flags]
    for ref in (xa_ref, xb_ref, z_ref):
        for k in range(2):
            both = jnp.concatenate(parts[2 * k:2 * k + 2], axis=0)
            ref[pl.ds(8 * B + 16 * k, 16), :] = both.astype(BF16)
    for copy in copies[2:]:
        copy.wait()
    for c in range(4):
        e = 2 * c + splits[2 * c]
        block = kept_ref[e]
        z_ref[pl.ds(B * c, B), :] = kept_ref[2 * c + 1 - gz]
        for ref, d in ((xa_ref, 1 - gx % 2), (xb_ref, gx % 2)):
            ref[pl.ds(B * c, B), :] = block
            ref[pl.ds(B * (4 + c), B), :] = faces[d, e]


def facts_in(ref):
    high, low = ref[pl.ds(8 * B, 16), :].astype(F32), ref[pl.ds(8 * B + 16, 16), :].astype(F32)
    return high[:8] + high[8:] + low[:8], low[8:]


def scaling(a, eye):
    picked = jnp.where(eye, a, 0.0)
    down = lax.rsqrt(jnp.sum(picked, axis=1, keepdims=True))
    along = lax.rsqrt(jnp.sum(picked, axis=0, keepdims=True))
    a = a * down * along
    bound = jnp.max(jnp.sum(jnp.abs(a), axis=0, keepdims=True), axis=1, keepdims=True)
    return a, down, along, 1.9 / bound


def inverse_kernel(
    split_ref, diag_ref, face_ref, solved_ref, fnorm_ref, fine_ref, inv_ref, rows, work, sems
):
    cols = range(4)
    flags = split_ref[...][0, 0]
    copies = []
    for c in cols:
        e = 2 * c + fine_of(flags, c)
        copies.append(pltpu.make_async_copy(face_ref.at[:, e], fine_ref.at[:, c], sems.at[c]))
        copies[-1].start()
    eye = (
        lax.broadcasted_iota(jnp.int32, (B, B), 0) == lax.broadcasted_iota(jnp.int32, (B, B), 1)
    )
    one = jnp.where(eye, 1.0, 0.0).astype(F32)
    mats = [diag_ref[2 * c + fine_of(flags, c)] for c in cols]
    parts = [scaling(m.astype(F32), eye) for m in mats]
    powers = [one - start * a for a, _, _, start in parts]
    sums = [one + p for p in powers]
    powers = [p.astype(BF16) for p in powers]
    for _ in range(4):
        powers = [mm(p, p).astype(BF16) for p in powers]
        sums = [s + mm(s.astype(BF16), p) for s, p in zip(sums, powers)]
    guess = [
        (s * (start * down) * along).astype(BF16) for s, (_, down, along, start) in zip(sums, parts)
    ]
    left = [one - mm(mats[c], guess[c]) for c in cols]
    small = [r.astype(BF16) for r in left]
    left = [r + mm(b, b) for r, b in zip(left, small)]
    better = []
    for c in cols:
        hi, lo = halves(left[c])
        better.append(guess[c].astype(F32) + (mm(guess[c], hi) + mm(guess[c], lo)))
    pairs = [halves(x) for x in better]
    left = [one - (mm(mats[c], pairs[c][0]) + mm(mats[c], pairs[c][1])) for c in cols]
    worst = jnp.zeros((1, B), F32)
    for c in cols:
        hi, lo = pairs[c]
        rhi, rlo = halves(left[c])
        fixed = (hi.astype(F32) + lo.astype(F32)) + (mm(hi, rhi) + (mm(hi, rlo) + mm(lo, rhi)))
        inv_ref[0, c], inv_ref[1, c], inv_ref[2, c] = thirds(fixed)
        worst = worst + jnp.sum(jnp.abs(left[c]), axis=0, keepdims=True)
    for copy in copies:
        copy.wait()
    for d in range(6):
        for c in cols:
            sums = square_sums(fine_ref[d, c])
            rows[pl.ds(8 * d + 2 * c, 1), :] = sums
            rows[pl.ds(8 * d + 2 * c + 1, 1), :] = sums
    fnorm_ref[...] = norms_of(rows[...])

    def solve():
        for c in cols:
            inv = jnp.concatenate([inv_ref[0, c], inv_ref[1, c]], axis=1)
            last = inv_ref[2, c]
            for d in (0, 2, 4):
                face = jnp.concatenate([fine_ref[d, c], fine_ref[d + 1, c]], axis=1)
                both = mm(inv, wide(face)) + mm(last, face)
                solved_ref[d, c] = both[:, :B]
                solved_ref[d + 1, c] = both[:, B:]

    solve()
    reached = jnp.max(worst) <= 1e-3

    @pl.when(jnp.logical_not(reached))
    def _():
        for c in cols:
            a, down, along, start = scaling(mats[c].astype(F32), eye)
            work[0] = a
            work[1] = one * start

            @pl.loop(0, 48)
            def _(_):
                x = work[1]
                work[1] = x + mm32(x, one - mm32(work[0], x))

            inv_ref[0, c], inv_ref[1, c], inv_ref[2, c] = thirds(work[1] * down * along)
        solve()


def shifted(own, beyond, step, edge):
    return jnp.where(edge, pltpu.roll(beyond, step, 0), pltpu.roll(own, step, 0))


def weights_of(facts_ref, halo_refs, fnorm_ref, weight_ref):
    gx, gy, gz = lax.axis_index("gx"), lax.axis_index("gy"), lax.axis_index("gz")
    ha, hb, hc, hd, hz = halo_refs
    row = lax.broadcasted_iota(jnp.int32, (8, B), 0)
    depth = row % 2
    even_x, even_y = gx % 2 == 0, gy % 2 == 0

    xa, xb, beyond = facts_in(ha), facts_in(hb), facts_in(hz)
    ya, yb = (hc[pl.ds(0, 8), :], hc[pl.ds(8, 8), :]), (hd[pl.ds(0, 8), :], hd[pl.ds(8, 8), :])

    def neighbours(part):
        own = facts_ref[pl.ds(8 * part, 8), :]
        z = beyond[part]
        return (
            jnp.where(even_x, xb[part], xa[part]),
            jnp.where(even_x, xa[part], xb[part]),
            shifted(own, jnp.where(even_y, yb[part], ya[part]), 2, row < 2),
            shifted(own, jnp.where(even_y, ya[part], yb[part]), 6, row >= 6),
            jnp.where(depth == 0, pltpu.roll(z, 7, 0), pltpu.roll(own, 1, 0)),
            jnp.where(depth == 1, pltpu.roll(z, 1, 0), pltpu.roll(own, 7, 0)),
        )

    present = (
        jnp.broadcast_to(gx > 0, (8, B)),
        jnp.broadcast_to(gx < lax.axis_size("gx") - 1, (8, B)),
        (row >= 2) | (gy > 0),
        (row < 6) | (gy < lax.axis_size("gy") - 1),
        (depth == 1) | (gz > 0),
        (depth == 0) | (gz < lax.axis_size("gz") - 1),
    )
    own_norm = facts_ref[pl.ds(0, 8), :]
    fine = facts_ref[pl.ds(8, 8), :] < 0.5
    norms, splits = neighbours(0), neighbours(1)
    total = jnp.zeros((8, B), F32)
    denom = jnp.zeros((8, B), F32)
    links = []
    for d in range(6):
        other = jnp.where(present[d], norms[d], 1.0)
        strength = jnp.where(present[d], fnorm_ref[pl.ds(8 * d, 8), :] / jnp.sqrt(own_norm * other), 0.0)
        linked = present[d] & (splits[d] > 0.5)
        total = total + strength
        denom = denom + jnp.where(linked, strength, 0.0)
        links.append(linked)
    ratio = total / jnp.where(fine, denom, 1.0)
    for d in range(6):
        weight_ref[d] = jnp.where(links[d] & fine, -ratio, 0.0)


def interp_kernel(
    split_ref, diag_ref, fine_ref, solved_ref, fnorm_ref, facts_ref, ha, hb, hc, hd, hz,
    code_ref, xa_ref, xb_ref, ya_ref, yb_ref, z_ref, all_ref, weight_ref,
):
    gx, gy = lax.axis_index("gx"), lax.axis_index("gy")
    flags = split_ref[...][0, 0]
    fines = [fine_of(flags, c) for c in range(4)]
    weights_of(facts_ref, (ha, hb, hc, hd, hz), fnorm_ref, weight_ref)

    even_x = gx % 2 == 0
    for c in range(4):
        for d in range(6):
            weight = weight_ref[d, pl.ds(2 * c + fines[c], 1), :]
            all_ref[d, c] = (weight * solved_ref[d, c]).astype(BF16)
        low, high = all_ref[0, c], all_ref[1, c]
        xa_ref[c] = jnp.where(even_x, high, low)
        xb_ref[c] = jnp.where(even_x, low, high)
        z_ref[c] = all_ref[4 + fines[c], c]
    row = lax.broadcasted_iota(jnp.int32, (8, B), 0)
    lane = lax.broadcasted_iota(jnp.int32, (8, B), 1)
    bit = jnp.where((row % 2 == 0) & (lane == 0), 1, 0) * lax.shift_left(1, row // 2)
    code = jnp.zeros((8, B), F32)
    splits = [facts_in(ha)[1], facts_in(hb)[1], hc[pl.ds(8, 8), :], hd[pl.ds(8, 8), :]]
    for place, theirs in enumerate(splits):
        code = code + theirs * (bit * (1 << (4 * place))).astype(F32)
    code = jnp.sum(jnp.sum(code, axis=0, keepdims=True), axis=1, keepdims=True)
    code_ref[...] = jnp.broadcast_to(code, (8, B)).astype(jnp.int32)
    up = gy % 2 == 0
    low, high = all_ref[2, 0], all_ref[3, 3]
    ya_ref[0, 0], yb_ref[0, 0] = jnp.where(up, high, low), jnp.where(up, low, high)
    low = contribs(diag_ref[fines[0]], [fine_ref[2, 0]], [low])[0]
    high = contribs(diag_ref[6 + fines[3]], [fine_ref[3, 3]], [high])[0]
    ya_ref[1, 0], yb_ref[1, 0] = jnp.where(up, high, low), jnp.where(up, low, high)


def contribs(a, faces, interps):
    found = []
    for s in range(0, len(faces), 2):
        pair = interps[s:s + 2]
        face = jnp.concatenate(faces[s:s + 2], axis=1)
        hi, lo = halves(mm(a, jnp.concatenate(pair, axis=1)) + face.astype(F32))
        for t, interp in enumerate(pair):
            lanes = slice(B * t, B * t + B)
            turned = jnp.transpose(interp)
            both = jnp.concatenate([turned, turned], axis=1)
            mixed = jnp.concatenate([hi[:, lanes], lo[:, lanes]], axis=0)
            found.append(mm(both, mixed).astype(BF16))
    return found


def near_kernel(
    split_ref, diag_ref, face_ref, fine_ref, all_ref, sum_ref, interp_ref, zero_ref, sems
):
    flags = split_ref[...][0, 0]
    fines = [fine_of(flags, c) for c in range(4)]
    zero_ref[...] = jnp.zeros((6, B, B), BF16)
    copies = []
    for c in range(4):
        e = 2 * c + fines[c]
        for block, to in ((all_ref.at[:, c], e), (zero_ref, 4 * c + 1 - e)):
            copies.append(pltpu.make_async_copy(block, interp_ref.at[:, to], sems.at[len(copies)]))
    for copy in copies[::2] + copies[1::2]:
        copy.start()
    parts = [[] for _ in range(4)]
    for c in range(4):
        z = fines[c]
        here = [(c, 1 - z, 4 + z, 5 - z, all_ref[5 - z, c])]
        if c > 0:
            here.append((c - 1, z, 3, 2, all_ref[2, c]))
        if c < 3:
            here.append((c + 1, z, 2, 3, all_ref[3, c]))
        found = contribs(
            diag_ref[2 * c + z], [fine_ref[d, c] for _, _, _, d, _ in here], [p for *_, p in here]
        )
        for (to, depth, back, _, interp), contrib in zip(here, found):
            product = mm(face_ref[back, 2 * to + depth], interp)
            parts[to].append((depth, contrib.astype(F32) + product))
    for c in range(4):
        for k in range(2):
            total = diag_ref[2 * c + k].astype(F32)
            for z, part in parts[c]:
                total = total + jnp.where(z == k, part, 0.0)
            sum_ref[2 * c + k] = total
    for copy in copies:
        copy.wait()


def bit_at(code, place):
    return lax.shift_right_logical(code, place) & 1


def computed(z, d, theirs, face, interp):
    return z, d, interp, contribs(theirs, [face], [interp])[0]


def from_four(z, d, sent, interp, c):
    theirs, face = sent[pl.ds(B * c, B), :], sent[pl.ds(B * (4 + c), B), :]
    return computed(z, d, theirs, face, interp[c])


def added(c, arrived, sum_ref, face_ref):
    totals = [sum_ref[2 * c], sum_ref[2 * c + 1]]
    for z, d, interp, contrib in arrived:
        part = contrib.astype(F32) + mm(face_ref[d, 2 * c + z], interp)
        totals = [total + jnp.where(z == k, part, 0.0) for k, total in enumerate(totals)]
    return totals


def middle_kernel(code_ref, sum_ref, face_ref, ha, hz, xa_ref, z_ref, total_ref):
    gx, gz = lax.axis_index("gx"), lax.axis_index("gz")
    code = code_ref[...][0, 0]
    for c in range(4):
        arrived = [
            from_four(1 - gz, 5 - gz, hz, z_ref, c),
            from_four(bit_at(code, c), 1 - gx % 2, ha, xa_ref, c),
        ]
        totals = added(c, arrived, sum_ref, face_ref)
        total_ref[2 * c], total_ref[2 * c + 1] = totals


def coarse_kernel(
    split_ref, code_ref, sum_ref, face_ref, hb, xb_ref, ya_ref, yb_ref,
    coarse_ref, total_ref, sems,
):
    gx, gy = lax.axis_index("gx"), lax.axis_index("gy")
    code = code_ref[...][0, 0]
    up = gy % 2 == 0
    flags = split_ref[...][0, 0]
    copies = []
    for c in (1, 2, 0, 3):
        arrived = [from_four(bit_at(code, 4 + c), gx % 2, hb, xb_ref, c)]
        if c in (0, 3):
            first = up if c == 3 else jnp.logical_not(up)
            edge = 0 if c == 3 else 3
            z = jnp.where(first, bit_at(code, 8 + edge), bit_at(code, 12 + edge))
            pair = [jnp.where(first, ya_ref[k, 0], yb_ref[k, 0]) for k in range(2)]
            arrived.append((z, 3 if c == 3 else 2, *pair))
        totals = added(c, arrived, sum_ref, face_ref)
        for k in range(2):
            e = 2 * c + k
            keep = split_at(flags, c, k) == 1
            total_ref[e] = jnp.where(keep, totals[k], 0.0)
            copies.append(pltpu.make_async_copy(total_ref.at[e], coarse_ref.at[e], sems.at[e]))
            copies[-1].start()
    for copy in copies:
        copy.wait()


def matching(size, start):
    pairs = [(i, i + 1) for i in range(start, size - 1, 2)]
    return pairs + [(b, a) for a, b in pairs]


def swap(x, axis, start):
    return lax.ppermute(x, axis, matching(lax.axis_size(axis), start))


def call(body, out_shape, in_specs, out_specs, scratch, flops):
    return pl.pallas_call(
        body,
        out_shape=out_shape,
        in_specs=in_specs,
        out_specs=out_specs,
        scratch_shapes=scratch,
        compiler_params=pltpu.CompilerParams(vmem_limit_bytes=LIMIT),
        cost_estimate=pl.CostEstimate(flops=flops, bytes_accessed=2 << 20, transcendentals=0),
    )


def on_device(diag_blocks, face_blocks, split):
    diag = diag_blocks.reshape(8, B, B)
    face = face_blocks.reshape(6, 8, B, B)
    split = jnp.transpose(split, (0, 2, 1))
    sds = jax.ShapeDtypeStruct
    dma = pltpu.SemaphoreType.DMA
    in_hbm = lambda x: pltpu.with_memory_space_constraint(x, pltpu.HBM)
    blocks = lambda *lead: sds(lead + (B, B), BF16)
    packed = sds((8 * B + 32, B), BF16)
    facts, flags, diag, pa, pb, pz = call(
        facts_kernel,
        (
            sds((16, B), F32), sds((8, B), jnp.int32), blocks(8),
            packed, packed, packed,
        ),
        [HBM] * 3, (VMEM,) * 6,
        [
            pltpu.VMEM((8, B), F32), pltpu.SMEM((1, 2, 4), jnp.int32),
            pltpu.VMEM((2, 8, B, B), BF16), dma((7,)),
        ],
        1 << 20,
    )(in_hbm(split), in_hbm(diag), in_hbm(face))
    ha, hb = swap(pa, "gx", 0), swap(pb, "gx", 1)
    hc, hd = swap(facts, "gy", 0), swap(facts, "gy", 1)
    hz = swap(pz, "gz", 0)
    solved, fnorm, fine = call(
        inverse_kernel, (sds((6, 4, B, B), F32), sds((48, B), F32), blocks(6, 4)),
        [VMEM, VMEM, HBM], (VMEM, VMEM, VMEM),
        [
            pltpu.VMEM((3, 4, B, B), BF16), pltpu.VMEM((48, B), F32), pltpu.VMEM((2, B, B), F32),
            dma((4,)),
        ],
        1 << 30,
    )(flags, diag, in_hbm(face))
    code, xa, xb, ya, yb, z, both = call(
        interp_kernel,
        (
            sds((8, B), jnp.int32), blocks(4), blocks(4), blocks(2, 1), blocks(2, 1), blocks(4),
            blocks(6, 4),
        ),
        [VMEM] * 11, (VMEM,) * 7, [pltpu.VMEM((6, 8, B), F32)], 1 << 30,
    )(flags, diag, fine, solved, fnorm, facts, ha, hb, hc, hd, hz)
    xa, xb = swap(xa, "gx", 0), swap(xb, "gx", 1)
    ya, yb = swap(ya, "gy", 0), swap(yb, "gy", 1)
    z = swap(z, "gz", 0)
    total, interp = call(
        near_kernel, (sds((8, B, B), F32), blocks(6, 8)), [VMEM] + [VMEM] * 4, (VMEM, HBM),
        [pltpu.VMEM((6, B, B), BF16), dma((8,))], 1 << 30,
    )(flags, diag, face, fine, both)
    total = call(
        middle_kernel, sds((8, B, B), F32), [VMEM] * 7, VMEM, [], 1 << 30,
    )(code, total, face, ha, hz, xa, z)
    coarse = call(
        coarse_kernel, sds((8, B, B), F32), [VMEM] * 8, HBM,
        [pltpu.VMEM((8, B, B), F32), dma((8,))], 1 << 30,
    )(flags, code, total, face, hb, xb, ya, yb)
    return interp.reshape(face_blocks.shape), coarse.reshape(diag_blocks.shape)


def solution(mesh):
    in_specs = (
        P("gx", "gy", "gz", None, None),
        P(None, "gx", "gy", "gz", None, None),
        P("gx", "gy", "gz"),
    )
    out_specs = (P(None, "gx", "gy", "gz", None, None), P("gx", "gy", "gz", None, None))
    return jax.shard_map(
        on_device, mesh=mesh, in_specs=in_specs, out_specs=out_specs, check_vma=False
    )
```

```python
import jax
import jax.numpy as jnp
from jax import lax
from jax.experimental import pallas as pl
from jax.experimental.pallas import tpu as pltpu
from jax.sharding import PartitionSpec as P


B = 128
F32 = jnp.float32
BF16 = jnp.bfloat16
VMEM = pl.BlockSpec(memory_space=pltpu.VMEM)
HBM = pl.BlockSpec(memory_space=pltpu.HBM)
LIMIT = 24 * 1024 * 1024


def mm(a, b):
    return jnp.dot(a, b, preferred_element_type=F32)


def mm32(a, b):
    return jnp.dot(a, b, preferred_element_type=F32, precision=lax.Precision.HIGHEST)


def halves(x):
    hi = x.astype(BF16)
    return hi, (x - hi.astype(F32)).astype(BF16)


def thirds(x):
    hi = x.astype(BF16)
    rest = x - hi.astype(F32)
    mid = rest.astype(BF16)
    return hi, mid, (rest - mid.astype(F32)).astype(BF16)


def wide(x):
    return jnp.concatenate([x, x], axis=0)


def split_at(flags, c, z):
    return lax.shift_right_logical(flags, 2 * c + z) & 1


def fine_of(flags, c):
    return split_at(flags, c, 0)


def square_sums(x):
    x = x.astype(F32)
    return jnp.sum(x * x, axis=0, keepdims=True)


def norms_of(rows):
    return jnp.broadcast_to(jnp.sqrt(jnp.sum(rows, axis=1, keepdims=True)), rows.shape)


def facts_kernel(
    split_ref, diag_ref, face_ref,
    facts_ref, flags_ref, kept_ref, xa_ref, xb_ref, z_ref, rows, held, faces, sems,
):
    gx, gz = lax.axis_index("gx"), lax.axis_index("gz")
    copies = [
        pltpu.make_async_copy(split_ref, held, sems.at[0]),
        pltpu.make_async_copy(diag_ref, kept_ref, sems.at[1]),
        pltpu.make_async_copy(face_ref.at[pl.ds(0, 2)], faces, sems.at[2]),
    ]
    for c in range(4):
        block, into = face_ref.at[5 - gz, 2 * c + 1 - gz], z_ref.at[pl.ds(B * (4 + c), B), :]
        copies.append(pltpu.make_async_copy(block, into, sems.at[3 + c]))
    for copy in copies:
        copy.start()
    copies[0].wait()
    row = lax.broadcasted_iota(jnp.int32, (8, B), 0)
    splits = [held[0, e % 2, e // 2] for e in range(8)]
    flags = jnp.zeros((8, B), F32)
    code = 0
    for e, split in enumerate(splits):
        flags = jnp.where(row == e, split.astype(F32), flags)
        code = code + split * (1 << e)
    flags_ref[...] = jnp.full((8, B), code, jnp.int32)
    facts_ref[pl.ds(8, 8), :] = flags
    copies[1].wait()
    for e in range(8):
        rows[pl.ds(e, 1), :] = square_sums(kept_ref[e])
    norms = norms_of(rows[...])
    facts_ref[pl.ds(0, 8), :] = norms
    parts = [part.astype(F32) for part in thirds(norms)] + [flags]
    for ref in (xa_ref, xb_ref, z_ref):
        for k in range(2):
            both = jnp.concatenate(parts[2 * k:2 * k + 2], axis=0)
            ref[pl.ds(8 * B + 16 * k, 16), :] = both.astype(BF16)
    for copy in copies[2:]:
        copy.wait()
    for c in range(4):
        e = 2 * c + splits[2 * c]
        block = kept_ref[e]
        z_ref[pl.ds(B * c, B), :] = kept_ref[2 * c + 1 - gz]
        for ref, d in ((xa_ref, 1 - gx % 2), (xb_ref, gx % 2)):
            ref[pl.ds(B * c, B), :] = block
            ref[pl.ds(B * (4 + c), B), :] = faces[d, e]


def facts_in(ref):
    high, low = ref[pl.ds(8 * B, 16), :].astype(F32), ref[pl.ds(8 * B + 16, 16), :].astype(F32)
    return high[:8] + high[8:] + low[:8], low[8:]


def scaling(a, eye):
    picked = jnp.where(eye, a, 0.0)
    down = lax.rsqrt(jnp.sum(picked, axis=1, keepdims=True))
    along = lax.rsqrt(jnp.sum(picked, axis=0, keepdims=True))
    a = a * down * along
    bound = jnp.max(jnp.sum(jnp.abs(a), axis=0, keepdims=True), axis=1, keepdims=True)
    return a, down, along, 1.9 / bound


def inverse_kernel(
    split_ref, diag_ref, face_ref, solved_ref, fnorm_ref, fine_ref, inv_ref, rows, work, sems
):
    cols = range(4)
    flags = split_ref[...][0, 0]
    copies = []
    for c in cols:
        e = 2 * c + fine_of(flags, c)
        copies.append(pltpu.make_async_copy(face_ref.at[:, e], fine_ref.at[:, c], sems.at[c]))
        copies[-1].start()
    eye = (
        lax.broadcasted_iota(jnp.int32, (B, B), 0) == lax.broadcasted_iota(jnp.int32, (B, B), 1)
    )
    one = jnp.where(eye, 1.0, 0.0).astype(F32)
    mats = [diag_ref[2 * c + fine_of(flags, c)] for c in cols]
    parts = [scaling(m.astype(F32), eye) for m in mats]
    powers = [one - start * a for a, _, _, start in parts]
    sums = [one + p for p in powers]
    powers = [p.astype(BF16) for p in powers]
    for _ in range(4):
        powers = [mm(p, p).astype(BF16) for p in powers]
        sums = [s + mm(s.astype(BF16), p) for s, p in zip(sums, powers)]
    guess = [
        (s * (start * down) * along).astype(BF16) for s, (_, down, along, start) in zip(sums, parts)
    ]
    left = [one - mm(mats[c], guess[c]) for c in cols]
    small = [r.astype(BF16) for r in left]
    left = [r + mm(b, b) for r, b in zip(left, small)]
    better = []
    for c in cols:
        hi, lo = halves(left[c])
        better.append(guess[c].astype(F32) + (mm(guess[c], hi) + mm(guess[c], lo)))
    pairs = [halves(x) for x in better]
    left = [one - (mm(mats[c], pairs[c][0]) + mm(mats[c], pairs[c][1])) for c in cols]
    worst = jnp.zeros((1, B), F32)
    for c in cols:
        hi, lo = pairs[c]
        rhi, rlo = halves(left[c])
        fixed = (hi.astype(F32) + lo.astype(F32)) + (mm(hi, rhi) + (mm(hi, rlo) + mm(lo, rhi)))
        inv_ref[0, c], inv_ref[1, c], inv_ref[2, c] = thirds(fixed)
        worst = worst + jnp.sum(jnp.abs(left[c]), axis=0, keepdims=True)
    for copy in copies:
        copy.wait()
    for d in range(6):
        for c in cols:
            sums = square_sums(fine_ref[d, c])
            rows[pl.ds(8 * d + 2 * c, 1), :] = sums
            rows[pl.ds(8 * d + 2 * c + 1, 1), :] = sums
    fnorm_ref[...] = norms_of(rows[...])

    def solve():
        for c in cols:
            inv = jnp.concatenate([inv_ref[0, c], inv_ref[1, c]], axis=1)
            last = inv_ref[2, c]
            for d in (0, 2, 4):
                face = jnp.concatenate([fine_ref[d, c], fine_ref[d + 1, c]], axis=1)
                both = mm(inv, wide(face)) + mm(last, face)
                solved_ref[d, c] = both[:, :B]
                solved_ref[d + 1, c] = both[:, B:]

    solve()
    reached = jnp.max(worst) <= 1e-3

    @pl.when(jnp.logical_not(reached))
    def _():
        for c in cols:
            a, down, along, start = scaling(mats[c].astype(F32), eye)
            work[0] = a
            work[1] = one * start

            @pl.loop(0, 48)
            def _(_):
                x = work[1]
                work[1] = x + mm32(x, one - mm32(work[0], x))

            inv_ref[0, c], inv_ref[1, c], inv_ref[2, c] = thirds(work[1] * down * along)
        solve()


def shifted(own, beyond, step, edge):
    return jnp.where(edge, pltpu.roll(beyond, step, 0), pltpu.roll(own, step, 0))


def weights_of(facts_ref, halo_refs, fnorm_ref, weight_ref):
    gx, gy, gz = lax.axis_index("gx"), lax.axis_index("gy"), lax.axis_index("gz")
    ha, hb, hc, hd, hz = halo_refs
    row = lax.broadcasted_iota(jnp.int32, (8, B), 0)
    depth = row % 2
    even_x, even_y = gx % 2 == 0, gy % 2 == 0

    xa, xb, beyond = facts_in(ha), facts_in(hb), facts_in(hz)
    ya, yb = (hc[pl.ds(0, 8), :], hc[pl.ds(8, 8), :]), (hd[pl.ds(0, 8), :], hd[pl.ds(8, 8), :])

    def neighbours(part):
        own = facts_ref[pl.ds(8 * part, 8), :]
        z = beyond[part]
        return (
            jnp.where(even_x, xb[part], xa[part]),
            jnp.where(even_x, xa[part], xb[part]),
            shifted(own, jnp.where(even_y, yb[part], ya[part]), 2, row < 2),
            shifted(own, jnp.where(even_y, ya[part], yb[part]), 6, row >= 6),
            jnp.where(depth == 0, pltpu.roll(z, 7, 0), pltpu.roll(own, 1, 0)),
            jnp.where(depth == 1, pltpu.roll(z, 1, 0), pltpu.roll(own, 7, 0)),
        )

    present = (
        jnp.broadcast_to(gx > 0, (8, B)),
        jnp.broadcast_to(gx < lax.axis_size("gx") - 1, (8, B)),
        (row >= 2) | (gy > 0),
        (row < 6) | (gy < lax.axis_size("gy") - 1),
        (depth == 1) | (gz > 0),
        (depth == 0) | (gz < lax.axis_size("gz") - 1),
    )
    own_norm = facts_ref[pl.ds(0, 8), :]
    fine = facts_ref[pl.ds(8, 8), :] < 0.5
    norms, splits = neighbours(0), neighbours(1)
    total = jnp.zeros((8, B), F32)
    denom = jnp.zeros((8, B), F32)
    links = []
    for d in range(6):
        other = jnp.where(present[d], norms[d], 1.0)
        strength = jnp.where(present[d], fnorm_ref[pl.ds(8 * d, 8), :] / jnp.sqrt(own_norm * other), 0.0)
        linked = present[d] & (splits[d] > 0.5)
        total = total + strength
        denom = denom + jnp.where(linked, strength, 0.0)
        links.append(linked)
    ratio = total / jnp.where(fine, denom, 1.0)
    for d in range(6):
        weight_ref[d] = jnp.where(links[d] & fine, -ratio, 0.0)


def interp_kernel(
    split_ref, diag_ref, fine_ref, solved_ref, fnorm_ref, facts_ref, ha, hb, hc, hd, hz,
    code_ref, xa_ref, xb_ref, ya_ref, yb_ref, z_ref, all_ref, weight_ref,
):
    gx, gy = lax.axis_index("gx"), lax.axis_index("gy")
    flags = split_ref[...][0, 0]
    fines = [fine_of(flags, c) for c in range(4)]
    weights_of(facts_ref, (ha, hb, hc, hd, hz), fnorm_ref, weight_ref)

    even_x = gx % 2 == 0
    for c in range(4):
        for d in range(6):
            weight = weight_ref[d, pl.ds(2 * c + fines[c], 1), :]
            all_ref[d, c] = (weight * solved_ref[d, c]).astype(BF16)
        low, high = all_ref[0, c], all_ref[1, c]
        xa_ref[c] = jnp.where(even_x, high, low)
        xb_ref[c] = jnp.where(even_x, low, high)
        z_ref[c] = all_ref[4 + fines[c], c]
    row = lax.broadcasted_iota(jnp.int32, (8, B), 0)
    lane = lax.broadcasted_iota(jnp.int32, (8, B), 1)
    bit = jnp.where((row % 2 == 0) & (lane == 0), 1, 0) * lax.shift_left(1, row // 2)
    code = jnp.zeros((8, B), F32)
    splits = [facts_in(ha)[1], facts_in(hb)[1], hc[pl.ds(8, 8), :], hd[pl.ds(8, 8), :]]
    for place, theirs in enumerate(splits):
        code = code + theirs * (bit * (1 << (4 * place))).astype(F32)
    code = jnp.sum(jnp.sum(code, axis=0, keepdims=True), axis=1, keepdims=True)
    code_ref[...] = jnp.broadcast_to(code, (8, B)).astype(jnp.int32)
    up = gy % 2 == 0
    low, high = all_ref[2, 0], all_ref[3, 3]
    ya_ref[0, 0], yb_ref[0, 0] = jnp.where(up, high, low), jnp.where(up, low, high)
    low = contribs(diag_ref[fines[0]], [fine_ref[2, 0]], [low])[0]
    high = contribs(diag_ref[6 + fines[3]], [fine_ref[3, 3]], [high])[0]
    ya_ref[1, 0], yb_ref[1, 0] = jnp.where(up, high, low), jnp.where(up, low, high)


def contribs(a, faces, interps):
    found = []
    for s in range(0, len(faces), 2):
        pair = interps[s:s + 2]
        face = jnp.concatenate(faces[s:s + 2], axis=1)
        hi, lo = halves(mm(a, jnp.concatenate(pair, axis=1)) + face.astype(F32))
        for t, interp in enumerate(pair):
            lanes = slice(B * t, B * t + B)
            turned = jnp.transpose(interp)
            both = jnp.concatenate([turned, turned], axis=1)
            mixed = jnp.concatenate([hi[:, lanes], lo[:, lanes]], axis=0)
            found.append(mm(both, mixed).astype(BF16))
    return found


def near_kernel(
    split_ref, diag_ref, face_ref, fine_ref, all_ref, sum_ref, interp_ref, zero_ref, sems
):
    flags = split_ref[...][0, 0]
    fines = [fine_of(flags, c) for c in range(4)]
    zero_ref[...] = jnp.zeros((6, B, B), BF16)
    copies = []
    for c in range(4):
        e = 2 * c + fines[c]
        for block, to in ((all_ref.at[:, c], e), (zero_ref, 4 * c + 1 - e)):
            copies.append(pltpu.make_async_copy(block, interp_ref.at[:, to], sems.at[len(copies)]))
    for copy in copies[::2] + copies[1::2]:
        copy.start()
    parts = [[] for _ in range(4)]
    for c in range(4):
        z = fines[c]
        here = [(c, 1 - z, 4 + z, 5 - z, all_ref[5 - z, c])]
        if c > 0:
            here.append((c - 1, z, 3, 2, all_ref[2, c]))
        if c < 3:
            here.append((c + 1, z, 2, 3, all_ref[3, c]))
        found = contribs(
            diag_ref[2 * c + z], [fine_ref[d, c] for _, _, _, d, _ in here], [p for *_, p in here]
        )
        for (to, depth, back, _, interp), contrib in zip(here, found):
            product = mm(face_ref[back, 2 * to + depth], interp)
            parts[to].append((depth, contrib.astype(F32) + product))
    for c in range(4):
        for k in range(2):
            total = diag_ref[2 * c + k].astype(F32)
            for z, part in parts[c]:
                total = total + jnp.where(z == k, part, 0.0)
            sum_ref[2 * c + k] = total
    for copy in copies:
        copy.wait()


def bit_at(code, place):
    return lax.shift_right_logical(code, place) & 1


def computed(z, d, theirs, face, interp):
    return z, d, interp, contribs(theirs, [face], [interp])[0]


def from_four(z, d, sent, interp, c):
    theirs, face = sent[pl.ds(B * c, B), :], sent[pl.ds(B * (4 + c), B), :]
    return computed(z, d, theirs, face, interp[c])


def added(c, arrived, sum_ref, face_ref):
    totals = [sum_ref[2 * c], sum_ref[2 * c + 1]]
    for z, d, interp, contrib in arrived:
        part = contrib.astype(F32) + mm(face_ref[d, 2 * c + z], interp)
        totals = [total + jnp.where(z == k, part, 0.0) for k, total in enumerate(totals)]
    return totals


def middle_kernel(code_ref, sum_ref, face_ref, ha, hz, xa_ref, z_ref, total_ref):
    gx, gz = lax.axis_index("gx"), lax.axis_index("gz")
    code = code_ref[...][0, 0]
    for c in range(4):
        arrived = [
            from_four(1 - gz, 5 - gz, hz, z_ref, c),
            from_four(bit_at(code, c), 1 - gx % 2, ha, xa_ref, c),
        ]
        totals = added(c, arrived, sum_ref, face_ref)
        total_ref[2 * c], total_ref[2 * c + 1] = totals


def late_kernel(code_ref, sum_ref, face_ref, hb, xb_ref, total_ref):
    gx = lax.axis_index("gx")
    code = code_ref[...][0, 0]
    for c in range(4):
        arrived = [from_four(bit_at(code, 4 + c), gx % 2, hb, xb_ref, c)]
        totals = added(c, arrived, sum_ref, face_ref)
        total_ref[2 * c], total_ref[2 * c + 1] = totals


def coarse_kernel(
    split_ref, code_ref, sum_ref, face_ref, ya_ref, yb_ref, coarse_ref, total_ref, sems
):
    gy = lax.axis_index("gy")
    code = code_ref[...][0, 0]
    up = gy % 2 == 0
    flags = split_ref[...][0, 0]
    copies = []
    for c in (1, 2, 0, 3):
        arrived = []
        if c in (0, 3):
            first = up if c == 3 else jnp.logical_not(up)
            edge = 0 if c == 3 else 3
            z = jnp.where(first, bit_at(code, 8 + edge), bit_at(code, 12 + edge))
            pair = [jnp.where(first, ya_ref[k, 0], yb_ref[k, 0]) for k in range(2)]
            arrived.append((z, 3 if c == 3 else 2, *pair))
        totals = added(c, arrived, sum_ref, face_ref)
        for k in range(2):
            keep = split_at(flags, c, k) == 1
            total_ref[2 * c + k] = jnp.where(keep, totals[k], 0.0)
        pair = pl.ds(2 * c, 2)
        copies.append(
            pltpu.make_async_copy(total_ref.at[pair], coarse_ref.at[pair], sems.at[c])
        )
        copies[-1].start()
    for copy in copies:
        copy.wait()


def matching(size, start):
    pairs = [(i, i + 1) for i in range(start, size - 1, 2)]
    return pairs + [(b, a) for a, b in pairs]


def swap(x, axis, start):
    return lax.ppermute(x, axis, matching(lax.axis_size(axis), start))


def call(body, out_shape, in_specs, out_specs, scratch, flops):
    return pl.pallas_call(
        body,
        out_shape=out_shape,
        in_specs=in_specs,
        out_specs=out_specs,
        scratch_shapes=scratch,
        compiler_params=pltpu.CompilerParams(vmem_limit_bytes=LIMIT),
        cost_estimate=pl.CostEstimate(flops=flops, bytes_accessed=2 << 20, transcendentals=0),
    )


def on_device(diag_blocks, face_blocks, split):
    diag = diag_blocks.reshape(8, B, B)
    face = face_blocks.reshape(6, 8, B, B)
    split = jnp.transpose(split, (0, 2, 1))
    sds = jax.ShapeDtypeStruct
    dma = pltpu.SemaphoreType.DMA
    in_hbm = lambda x: pltpu.with_memory_space_constraint(x, pltpu.HBM)
    blocks = lambda *lead: sds(lead + (B, B), BF16)
    packed = sds((8 * B + 32, B), BF16)
    facts, flags, diag, pa, pb, pz = call(
        facts_kernel,
        (
            sds((16, B), F32), sds((8, B), jnp.int32), blocks(8),
            packed, packed, packed,
        ),
        [HBM] * 3, (VMEM,) * 6,
        [
            pltpu.VMEM((8, B), F32), pltpu.SMEM((1, 2, 4), jnp.int32),
            pltpu.VMEM((2, 8, B, B), BF16), dma((7,)),
        ],
        1 << 20,
    )(in_hbm(split), in_hbm(diag), in_hbm(face))
    ha, hb = swap(pa, "gx", 0), swap(pb, "gx", 1)
    hc, hd = swap(facts, "gy", 0), swap(facts, "gy", 1)
    hz = swap(pz, "gz", 0)
    solved, fnorm, fine = call(
        inverse_kernel, (sds((6, 4, B, B), F32), sds((48, B), F32), blocks(6, 4)),
        [VMEM, VMEM, HBM], (VMEM, VMEM, VMEM),
        [
            pltpu.VMEM((3, 4, B, B), BF16), pltpu.VMEM((48, B), F32), pltpu.VMEM((2, B, B), F32),
            dma((4,)),
        ],
        1 << 30,
    )(flags, diag, in_hbm(face))
    code, xa, xb, ya, yb, z, both = call(
        interp_kernel,
        (
            sds((8, B), jnp.int32), blocks(4), blocks(4), blocks(2, 1), blocks(2, 1), blocks(4),
            blocks(6, 4),
        ),
        [VMEM] * 11, (VMEM,) * 7, [pltpu.VMEM((6, 8, B), F32)], 1 << 30,
    )(flags, diag, fine, solved, fnorm, facts, ha, hb, hc, hd, hz)
    xa, xb = swap(xa, "gx", 0), swap(xb, "gx", 1)
    ya, yb = swap(ya, "gy", 0), swap(yb, "gy", 1)
    z = swap(z, "gz", 0)
    total, interp = call(
        near_kernel, (sds((8, B, B), F32), blocks(6, 8)), [VMEM] + [VMEM] * 4, (VMEM, HBM),
        [pltpu.VMEM((6, B, B), BF16), dma((8,))], 1 << 30,
    )(flags, diag, face, fine, both)
    total = call(
        middle_kernel, sds((8, B, B), F32), [VMEM] * 7, VMEM, [], 1 << 30,
    )(code, total, face, ha, hz, xa, z)
    total = call(
        late_kernel, sds((8, B, B), F32), [VMEM] * 5, VMEM, [], 1 << 30,
    )(code, total, face, hb, xb)
    coarse = call(
        coarse_kernel, sds((8, B, B), F32), [VMEM] * 6, HBM,
        [pltpu.VMEM((8, B, B), F32), dma((4,))], 1 << 30,
    )(flags, code, total, face, ya, yb)
    return interp.reshape(face_blocks.shape), coarse.reshape(diag_blocks.shape)


def solution(mesh):
    in_specs = (
        P("gx", "gy", "gz", None, None),
        P(None, "gx", "gy", "gz", None, None),
        P("gx", "gy", "gz"),
    )
    out_specs = (P(None, "gx", "gy", "gz", None, None), P("gx", "gy", "gz", None, None))
    return jax.shard_map(
        on_device, mesh=mesh, in_specs=in_specs, out_specs=out_specs, check_vma=False
    )
```

```python
import jax
import jax.numpy as jnp
from jax import lax
from jax.experimental import pallas as pl
from jax.experimental.pallas import tpu as pltpu
from jax.sharding import PartitionSpec as P


B = 128
F32 = jnp.float32
BF16 = jnp.bfloat16
VMEM = pl.BlockSpec(memory_space=pltpu.VMEM)
HBM = pl.BlockSpec(memory_space=pltpu.HBM)
LIMIT = 24 * 1024 * 1024
HALF = 64
FACES = 272
FACTS = 784


def mm(a, b):
    return jnp.dot(a, b, preferred_element_type=F32)


def mm32(a, b):
    return jnp.dot(a, b, preferred_element_type=F32, precision=lax.Precision.HIGHEST)


def halves(x):
    hi = x.astype(BF16)
    return hi, (x - hi.astype(F32)).astype(BF16)


def thirds(x):
    hi = x.astype(BF16)
    rest = x - hi.astype(F32)
    mid = rest.astype(BF16)
    return hi, mid, (rest - mid.astype(F32)).astype(BF16)


def wide(x):
    return jnp.concatenate([x, x], axis=0)


def split_at(flags, c, z):
    return lax.shift_right_logical(flags, 2 * c + z) & 1


def fine_of(flags, c):
    return split_at(flags, c, 0)


def square_sums(x):
    x = x.astype(F32)
    return jnp.sum(x * x, axis=0, keepdims=True)


def norms_of(rows):
    return jnp.broadcast_to(jnp.sqrt(jnp.sum(rows, axis=1, keepdims=True)), rows.shape)


def facts_kernel(
    split_ref, diag_ref, face_ref,
    facts_ref, flags_ref, kept_ref, xa_ref, xb_ref, z_ref, rows, held, faces, sems,
):
    gx, gz = lax.axis_index("gx"), lax.axis_index("gz")
    copies = [
        pltpu.make_async_copy(split_ref, held, sems.at[0]),
        pltpu.make_async_copy(diag_ref, kept_ref, sems.at[1]),
        pltpu.make_async_copy(face_ref.at[pl.ds(0, 2)], faces, sems.at[2]),
    ]
    for c in range(4):
        block, into = face_ref.at[5 - gz, 2 * c + 1 - gz], z_ref.at[pl.ds(B * (4 + c), B), :]
        copies.append(pltpu.make_async_copy(block, into, sems.at[3 + c]))
    for copy in copies:
        copy.start()
    copies[0].wait()
    row = lax.broadcasted_iota(jnp.int32, (8, B), 0)
    splits = [held[0, e % 2, e // 2] for e in range(8)]
    flags = jnp.zeros((8, B), F32)
    code = 0
    for e, split in enumerate(splits):
        flags = jnp.where(row == e, split.astype(F32), flags)
        code = code + split * (1 << e)
    flags_ref[...] = jnp.full((8, B), code, jnp.int32)
    facts_ref[pl.ds(8, 8), :] = flags
    copies[1].wait()
    for e in range(8):
        rows[pl.ds(e, 1), :] = square_sums(kept_ref[e])
    norms = norms_of(rows[pl.ds(0, 8), :])
    facts_ref[pl.ds(0, 8), :] = norms
    parts = [part.astype(F32) for part in thirds(norms)] + [flags]
    for ref, start in ((xa_ref, FACTS), (xb_ref, FACTS), (z_ref, 8 * B)):
        for k in range(2):
            both = jnp.concatenate(parts[2 * k:2 * k + 2], axis=0)
            ref[pl.ds(start + 16 * k, 16), :] = both.astype(BF16)
    row = lax.broadcasted_iota(jnp.int32, (HALF, B), 0)
    lane = lax.broadcasted_iota(jnp.int32, (HALF, B), 1)
    rows[pl.ds(8, 8), :] = jnp.zeros((8, B), F32)
    for c in range(4):
        block = kept_ref[2 * c + splits[2 * c]].astype(F32)
        top, bottom = block[:HALF], block[HALF:]
        folded = jnp.where((lane >= HALF) | (row >= lane), top, pltpu.roll(bottom, HALF, 1))
        folded = folded.astype(BF16)
        rows[pl.ds(8 + c, 1), :] = jnp.sum(
            jnp.where(row == lane - HALF, bottom, 0.0), axis=0, keepdims=True
        )
        for ref in (xa_ref, xb_ref):
            ref[pl.ds(HALF * c, HALF), :] = folded
    tail = jnp.concatenate([rows[pl.ds(8, 8), :], jnp.zeros((8, B), F32)], axis=0).astype(BF16)
    for ref in (xa_ref, xb_ref):
        ref[pl.ds(4 * HALF, 16), :] = tail
    for copy in copies[2:]:
        copy.wait()
    for c in range(4):
        e = 2 * c + splits[2 * c]
        z_ref[pl.ds(B * c, B), :] = kept_ref[2 * c + 1 - gz]
        for ref, d in ((xa_ref, 1 - gx % 2), (xb_ref, gx % 2)):
            ref[pl.ds(FACES + B * c, B), :] = faces[d, e]


def unfolded(ref, c):
    row = lax.broadcasted_iota(jnp.int32, (HALF, B), 0)
    lane = lax.broadcasted_iota(jnp.int32, (HALF, B), 1)
    folded = ref[pl.ds(HALF * c, HALF), :].astype(F32)
    turned = jnp.transpose(jnp.concatenate([folded, folded], axis=0))
    corner = ref[pl.ds(4 * HALF, 16), :].astype(F32)[c:c + 1]
    top = jnp.where((lane >= HALF) | (row >= lane), folded, turned[:HALF])
    low = jnp.where(row < lane - HALF, pltpu.roll(folded, HALF, 1), turned[:HALF])
    low = jnp.where(row == lane - HALF, corner, low)
    bottom = jnp.where(lane < HALF, turned[HALF:], low)
    return jnp.concatenate([top, bottom], axis=0).astype(BF16)


def facts_in(ref, start):
    high, low = ref[pl.ds(start, 16), :].astype(F32), ref[pl.ds(start + 16, 16), :].astype(F32)
    return high[:8] + high[8:] + low[:8], low[8:]


def scaling(a, eye):
    picked = jnp.where(eye, a, 0.0)
    down = lax.rsqrt(jnp.sum(picked, axis=1, keepdims=True))
    along = lax.rsqrt(jnp.sum(picked, axis=0, keepdims=True))
    a = a * down * along
    bound = jnp.max(jnp.sum(jnp.abs(a), axis=0, keepdims=True), axis=1, keepdims=True)
    return a, down, along, 1.9 / bound


def inverse_kernel(
    split_ref, diag_ref, face_ref, solved_ref, fnorm_ref, fine_ref, inv_ref, rows, work, sems
):
    cols = range(4)
    flags = split_ref[...][0, 0]
    copies = []
    for c in cols:
        e = 2 * c + fine_of(flags, c)
        copies.append(pltpu.make_async_copy(face_ref.at[:, e], fine_ref.at[:, c], sems.at[c]))
        copies[-1].start()
    eye = (
        lax.broadcasted_iota(jnp.int32, (B, B), 0) == lax.broadcasted_iota(jnp.int32, (B, B), 1)
    )
    one = jnp.where(eye, 1.0, 0.0).astype(F32)
    mats = [diag_ref[2 * c + fine_of(flags, c)] for c in cols]
    parts = [scaling(m.astype(F32), eye) for m in mats]
    powers = [one - start * a for a, _, _, start in parts]
    sums = [one + p for p in powers]
    powers = [p.astype(BF16) for p in powers]
    for _ in range(3):
        powers = [mm(p, p).astype(BF16) for p in powers]
        sums = [s + mm(s.astype(BF16), p) for s, p in zip(sums, powers)]
    guess = [
        (s * (start * down) * along).astype(BF16) for s, (_, down, along, start) in zip(sums, parts)
    ]
    left = [one - mm(mats[c], guess[c]) for c in cols]
    small = [r.astype(BF16) for r in left]
    left = [r + mm(b, b) for r, b in zip(left, small)]
    better = []
    for c in cols:
        hi, lo = halves(left[c])
        better.append(guess[c].astype(F32) + (mm(guess[c], hi) + mm(guess[c], lo)))
    pairs = [halves(x) for x in better]
    left = [one - (mm(mats[c], pairs[c][0]) + mm(mats[c], pairs[c][1])) for c in cols]
    worst = jnp.zeros((1, B), F32)
    for c in cols:
        hi, lo = pairs[c]
        rhi, rlo = halves(left[c])
        fixed = (hi.astype(F32) + lo.astype(F32)) + (mm(hi, rhi) + (mm(hi, rlo) + mm(lo, rhi)))
        inv_ref[0, c], inv_ref[1, c], inv_ref[2, c] = thirds(fixed)
        worst = worst + jnp.sum(jnp.abs(left[c]), axis=0, keepdims=True)
    for copy in copies:
        copy.wait()
    for d in range(6):
        for c in cols:
            sums = square_sums(fine_ref[d, c])
            rows[pl.ds(8 * d + 2 * c, 1), :] = sums
            rows[pl.ds(8 * d + 2 * c + 1, 1), :] = sums
    fnorm_ref[...] = norms_of(rows[...])

    def solve():
        for c in cols:
            inv = jnp.concatenate([inv_ref[0, c], inv_ref[1, c]], axis=1)
            last = inv_ref[2, c]
            for d in (0, 2, 4):
                face = jnp.concatenate([fine_ref[d, c], fine_ref[d + 1, c]], axis=1)
                both = mm(inv, wide(face)) + mm(last, face)
                solved_ref[d, c] = both[:, :B]
                solved_ref[d + 1, c] = both[:, B:]

    solve()
    reached = jnp.max(worst) <= 1e-3

    @pl.when(jnp.logical_not(reached))
    def _():
        for c in cols:
            a, down, along, start = scaling(mats[c].astype(F32), eye)
            work[0] = a
            work[1] = one * start

            @pl.loop(0, 48)
            def _(_):
                x = work[1]
                work[1] = x + mm32(x, one - mm32(work[0], x))

            inv_ref[0, c], inv_ref[1, c], inv_ref[2, c] = thirds(work[1] * down * along)
        solve()


def shifted(own, beyond, step, edge):
    return jnp.where(edge, pltpu.roll(beyond, step, 0), pltpu.roll(own, step, 0))


def weights_of(facts_ref, halo_refs, fnorm_ref, weight_ref):
    gx, gy, gz = lax.axis_index("gx"), lax.axis_index("gy"), lax.axis_index("gz")
    ha, hb, hc, hd, hz = halo_refs
    row = lax.broadcasted_iota(jnp.int32, (8, B), 0)
    depth = row % 2
    even_x, even_y = gx % 2 == 0, gy % 2 == 0

    xa, xb, beyond = facts_in(ha, FACTS), facts_in(hb, FACTS), facts_in(hz, 8 * B)
    ya, yb = (hc[pl.ds(0, 8), :], hc[pl.ds(8, 8), :]), (hd[pl.ds(0, 8), :], hd[pl.ds(8, 8), :])

    def neighbours(part):
        own = facts_ref[pl.ds(8 * part, 8), :]
        z = beyond[part]
        return (
            jnp.where(even_x, xb[part], xa[part]),
            jnp.where(even_x, xa[part], xb[part]),
            shifted(own, jnp.where(even_y, yb[part], ya[part]), 2, row < 2),
            shifted(own, jnp.where(even_y, ya[part], yb[part]), 6, row >= 6),
            jnp.where(depth == 0, pltpu.roll(z, 7, 0), pltpu.roll(own, 1, 0)),
            jnp.where(depth == 1, pltpu.roll(z, 1, 0), pltpu.roll(own, 7, 0)),
        )

    present = (
        jnp.broadcast_to(gx > 0, (8, B)),
        jnp.broadcast_to(gx < lax.axis_size("gx") - 1, (8, B)),
        (row >= 2) | (gy > 0),
        (row < 6) | (gy < lax.axis_size("gy") - 1),
        (depth == 1) | (gz > 0),
        (depth == 0) | (gz < lax.axis_size("gz") - 1),
    )
    own_norm = facts_ref[pl.ds(0, 8), :]
    fine = facts_ref[pl.ds(8, 8), :] < 0.5
    norms, splits = neighbours(0), neighbours(1)
    total = jnp.zeros((8, B), F32)
    denom = jnp.zeros((8, B), F32)
    links = []
    for d in range(6):
        other = jnp.where(present[d], norms[d], 1.0)
        strength = jnp.where(present[d], fnorm_ref[pl.ds(8 * d, 8), :] / jnp.sqrt(own_norm * other), 0.0)
        linked = present[d] & (splits[d] > 0.5)
        total = total + strength
        denom = denom + jnp.where(linked, strength, 0.0)
        links.append(linked)
    ratio = total / jnp.where(fine, denom, 1.0)
    for d in range(6):
        weight_ref[d] = jnp.where(links[d] & fine, -ratio, 0.0)


def interp_kernel(
    split_ref, diag_ref, fine_ref, solved_ref, fnorm_ref, facts_ref, ha, hb, hc, hd, hz,
    code_ref, xa_ref, xb_ref, ya_ref, yb_ref, z_ref, all_ref, weight_ref,
):
    gx, gy = lax.axis_index("gx"), lax.axis_index("gy")
    flags = split_ref[...][0, 0]
    fines = [fine_of(flags, c) for c in range(4)]
    weights_of(facts_ref, (ha, hb, hc, hd, hz), fnorm_ref, weight_ref)

    even_x = gx % 2 == 0
    for c in range(4):
        for d in range(6):
            weight = weight_ref[d, pl.ds(2 * c + fines[c], 1), :]
            all_ref[d, c] = (weight * solved_ref[d, c]).astype(BF16)
        low, high = all_ref[0, c], all_ref[1, c]
        xa_ref[c] = jnp.where(even_x, high, low)
        xb_ref[c] = jnp.where(even_x, low, high)
        z_ref[c] = all_ref[4 + fines[c], c]
    row = lax.broadcasted_iota(jnp.int32, (8, B), 0)
    lane = lax.broadcasted_iota(jnp.int32, (8, B), 1)
    bit = jnp.where((row % 2 == 0) & (lane == 0), 1, 0) * lax.shift_left(1, row // 2)
    code = jnp.zeros((8, B), F32)
    splits = [facts_in(ha, FACTS)[1], facts_in(hb, FACTS)[1], hc[pl.ds(8, 8), :], hd[pl.ds(8, 8), :]]
    for place, theirs in enumerate(splits):
        code = code + theirs * (bit * (1 << (4 * place))).astype(F32)
    code = jnp.sum(jnp.sum(code, axis=0, keepdims=True), axis=1, keepdims=True)
    code_ref[...] = jnp.broadcast_to(code, (8, B)).astype(jnp.int32)
    up = gy % 2 == 0
    low, high = all_ref[2, 0], all_ref[3, 3]
    ya_ref[0, 0], yb_ref[0, 0] = jnp.where(up, high, low), jnp.where(up, low, high)
    low = contribs(diag_ref[fines[0]], [fine_ref[2, 0]], [low])[0]
    high = contribs(diag_ref[6 + fines[3]], [fine_ref[3, 3]], [high])[0]
    ya_ref[1, 0], yb_ref[1, 0] = jnp.where(up, high, low), jnp.where(up, low, high)


def contribs(a, faces, interps):
    found = []
    for s in range(0, len(faces), 2):
        pair = interps[s:s + 2]
        face = jnp.concatenate(faces[s:s + 2], axis=1)
        hi, lo = halves(mm(a, jnp.concatenate(pair, axis=1)) + face.astype(F32))
        for t, interp in enumerate(pair):
            lanes = slice(B * t, B * t + B)
            turned = jnp.transpose(interp)
            both = jnp.concatenate([turned, turned], axis=1)
            mixed = jnp.concatenate([hi[:, lanes], lo[:, lanes]], axis=0)
            found.append(mm(both, mixed).astype(BF16))
    return found


def near_kernel(
    split_ref, diag_ref, face_ref, fine_ref, all_ref, ha, hb, sum_ref, interp_ref, far_ref,
    zero_ref, sems,
):
    flags = split_ref[...][0, 0]
    fines = [fine_of(flags, c) for c in range(4)]
    zero_ref[...] = jnp.zeros((6, B, B), BF16)
    copies = []
    for c in range(4):
        e = 2 * c + fines[c]
        for block, to in ((all_ref.at[:, c], e), (zero_ref, 4 * c + 1 - e)):
            copies.append(pltpu.make_async_copy(block, interp_ref.at[:, to], sems.at[len(copies)]))
    for copy in copies[::2] + copies[1::2]:
        copy.start()
    parts = [[] for _ in range(4)]
    for c in range(4):
        z = fines[c]
        here = [(c, 1 - z, 4 + z, 5 - z, all_ref[5 - z, c])]
        if c > 0:
            here.append((c - 1, z, 3, 2, all_ref[2, c]))
        if c < 3:
            here.append((c + 1, z, 2, 3, all_ref[3, c]))
        found = contribs(
            diag_ref[2 * c + z], [fine_ref[d, c] for _, _, _, d, _ in here], [p for *_, p in here]
        )
        for (to, depth, back, _, interp), contrib in zip(here, found):
            product = mm(face_ref[back, 2 * to + depth], interp)
            parts[to].append((depth, contrib.astype(F32) + product))
    for c in range(4):
        for k in range(2):
            total = diag_ref[2 * c + k].astype(F32)
            for z, part in parts[c]:
                total = total + jnp.where(z == k, part, 0.0)
            sum_ref[2 * c + k] = total
    for c in range(4):
        far_ref[0, c], far_ref[1, c] = unfolded(ha, c), unfolded(hb, c)
    for copy in copies:
        copy.wait()


def bit_at(code, place):
    return lax.shift_right_logical(code, place) & 1


def computed(z, d, theirs, face, interp):
    return z, d, interp, contribs(theirs, [face], [interp])[0]


def from_four(z, d, sent, interp, c):
    theirs, face = sent[pl.ds(B * c, B), :], sent[pl.ds(B * (4 + c), B), :]
    return computed(z, d, theirs, face, interp[c])


def from_x(z, d, theirs, sent, interp, c):
    return computed(z, d, theirs, sent[pl.ds(FACES + B * c, B), :], interp[c])


def added(c, arrived, sum_ref, face_ref):
    totals = [sum_ref[2 * c], sum_ref[2 * c + 1]]
    for z, d, interp, contrib in arrived:
        part = contrib.astype(F32) + mm(face_ref[d, 2 * c + z], interp)
        totals = [total + jnp.where(z == k, part, 0.0) for k, total in enumerate(totals)]
    return totals


def middle_kernel(code_ref, sum_ref, face_ref, far_ref, ha, hz, xa_ref, z_ref, total_ref):
    gx, gz = lax.axis_index("gx"), lax.axis_index("gz")
    code = code_ref[...][0, 0]
    for c in range(4):
        arrived = [
            from_four(1 - gz, 5 - gz, hz, z_ref, c),
            from_x(bit_at(code, c), 1 - gx % 2, far_ref[0, c], ha, xa_ref, c),
        ]
        totals = added(c, arrived, sum_ref, face_ref)
        total_ref[2 * c], total_ref[2 * c + 1] = totals


def late_kernel(code_ref, sum_ref, face_ref, far_ref, hb, xb_ref, total_ref):
    gx = lax.axis_index("gx")
    code = code_ref[...][0, 0]
    for c in range(4):
        arrived = [from_x(bit_at(code, 4 + c), gx % 2, far_ref[1, c], hb, xb_ref, c)]
        totals = added(c, arrived, sum_ref, face_ref)
        total_ref[2 * c], total_ref[2 * c + 1] = totals


def coarse_kernel(
    split_ref, code_ref, sum_ref, face_ref, ya_ref, yb_ref, coarse_ref, total_ref, sems
):
    gy = lax.axis_index("gy")
    code = code_ref[...][0, 0]
    up = gy % 2 == 0
    flags = split_ref[...][0, 0]
    copies = []
    for c in (1, 2, 0, 3):
        arrived = []
        if c in (0, 3):
            first = up if c == 3 else jnp.logical_not(up)
            edge = 0 if c == 3 else 3
            z = jnp.where(first, bit_at(code, 8 + edge), bit_at(code, 12 + edge))
            pair = [jnp.where(first, ya_ref[k, 0], yb_ref[k, 0]) for k in range(2)]
            arrived.append((z, 3 if c == 3 else 2, *pair))
        totals = added(c, arrived, sum_ref, face_ref)
        for k in range(2):
            keep = split_at(flags, c, k) == 1
            total_ref[2 * c + k] = jnp.where(keep, totals[k], 0.0)
        pair = pl.ds(2 * c, 2)
        copies.append(
            pltpu.make_async_copy(total_ref.at[pair], coarse_ref.at[pair], sems.at[c])
        )
        copies[-1].start()
    for copy in copies:
        copy.wait()


def matching(size, start):
    pairs = [(i, i + 1) for i in range(start, size - 1, 2)]
    return pairs + [(b, a) for a, b in pairs]


def swap(x, axis, start):
    return lax.ppermute(x, axis, matching(lax.axis_size(axis), start))


def call(body, out_shape, in_specs, out_specs, scratch, flops):
    return pl.pallas_call(
        body,
        out_shape=out_shape,
        in_specs=in_specs,
        out_specs=out_specs,
        scratch_shapes=scratch,
        compiler_params=pltpu.CompilerParams(vmem_limit_bytes=LIMIT),
        cost_estimate=pl.CostEstimate(flops=flops, bytes_accessed=2 << 20, transcendentals=0),
    )


def on_device(diag_blocks, face_blocks, split):
    diag = diag_blocks.reshape(8, B, B)
    face = face_blocks.reshape(6, 8, B, B)
    split = jnp.transpose(split, (0, 2, 1))
    sds = jax.ShapeDtypeStruct
    dma = pltpu.SemaphoreType.DMA
    in_hbm = lambda x: pltpu.with_memory_space_constraint(x, pltpu.HBM)
    blocks = lambda *lead: sds(lead + (B, B), BF16)
    packed = lambda rows: sds((rows, B), BF16)
    facts, flags, diag, pa, pb, pz = call(
        facts_kernel,
        (
            sds((16, B), F32), sds((8, B), jnp.int32), blocks(8),
            packed(FACTS + 32), packed(FACTS + 32), packed(8 * B + 32),
        ),
        [HBM] * 3, (VMEM,) * 6,
        [
            pltpu.VMEM((16, B), F32), pltpu.SMEM((1, 2, 4), jnp.int32),
            pltpu.VMEM((2, 8, B, B), BF16), dma((7,)),
        ],
        1 << 20,
    )(in_hbm(split), in_hbm(diag), in_hbm(face))
    ha, hb = swap(pa, "gx", 0), swap(pb, "gx", 1)
    hc, hd = swap(facts, "gy", 0), swap(facts, "gy", 1)
    hz = swap(pz, "gz", 0)
    solved, fnorm, fine = call(
        inverse_kernel, (sds((6, 4, B, B), F32), sds((48, B), F32), blocks(6, 4)),
        [VMEM, VMEM, HBM], (VMEM, VMEM, VMEM),
        [
            pltpu.VMEM((3, 4, B, B), BF16), pltpu.VMEM((48, B), F32), pltpu.VMEM((2, B, B), F32),
            dma((4,)),
        ],
        1 << 30,
    )(flags, diag, in_hbm(face))
    code, xa, xb, ya, yb, z, both = call(
        interp_kernel,
        (
            sds((8, B), jnp.int32), blocks(4), blocks(4), blocks(2, 1), blocks(2, 1), blocks(4),
            blocks(6, 4),
        ),
        [VMEM] * 11, (VMEM,) * 7, [pltpu.VMEM((6, 8, B), F32)], 1 << 30,
    )(flags, diag, fine, solved, fnorm, facts, ha, hb, hc, hd, hz)
    xa, xb = swap(xa, "gx", 0), swap(xb, "gx", 1)
    ya, yb = swap(ya, "gy", 0), swap(yb, "gy", 1)
    z = swap(z, "gz", 0)
    total, interp, far = call(
        near_kernel, (sds((8, B, B), F32), blocks(6, 8), blocks(2, 4)), [VMEM] * 7,
        (VMEM, HBM, VMEM), [pltpu.VMEM((6, B, B), BF16), dma((8,))], 1 << 30,
    )(flags, diag, face, fine, both, ha, hb)
    total = call(
        middle_kernel, sds((8, B, B), F32), [VMEM] * 8, VMEM, [], 1 << 30,
    )(code, total, face, far, ha, hz, xa, z)
    total = call(
        late_kernel, sds((8, B, B), F32), [VMEM] * 6, VMEM, [], 1 << 30,
    )(code, total, face, far, hb, xb)
    coarse = call(
        coarse_kernel, sds((8, B, B), F32), [VMEM] * 6, HBM,
        [pltpu.VMEM((8, B, B), F32), dma((4,))], 1 << 30,
    )(flags, code, total, face, ya, yb)
    return interp.reshape(face_blocks.shape), coarse.reshape(diag_blocks.shape)


def solution(mesh):
    in_specs = (
        P("gx", "gy", "gz", None, None),
        P(None, "gx", "gy", "gz", None, None),
        P("gx", "gy", "gz"),
    )
    out_specs = (P(None, "gx", "gy", "gz", None, None), P("gx", "gy", "gz", None, None))
    return jax.shard_map(
        on_device, mesh=mesh, in_specs=in_specs, out_specs=out_specs, check_vma=False
    )
```

```python
import jax
import jax.numpy as jnp
from jax import lax
from jax.experimental import pallas as pl
from jax.experimental.pallas import tpu as pltpu
from jax.sharding import PartitionSpec as P


B = 128
F32 = jnp.float32
BF16 = jnp.bfloat16
VMEM = pl.BlockSpec(memory_space=pltpu.VMEM)
HBM = pl.BlockSpec(memory_space=pltpu.HBM)
LIMIT = 24 * 1024 * 1024
HALF = 64
FACES = 272
FACTS = 784


def mm(a, b):
    return jnp.dot(a, b, preferred_element_type=F32)


def mm32(a, b):
    return jnp.dot(a, b, preferred_element_type=F32, precision=lax.Precision.HIGHEST)


def halves(x):
    hi = x.astype(BF16)
    return hi, (x - hi.astype(F32)).astype(BF16)


def thirds(x):
    hi = x.astype(BF16)
    rest = x - hi.astype(F32)
    mid = rest.astype(BF16)
    return hi, mid, (rest - mid.astype(F32)).astype(BF16)


def wide(x):
    return jnp.concatenate([x, x], axis=0)


def split_at(flags, c, z):
    return lax.shift_right_logical(flags, 2 * c + z) & 1


def fine_of(flags, c):
    return split_at(flags, c, 0)


def square_sums(x):
    x = x.astype(F32)
    return jnp.sum(x * x, axis=0, keepdims=True)


def norms_of(rows):
    return jnp.broadcast_to(jnp.sqrt(jnp.sum(rows, axis=1, keepdims=True)), rows.shape)


def facts_kernel(
    split_ref, diag_ref, face_ref,
    facts_ref, flags_ref, kept_ref, xa_ref, xb_ref, z_ref, rows, held, faces, sems,
):
    gx, gz = lax.axis_index("gx"), lax.axis_index("gz")
    copies = [
        pltpu.make_async_copy(split_ref, held, sems.at[0]),
        pltpu.make_async_copy(diag_ref, kept_ref, sems.at[1]),
        pltpu.make_async_copy(face_ref.at[pl.ds(0, 2)], faces, sems.at[2]),
    ]
    for c in range(4):
        block, into = face_ref.at[5 - gz, 2 * c + 1 - gz], z_ref.at[pl.ds(B * (4 + c), B), :]
        copies.append(pltpu.make_async_copy(block, into, sems.at[3 + c]))
    for copy in copies:
        copy.start()
    copies[0].wait()
    row = lax.broadcasted_iota(jnp.int32, (8, B), 0)
    splits = [held[0, e % 2, e // 2] for e in range(8)]
    flags = jnp.zeros((8, B), F32)
    code = 0
    for e, split in enumerate(splits):
        flags = jnp.where(row == e, split.astype(F32), flags)
        code = code + split * (1 << e)
    flags_ref[...] = jnp.full((8, B), code, jnp.int32)
    facts_ref[pl.ds(8, 8), :] = flags
    copies[1].wait()
    for e in range(8):
        rows[pl.ds(e, 1), :] = square_sums(kept_ref[e])
    norms = norms_of(rows[pl.ds(0, 8), :])
    facts_ref[pl.ds(0, 8), :] = norms
    parts = [part.astype(F32) for part in thirds(norms)] + [flags]
    for ref, start in ((xa_ref, FACTS), (xb_ref, FACTS), (z_ref, 8 * B)):
        for k in range(2):
            both = jnp.concatenate(parts[2 * k:2 * k + 2], axis=0)
            ref[pl.ds(start + 16 * k, 16), :] = both.astype(BF16)
    row = lax.broadcasted_iota(jnp.int32, (HALF, B), 0)
    lane = lax.broadcasted_iota(jnp.int32, (HALF, B), 1)
    rows[pl.ds(8, 8), :] = jnp.zeros((8, B), F32)
    for c in range(4):
        block = kept_ref[2 * c + splits[2 * c]].astype(F32)
        top, bottom = block[:HALF], block[HALF:]
        folded = jnp.where((lane >= HALF) | (row >= lane), top, pltpu.roll(bottom, HALF, 1))
        folded = folded.astype(BF16)
        rows[pl.ds(8 + c, 1), :] = jnp.sum(
            jnp.where(row == lane - HALF, bottom, 0.0), axis=0, keepdims=True
        )
        for ref in (xa_ref, xb_ref):
            ref[pl.ds(HALF * c, HALF), :] = folded
    tail = jnp.concatenate([rows[pl.ds(8, 8), :], jnp.zeros((8, B), F32)], axis=0).astype(BF16)
    for ref in (xa_ref, xb_ref):
        ref[pl.ds(4 * HALF, 16), :] = tail
    for copy in copies[2:]:
        copy.wait()
    for c in range(4):
        e = 2 * c + splits[2 * c]
        z_ref[pl.ds(B * c, B), :] = kept_ref[2 * c + 1 - gz]
        for ref, d in ((xa_ref, 1 - gx % 2), (xb_ref, gx % 2)):
            ref[pl.ds(FACES + B * c, B), :] = faces[d, e]


def unfolded(ref, c):
    row = lax.broadcasted_iota(jnp.int32, (HALF, B), 0)
    lane = lax.broadcasted_iota(jnp.int32, (HALF, B), 1)
    folded = ref[pl.ds(HALF * c, HALF), :].astype(F32)
    turned = jnp.transpose(jnp.concatenate([folded, folded], axis=0))
    corner = ref[pl.ds(4 * HALF, 16), :].astype(F32)[c:c + 1]
    top = jnp.where((lane >= HALF) | (row >= lane), folded, turned[:HALF])
    low = jnp.where(row < lane - HALF, pltpu.roll(folded, HALF, 1), turned[:HALF])
    low = jnp.where(row == lane - HALF, corner, low)
    bottom = jnp.where(lane < HALF, turned[HALF:], low)
    return jnp.concatenate([top, bottom], axis=0).astype(BF16)


def facts_in(ref, start):
    high, low = ref[pl.ds(start, 16), :].astype(F32), ref[pl.ds(start + 16, 16), :].astype(F32)
    return high[:8] + high[8:] + low[:8], low[8:]


def scaling(a, eye):
    picked = jnp.where(eye, a, 0.0)
    down = lax.rsqrt(jnp.sum(picked, axis=1, keepdims=True))
    along = lax.rsqrt(jnp.sum(picked, axis=0, keepdims=True))
    a = a * down * along
    bound = jnp.max(jnp.sum(jnp.abs(a), axis=0, keepdims=True), axis=1, keepdims=True)
    return a, down, along, 1.9 / bound


def inverse_kernel(
    split_ref, diag_ref, face_ref, solved_ref, fnorm_ref, fine_ref, inv_ref, rows, work, sems
):
    cols = range(4)
    flags = split_ref[...][0, 0]
    copies = []
    for c in cols:
        e = 2 * c + fine_of(flags, c)
        copies.append(pltpu.make_async_copy(face_ref.at[:, e], fine_ref.at[:, c], sems.at[c]))
        copies[-1].start()
    eye = (
        lax.broadcasted_iota(jnp.int32, (B, B), 0) == lax.broadcasted_iota(jnp.int32, (B, B), 1)
    )
    one = jnp.where(eye, 1.0, 0.0).astype(F32)
    mats = [diag_ref[2 * c + fine_of(flags, c)] for c in cols]
    parts = [scaling(m.astype(F32), eye) for m in mats]
    powers = [one - start * a for a, _, _, start in parts]
    sums = [one + p for p in powers]
    powers = [p.astype(BF16) for p in powers]
    for _ in range(3):
        powers = [mm(p, p).astype(BF16) for p in powers]
        sums = [s + mm(s.astype(BF16), p) for s, p in zip(sums, powers)]
    guess = [
        (s * (start * down) * along).astype(BF16) for s, (_, down, along, start) in zip(sums, parts)
    ]
    left = [one - mm(mats[c], guess[c]) for c in cols]
    small = [r.astype(BF16) for r in left]
    left = [r + mm(b, b) for r, b in zip(left, small)]
    better = []
    for c in cols:
        hi, lo = halves(left[c])
        better.append(guess[c].astype(F32) + (mm(guess[c], hi) + mm(guess[c], lo)))
    pairs = [halves(x) for x in better]
    left = [one - (mm(mats[c], pairs[c][0]) + mm(mats[c], pairs[c][1])) for c in cols]
    worst = jnp.zeros((1, B), F32)
    for c in cols:
        hi, lo = pairs[c]
        rhi, rlo = halves(left[c])
        fixed = (hi.astype(F32) + lo.astype(F32)) + (mm(hi, rhi) + (mm(hi, rlo) + mm(lo, rhi)))
        inv_ref[0, c], inv_ref[1, c], inv_ref[2, c] = thirds(fixed)
        worst = worst + jnp.sum(jnp.abs(left[c]), axis=0, keepdims=True)
    for copy in copies:
        copy.wait()
    for d in range(6):
        for c in cols:
            sums = square_sums(fine_ref[d, c])
            rows[pl.ds(8 * d + 2 * c, 1), :] = sums
            rows[pl.ds(8 * d + 2 * c + 1, 1), :] = sums
    fnorm_ref[...] = norms_of(rows[...])

    def solve():
        for c in cols:
            inv = jnp.concatenate([inv_ref[0, c], inv_ref[1, c]], axis=1)
            last = inv_ref[2, c]
            for d in (0, 2, 4):
                face = jnp.concatenate([fine_ref[d, c], fine_ref[d + 1, c]], axis=1)
                both = mm(inv, wide(face)) + mm(last, face)
                solved_ref[d, c] = both[:, :B]
                solved_ref[d + 1, c] = both[:, B:]

    solve()
    reached = jnp.max(worst) <= 1e-3

    @pl.when(jnp.logical_not(reached))
    def _():
        for c in cols:
            a, down, along, start = scaling(mats[c].astype(F32), eye)
            work[0] = a
            work[1] = one * start

            @pl.loop(0, 48)
            def _(_):
                x = work[1]
                work[1] = x + mm32(x, one - mm32(work[0], x))

            inv_ref[0, c], inv_ref[1, c], inv_ref[2, c] = thirds(work[1] * down * along)
        solve()


def shifted(own, beyond, step, edge):
    return jnp.where(edge, pltpu.roll(beyond, step, 0), pltpu.roll(own, step, 0))


def weights_of(facts_ref, halo_refs, fnorm_ref, weight_ref):
    gx, gy, gz = lax.axis_index("gx"), lax.axis_index("gy"), lax.axis_index("gz")
    ha, hb, hc, hd, hz = halo_refs
    row = lax.broadcasted_iota(jnp.int32, (8, B), 0)
    depth = row % 2
    even_x, even_y = gx % 2 == 0, gy % 2 == 0

    xa, xb, beyond = facts_in(ha, FACTS), facts_in(hb, FACTS), facts_in(hz, 8 * B)
    ya, yb = (hc[pl.ds(0, 8), :], hc[pl.ds(8, 8), :]), (hd[pl.ds(0, 8), :], hd[pl.ds(8, 8), :])

    def neighbours(part):
        own = facts_ref[pl.ds(8 * part, 8), :]
        z = beyond[part]
        return (
            jnp.where(even_x, xb[part], xa[part]),
            jnp.where(even_x, xa[part], xb[part]),
            shifted(own, jnp.where(even_y, yb[part], ya[part]), 2, row < 2),
            shifted(own, jnp.where(even_y, ya[part], yb[part]), 6, row >= 6),
            jnp.where(depth == 0, pltpu.roll(z, 7, 0), pltpu.roll(own, 1, 0)),
            jnp.where(depth == 1, pltpu.roll(z, 1, 0), pltpu.roll(own, 7, 0)),
        )

    present = (
        jnp.broadcast_to(gx > 0, (8, B)),
        jnp.broadcast_to(gx < lax.axis_size("gx") - 1, (8, B)),
        (row >= 2) | (gy > 0),
        (row < 6) | (gy < lax.axis_size("gy") - 1),
        (depth == 1) | (gz > 0),
        (depth == 0) | (gz < lax.axis_size("gz") - 1),
    )
    own_norm = facts_ref[pl.ds(0, 8), :]
    fine = facts_ref[pl.ds(8, 8), :] < 0.5
    norms, splits = neighbours(0), neighbours(1)
    total = jnp.zeros((8, B), F32)
    denom = jnp.zeros((8, B), F32)
    links = []
    for d in range(6):
        other = jnp.where(present[d], norms[d], 1.0)
        strength = jnp.where(present[d], fnorm_ref[pl.ds(8 * d, 8), :] / jnp.sqrt(own_norm * other), 0.0)
        linked = present[d] & (splits[d] > 0.5)
        total = total + strength
        denom = denom + jnp.where(linked, strength, 0.0)
        links.append(linked)
    ratio = total / jnp.where(fine, denom, 1.0)
    for d in range(6):
        weight_ref[d] = jnp.where(links[d] & fine, -ratio, 0.0)


def interp_kernel(
    split_ref, diag_ref, fine_ref, solved_ref, fnorm_ref, facts_ref, ha, hb, hc, hd, hz,
    code_ref, xa_ref, xb_ref, ya_ref, yb_ref, z_ref, all_ref, weight_ref,
):
    gx, gy = lax.axis_index("gx"), lax.axis_index("gy")
    flags = split_ref[...][0, 0]
    fines = [fine_of(flags, c) for c in range(4)]
    weights_of(facts_ref, (ha, hb, hc, hd, hz), fnorm_ref, weight_ref)

    even_x = gx % 2 == 0
    for c in range(4):
        for d in range(6):
            weight = weight_ref[d, pl.ds(2 * c + fines[c], 1), :]
            all_ref[d, c] = (weight * solved_ref[d, c]).astype(BF16)
        low, high = all_ref[0, c], all_ref[1, c]
        xa_ref[c] = jnp.where(even_x, high, low)
        xb_ref[c] = jnp.where(even_x, low, high)
        z_ref[c] = all_ref[4 + fines[c], c]
    row = lax.broadcasted_iota(jnp.int32, (8, B), 0)
    lane = lax.broadcasted_iota(jnp.int32, (8, B), 1)
    bit = jnp.where((row % 2 == 0) & (lane == 0), 1, 0) * lax.shift_left(1, row // 2)
    code = jnp.zeros((8, B), F32)
    splits = [facts_in(ha, FACTS)[1], facts_in(hb, FACTS)[1], hc[pl.ds(8, 8), :], hd[pl.ds(8, 8), :]]
    for place, theirs in enumerate(splits):
        code = code + theirs * (bit * (1 << (4 * place))).astype(F32)
    code = jnp.sum(jnp.sum(code, axis=0, keepdims=True), axis=1, keepdims=True)
    code_ref[...] = jnp.broadcast_to(code, (8, B)).astype(jnp.int32)
    up = gy % 2 == 0
    low, high = all_ref[2, 0], all_ref[3, 3]
    ya_ref[0, 0], yb_ref[0, 0] = jnp.where(up, high, low), jnp.where(up, low, high)
    low = contribs(diag_ref[fines[0]], [fine_ref[2, 0]], [low])[0]
    high = contribs(diag_ref[6 + fines[3]], [fine_ref[3, 3]], [high])[0]
    ya_ref[1, 0], yb_ref[1, 0] = jnp.where(up, high, low), jnp.where(up, low, high)


def contribs(a, faces, interps):
    found = []
    for s in range(0, len(faces), 2):
        pair = interps[s:s + 2]
        face = jnp.concatenate(faces[s:s + 2], axis=1)
        hi, lo = halves(mm(a, jnp.concatenate(pair, axis=1)) + face.astype(F32))
        for t, interp in enumerate(pair):
            lanes = slice(B * t, B * t + B)
            turned = jnp.transpose(interp)
            both = jnp.concatenate([turned, turned], axis=1)
            mixed = jnp.concatenate([hi[:, lanes], lo[:, lanes]], axis=0)
            found.append(mm(both, mixed).astype(BF16))
    return found


def near_kernel(
    split_ref, diag_ref, face_ref, fine_ref, all_ref, ha, hb, sum_ref, interp_ref, far_ref,
    zero_ref, sems,
):
    flags = split_ref[...][0, 0]
    fines = [fine_of(flags, c) for c in range(4)]
    zero_ref[...] = jnp.zeros((6, B, B), BF16)
    copies = []
    for c in range(4):
        e = 2 * c + fines[c]
        for block, to in ((all_ref.at[:, c], e), (zero_ref, 4 * c + 1 - e)):
            copies.append(pltpu.make_async_copy(block, interp_ref.at[:, to], sems.at[len(copies)]))
    for copy in copies[::2] + copies[1::2]:
        copy.start()
    parts = [[] for _ in range(4)]
    for c in range(4):
        z = fines[c]
        here = [(c, 1 - z, 4 + z, 5 - z, all_ref[5 - z, c])]
        if c > 0:
            here.append((c - 1, z, 3, 2, all_ref[2, c]))
        if c < 3:
            here.append((c + 1, z, 2, 3, all_ref[3, c]))
        found = contribs(
            diag_ref[2 * c + z], [fine_ref[d, c] for _, _, _, d, _ in here], [p for *_, p in here]
        )
        for (to, depth, back, _, interp), contrib in zip(here, found):
            product = mm(face_ref[back, 2 * to + depth], interp)
            parts[to].append((depth, contrib.astype(F32) + product))
    for c in range(4):
        for k in range(2):
            total = diag_ref[2 * c + k].astype(F32)
            for z, part in parts[c]:
                total = total + jnp.where(z == k, part, 0.0)
            sum_ref[2 * c + k] = total
    for c in range(4):
        far_ref[0, c], far_ref[1, c] = unfolded(ha, c), unfolded(hb, c)
    for copy in copies:
        copy.wait()


def bit_at(code, place):
    return lax.shift_right_logical(code, place) & 1


def computed(z, d, theirs, face, interp):
    return z, d, interp, contribs(theirs, [face], [interp])[0]


def from_four(z, d, sent, interp, c):
    theirs, face = sent[pl.ds(B * c, B), :], sent[pl.ds(B * (4 + c), B), :]
    return computed(z, d, theirs, face, interp[c])


def from_x(z, d, theirs, sent, interp, c):
    return computed(z, d, theirs, sent[pl.ds(FACES + B * c, B), :], interp[c])


def added(c, arrived, sum_ref, face_ref):
    totals = [sum_ref[2 * c], sum_ref[2 * c + 1]]
    for z, d, interp, contrib in arrived:
        part = contrib.astype(F32) + mm(face_ref[d, 2 * c + z], interp)
        totals = [total + jnp.where(z == k, part, 0.0) for k, total in enumerate(totals)]
    return totals


def middle_kernel(code_ref, sum_ref, face_ref, far_ref, ha, hz, xa_ref, z_ref, total_ref):
    gx, gz = lax.axis_index("gx"), lax.axis_index("gz")
    code = code_ref[...][0, 0]
    for c in range(4):
        arrived = [
            from_four(1 - gz, 5 - gz, hz, z_ref, c),
            from_x(bit_at(code, c), 1 - gx % 2, far_ref[0, c], ha, xa_ref, c),
        ]
        totals = added(c, arrived, sum_ref, face_ref)
        total_ref[2 * c], total_ref[2 * c + 1] = totals


def late_kernel(
    split_ref, code_ref, sum_ref, face_ref, far_ref, hb, xb_ref, total_ref, coarse_ref, done_ref, sems
):
    gx = lax.axis_index("gx")
    code = code_ref[...][0, 0]
    flags = split_ref[...][0, 0]
    for c in (1, 2, 0, 3):
        arrived = [from_x(bit_at(code, 4 + c), gx % 2, far_ref[1, c], hb, xb_ref, c)]
        totals = added(c, arrived, sum_ref, face_ref)
        for k in range(2):
            if c in (1, 2):
                keep = split_at(flags, c, k) == 1
                done_ref[2 * c + k - 2] = jnp.where(keep, totals[k], 0.0)
            else:
                total_ref[2 * (c // 3) + k] = totals[k]
        if c == 2:
            copy = pltpu.make_async_copy(done_ref, coarse_ref.at[pl.ds(2, 4)], sems.at[0])
            copy.start()
    copy.wait()


def coarse_kernel(
    split_ref, code_ref, sum_ref, face_ref, ya_ref, yb_ref, part_ref, coarse_ref, total_ref, sems
):
    gy = lax.axis_index("gy")
    code = code_ref[...][0, 0]
    up = gy % 2 == 0
    flags = split_ref[...][0, 0]
    copies = []
    for c in (0, 3):
        first = up if c == 3 else jnp.logical_not(up)
        edge = 0 if c == 3 else 3
        z = jnp.where(first, bit_at(code, 8 + edge), bit_at(code, 12 + edge))
        interp, contrib = (jnp.where(first, ya_ref[k, 0], yb_ref[k, 0]) for k in range(2))
        product = mm(face_ref[3 if c == 3 else 2, 2 * c + z], interp)
        part = contrib.astype(F32) + product
        for k in range(2):
            place = 2 * (c // 3) + k
            total = sum_ref[place] + jnp.where(z == k, part, 0.0)
            keep = split_at(flags, c, k) == 1
            total_ref[place] = jnp.where(keep, total, 0.0)
        copies.append(
            pltpu.make_async_copy(
                total_ref.at[pl.ds(2 * (c // 3), 2)], coarse_ref.at[pl.ds(2 * c, 2)],
                sems.at[c // 3],
            )
        )
        copies[-1].start()
    for copy in copies:
        copy.wait()


def matching(size, start):
    pairs = [(i, i + 1) for i in range(start, size - 1, 2)]
    return pairs + [(b, a) for a, b in pairs]


def swap(x, axis, start):
    return lax.ppermute(x, axis, matching(lax.axis_size(axis), start))


def call(body, out_shape, in_specs, out_specs, scratch, flops, aliases={}):
    return pl.pallas_call(
        body,
        out_shape=out_shape,
        in_specs=in_specs,
        out_specs=out_specs,
        scratch_shapes=scratch,
        compiler_params=pltpu.CompilerParams(vmem_limit_bytes=LIMIT),
        cost_estimate=pl.CostEstimate(flops=flops, bytes_accessed=2 << 20, transcendentals=0),
        input_output_aliases=aliases,
    )


def on_device(diag_blocks, face_blocks, split):
    diag = diag_blocks.reshape(8, B, B)
    face = face_blocks.reshape(6, 8, B, B)
    split = jnp.transpose(split, (0, 2, 1))
    sds = jax.ShapeDtypeStruct
    dma = pltpu.SemaphoreType.DMA
    in_hbm = lambda x: pltpu.with_memory_space_constraint(x, pltpu.HBM)
    blocks = lambda *lead: sds(lead + (B, B), BF16)
    packed = lambda rows: sds((rows, B), BF16)
    facts, flags, diag, pa, pb, pz = call(
        facts_kernel,
        (
            sds((16, B), F32), sds((8, B), jnp.int32), blocks(8),
            packed(FACTS + 32), packed(FACTS + 32), packed(8 * B + 32),
        ),
        [HBM] * 3, (VMEM,) * 6,
        [
            pltpu.VMEM((16, B), F32), pltpu.SMEM((1, 2, 4), jnp.int32),
            pltpu.VMEM((2, 8, B, B), BF16), dma((7,)),
        ],
        1 << 20,
    )(in_hbm(split), in_hbm(diag), in_hbm(face))
    ha, hb = swap(pa, "gx", 0), swap(pb, "gx", 1)
    hc, hd = swap(facts, "gy", 0), swap(facts, "gy", 1)
    hz = swap(pz, "gz", 0)
    solved, fnorm, fine = call(
        inverse_kernel, (sds((6, 4, B, B), F32), sds((48, B), F32), blocks(6, 4)),
        [VMEM, VMEM, HBM], (VMEM, VMEM, VMEM),
        [
            pltpu.VMEM((3, 4, B, B), BF16), pltpu.VMEM((48, B), F32), pltpu.VMEM((2, B, B), F32),
            dma((4,)),
        ],
        1 << 30,
    )(flags, diag, in_hbm(face))
    code, xa, xb, ya, yb, z, both = call(
        interp_kernel,
        (
            sds((8, B), jnp.int32), blocks(4), blocks(4), blocks(2, 1), blocks(2, 1), blocks(4),
            blocks(6, 4),
        ),
        [VMEM] * 11, (VMEM,) * 7, [pltpu.VMEM((6, 8, B), F32)], 1 << 30,
    )(flags, diag, fine, solved, fnorm, facts, ha, hb, hc, hd, hz)
    xa, xb = swap(xa, "gx", 0), swap(xb, "gx", 1)
    ya, yb = swap(ya, "gy", 0), swap(yb, "gy", 1)
    z = swap(z, "gz", 0)
    total, interp, far = call(
        near_kernel, (sds((8, B, B), F32), blocks(6, 8), blocks(2, 4)), [VMEM] * 7,
        (VMEM, HBM, VMEM), [pltpu.VMEM((6, B, B), BF16), dma((8,))], 1 << 30,
    )(flags, diag, face, fine, both, ha, hb)
    total = call(
        middle_kernel, sds((8, B, B), F32), [VMEM] * 8, VMEM, [], 1 << 30,
    )(code, total, face, far, ha, hz, xa, z)
    total, coarse = call(
        late_kernel, (sds((4, B, B), F32), sds((8, B, B), F32)), [VMEM] * 7, (VMEM, HBM),
        [pltpu.VMEM((4, B, B), F32), dma((1,))], 1 << 30,
    )(flags, code, total, face, far, hb, xb)
    coarse = call(
        coarse_kernel, sds((8, B, B), F32), [VMEM] * 6 + [HBM], HBM,
        [pltpu.VMEM((4, B, B), F32), dma((2,))], 1 << 30, {6: 0},
    )(flags, code, total, face, ya, yb, coarse)
    return interp.reshape(face_blocks.shape), coarse.reshape(diag_blocks.shape)


def solution(mesh):
    in_specs = (
        P("gx", "gy", "gz", None, None),
        P(None, "gx", "gy", "gz", None, None),
        P("gx", "gy", "gz"),
    )
    out_specs = (P(None, "gx", "gy", "gz", None, None), P("gx", "gy", "gz", None, None))
    return jax.shard_map(
        on_device, mesh=mesh, in_specs=in_specs, out_specs=out_specs, check_vma=False
    )
```

```python
import jax
import jax.numpy as jnp
from jax import lax
from jax.experimental import pallas as pl
from jax.experimental.pallas import tpu as pltpu
from jax.sharding import PartitionSpec as P


B = 128
F32 = jnp.float32
BF16 = jnp.bfloat16
VMEM = pl.BlockSpec(memory_space=pltpu.VMEM)
HBM = pl.BlockSpec(memory_space=pltpu.HBM)
LIMIT = 24 * 1024 * 1024
HALF = 64
FACES = 272
FACTS = 784


def mm(a, b):
    return jnp.dot(a, b, preferred_element_type=F32)


def mm32(a, b):
    return jnp.dot(a, b, preferred_element_type=F32, precision=lax.Precision.HIGHEST)


def halves(x):
    hi = x.astype(BF16)
    return hi, (x - hi.astype(F32)).astype(BF16)


def thirds(x):
    hi = x.astype(BF16)
    rest = x - hi.astype(F32)
    mid = rest.astype(BF16)
    return hi, mid, (rest - mid.astype(F32)).astype(BF16)


def wide(x):
    return jnp.concatenate([x, x], axis=0)


def split_at(flags, c, z):
    return lax.shift_right_logical(flags, 2 * c + z) & 1


def fine_of(flags, c):
    return split_at(flags, c, 0)


def square_sums(x):
    x = x.astype(F32)
    return jnp.sum(x * x, axis=0, keepdims=True)


def norms_of(rows):
    return jnp.broadcast_to(jnp.sqrt(jnp.sum(rows, axis=1, keepdims=True)), rows.shape)


def facts_kernel(
    split_ref, diag_ref, face_ref,
    facts_ref, flags_ref, kept_ref, xa_ref, xb_ref, z_ref, rows, held, faces, sems,
):
    gx, gz = lax.axis_index("gx"), lax.axis_index("gz")
    copies = [
        pltpu.make_async_copy(split_ref, held, sems.at[0]),
        pltpu.make_async_copy(diag_ref.at[pl.ds(0, 4)], kept_ref.at[pl.ds(0, 4)], sems.at[1]),
        pltpu.make_async_copy(face_ref.at[pl.ds(0, 2)], faces, sems.at[2]),
    ]
    for c in range(4):
        block, into = face_ref.at[5 - gz, 2 * c + 1 - gz], z_ref.at[pl.ds(B * (4 + c), B), :]
        copies.append(pltpu.make_async_copy(block, into, sems.at[3 + c]))
    half = pltpu.make_async_copy(diag_ref.at[pl.ds(4, 4)], kept_ref.at[pl.ds(4, 4)], sems.at[7])
    for copy in copies[:2] + [half] + copies[2:]:
        copy.start()
    copies[0].wait()
    row = lax.broadcasted_iota(jnp.int32, (8, B), 0)
    splits = [held[0, e % 2, e // 2] for e in range(8)]
    flags = jnp.zeros((8, B), F32)
    code = 0
    for e, split in enumerate(splits):
        flags = jnp.where(row == e, split.astype(F32), flags)
        code = code + split * (1 << e)
    flags_ref[...] = jnp.full((8, B), code, jnp.int32)
    facts_ref[pl.ds(8, 8), :] = flags
    copies[1].wait()
    for e in range(8):
        if e == 4:
            half.wait()
        rows[pl.ds(e, 1), :] = square_sums(kept_ref[e])
    norms = norms_of(rows[pl.ds(0, 8), :])
    facts_ref[pl.ds(0, 8), :] = norms
    parts = [part.astype(F32) for part in thirds(norms)] + [flags]
    for ref, start in ((xa_ref, FACTS), (xb_ref, FACTS), (z_ref, 8 * B)):
        for k in range(2):
            both = jnp.concatenate(parts[2 * k:2 * k + 2], axis=0)
            ref[pl.ds(start + 16 * k, 16), :] = both.astype(BF16)
    row = lax.broadcasted_iota(jnp.int32, (HALF, B), 0)
    lane = lax.broadcasted_iota(jnp.int32, (HALF, B), 1)
    rows[pl.ds(8, 8), :] = jnp.zeros((8, B), F32)
    for c in range(4):
        block = kept_ref[2 * c + splits[2 * c]].astype(F32)
        top, bottom = block[:HALF], block[HALF:]
        folded = jnp.where((lane >= HALF) | (row >= lane), top, pltpu.roll(bottom, HALF, 1))
        folded = folded.astype(BF16)
        rows[pl.ds(8 + c, 1), :] = jnp.sum(
            jnp.where(row == lane - HALF, bottom, 0.0), axis=0, keepdims=True
        )
        for ref in (xa_ref, xb_ref):
            ref[pl.ds(HALF * c, HALF), :] = folded
    tail = jnp.concatenate([rows[pl.ds(8, 8), :], jnp.zeros((8, B), F32)], axis=0).astype(BF16)
    for ref in (xa_ref, xb_ref):
        ref[pl.ds(4 * HALF, 16), :] = tail
    for copy in copies[2:]:
        copy.wait()
    for c in range(4):
        e = 2 * c + splits[2 * c]
        z_ref[pl.ds(B * c, B), :] = kept_ref[2 * c + 1 - gz]
        for ref, d in ((xa_ref, 1 - gx % 2), (xb_ref, gx % 2)):
            ref[pl.ds(FACES + B * c, B), :] = faces[d, e]


def unfolded(ref, c):
    row = lax.broadcasted_iota(jnp.int32, (HALF, B), 0)
    lane = lax.broadcasted_iota(jnp.int32, (HALF, B), 1)
    folded = ref[pl.ds(HALF * c, HALF), :].astype(F32)
    turned = jnp.transpose(jnp.concatenate([folded, folded], axis=0))
    corner = ref[pl.ds(4 * HALF, 16), :].astype(F32)[c:c + 1]
    top = jnp.where((lane >= HALF) | (row >= lane), folded, turned[:HALF])
    low = jnp.where(row < lane - HALF, pltpu.roll(folded, HALF, 1), turned[:HALF])
    low = jnp.where(row == lane - HALF, corner, low)
    bottom = jnp.where(lane < HALF, turned[HALF:], low)
    return jnp.concatenate([top, bottom], axis=0).astype(BF16)


def facts_in(ref, start):
    high, low = ref[pl.ds(start, 16), :].astype(F32), ref[pl.ds(start + 16, 16), :].astype(F32)
    return high[:8] + high[8:] + low[:8], low[8:]


def scaling(a, eye):
    picked = jnp.where(eye, a, 0.0)
    down = lax.rsqrt(jnp.sum(picked, axis=1, keepdims=True))
    along = lax.rsqrt(jnp.sum(picked, axis=0, keepdims=True))
    a = a * down * along
    bound = jnp.max(jnp.sum(jnp.abs(a), axis=0, keepdims=True), axis=1, keepdims=True)
    return a, down, along, 1.9 / bound


def inverse_kernel(
    split_ref, diag_ref, face_ref, solved_ref, fnorm_ref, fine_ref, inv_ref, rows, work, sems
):
    cols = range(4)
    flags = split_ref[...][0, 0]
    copies = []
    for c in cols:
        e = 2 * c + fine_of(flags, c)
        copies.append(pltpu.make_async_copy(face_ref.at[:, e], fine_ref.at[:, c], sems.at[c]))
        copies[-1].start()
    eye = (
        lax.broadcasted_iota(jnp.int32, (B, B), 0) == lax.broadcasted_iota(jnp.int32, (B, B), 1)
    )
    one = jnp.where(eye, 1.0, 0.0).astype(F32)
    mats = [diag_ref[2 * c + fine_of(flags, c)] for c in cols]
    parts = [scaling(m.astype(F32), eye) for m in mats]
    powers = [one - start * a for a, _, _, start in parts]
    sums = [one + p for p in powers]
    powers = [p.astype(BF16) for p in powers]
    for _ in range(3):
        powers = [mm(p, p).astype(BF16) for p in powers]
        sums = [s + mm(s.astype(BF16), p) for s, p in zip(sums, powers)]
    guess = [
        (s * (start * down) * along).astype(BF16) for s, (_, down, along, start) in zip(sums, parts)
    ]
    left = [one - mm(mats[c], guess[c]) for c in cols]
    small = [r.astype(BF16) for r in left]
    left = [r + mm(b, b) for r, b in zip(left, small)]
    better = []
    for c in cols:
        hi, lo = halves(left[c])
        better.append(guess[c].astype(F32) + (mm(guess[c], hi) + mm(guess[c], lo)))
    pairs = [halves(x) for x in better]
    left = [one - (mm(mats[c], pairs[c][0]) + mm(mats[c], pairs[c][1])) for c in cols]
    worst = jnp.zeros((1, B), F32)
    for c in cols:
        hi, lo = pairs[c]
        rhi, rlo = halves(left[c])
        fixed = (hi.astype(F32) + lo.astype(F32)) + (mm(hi, rhi) + (mm(hi, rlo) + mm(lo, rhi)))
        inv_ref[0, c], inv_ref[1, c], inv_ref[2, c] = thirds(fixed)
        worst = worst + jnp.sum(jnp.abs(left[c]), axis=0, keepdims=True)
    for copy in copies:
        copy.wait()
    for d in range(6):
        for c in cols:
            sums = square_sums(fine_ref[d, c])
            rows[pl.ds(8 * d + 2 * c, 1), :] = sums
            rows[pl.ds(8 * d + 2 * c + 1, 1), :] = sums
    fnorm_ref[...] = norms_of(rows[...])

    def solve():
        for c in cols:
            inv = jnp.concatenate([inv_ref[0, c], inv_ref[1, c]], axis=1)
            last = inv_ref[2, c]
            for d in (0, 2, 4):
                face = jnp.concatenate([fine_ref[d, c], fine_ref[d + 1, c]], axis=1)
                both = mm(inv, wide(face)) + mm(last, face)
                solved_ref[d, c] = both[:, :B]
                solved_ref[d + 1, c] = both[:, B:]

    solve()
    reached = jnp.max(worst) <= 1e-3

    @pl.when(jnp.logical_not(reached))
    def _():
        for c in cols:
            a, down, along, start = scaling(mats[c].astype(F32), eye)
            work[0] = a
            work[1] = one * start

            @pl.loop(0, 48)
            def _(_):
                x = work[1]
                work[1] = x + mm32(x, one - mm32(work[0], x))

            inv_ref[0, c], inv_ref[1, c], inv_ref[2, c] = thirds(work[1] * down * along)
        solve()


def shifted(own, beyond, step, edge):
    return jnp.where(edge, pltpu.roll(beyond, step, 0), pltpu.roll(own, step, 0))


def weights_of(facts_ref, halo_refs, fnorm_ref, weight_ref):
    gx, gy, gz = lax.axis_index("gx"), lax.axis_index("gy"), lax.axis_index("gz")
    ha, hb, hc, hd, hz = halo_refs
    row = lax.broadcasted_iota(jnp.int32, (8, B), 0)
    depth = row % 2
    even_x, even_y = gx % 2 == 0, gy % 2 == 0

    xa, xb, beyond = facts_in(ha, FACTS), facts_in(hb, FACTS), facts_in(hz, 8 * B)
    ya, yb = (hc[pl.ds(0, 8), :], hc[pl.ds(8, 8), :]), (hd[pl.ds(0, 8), :], hd[pl.ds(8, 8), :])

    def neighbours(part):
        own = facts_ref[pl.ds(8 * part, 8), :]
        z = beyond[part]
        return (
            jnp.where(even_x, xb[part], xa[part]),
            jnp.where(even_x, xa[part], xb[part]),
            shifted(own, jnp.where(even_y, yb[part], ya[part]), 2, row < 2),
            shifted(own, jnp.where(even_y, ya[part], yb[part]), 6, row >= 6),
            jnp.where(depth == 0, pltpu.roll(z, 7, 0), pltpu.roll(own, 1, 0)),
            jnp.where(depth == 1, pltpu.roll(z, 1, 0), pltpu.roll(own, 7, 0)),
        )

    present = (
        jnp.broadcast_to(gx > 0, (8, B)),
        jnp.broadcast_to(gx < lax.axis_size("gx") - 1, (8, B)),
        (row >= 2) | (gy > 0),
        (row < 6) | (gy < lax.axis_size("gy") - 1),
        (depth == 1) | (gz > 0),
        (depth == 0) | (gz < lax.axis_size("gz") - 1),
    )
    own_norm = facts_ref[pl.ds(0, 8), :]
    fine = facts_ref[pl.ds(8, 8), :] < 0.5
    norms, splits = neighbours(0), neighbours(1)
    total = jnp.zeros((8, B), F32)
    denom = jnp.zeros((8, B), F32)
    links = []
    for d in range(6):
        other = jnp.where(present[d], norms[d], 1.0)
        strength = jnp.where(present[d], fnorm_ref[pl.ds(8 * d, 8), :] / jnp.sqrt(own_norm * other), 0.0)
        linked = present[d] & (splits[d] > 0.5)
        total = total + strength
        denom = denom + jnp.where(linked, strength, 0.0)
        links.append(linked)
    ratio = total / jnp.where(fine, denom, 1.0)
    for d in range(6):
        weight_ref[d] = jnp.where(links[d] & fine, -ratio, 0.0)


def interp_kernel(
    split_ref, diag_ref, fine_ref, solved_ref, fnorm_ref, facts_ref, ha, hb, hc, hd, hz,
    code_ref, xa_ref, xb_ref, ya_ref, yb_ref, z_ref, all_ref, weight_ref,
):
    gx, gy = lax.axis_index("gx"), lax.axis_index("gy")
    flags = split_ref[...][0, 0]
    fines = [fine_of(flags, c) for c in range(4)]
    weights_of(facts_ref, (ha, hb, hc, hd, hz), fnorm_ref, weight_ref)

    even_x = gx % 2 == 0
    for c in range(4):
        for d in range(6):
            weight = weight_ref[d, pl.ds(2 * c + fines[c], 1), :]
            all_ref[d, c] = (weight * solved_ref[d, c]).astype(BF16)
        low, high = all_ref[0, c], all_ref[1, c]
        xa_ref[c] = jnp.where(even_x, high, low)
        xb_ref[c] = jnp.where(even_x, low, high)
        z_ref[c] = all_ref[4 + fines[c], c]
    row = lax.broadcasted_iota(jnp.int32, (8, B), 0)
    lane = lax.broadcasted_iota(jnp.int32, (8, B), 1)
    bit = jnp.where((row % 2 == 0) & (lane == 0), 1, 0) * lax.shift_left(1, row // 2)
    code = jnp.zeros((8, B), F32)
    splits = [facts_in(ha, FACTS)[1], facts_in(hb, FACTS)[1], hc[pl.ds(8, 8), :], hd[pl.ds(8, 8), :]]
    for place, theirs in enumerate(splits):
        code = code + theirs * (bit * (1 << (4 * place))).astype(F32)
    code = jnp.sum(jnp.sum(code, axis=0, keepdims=True), axis=1, keepdims=True)
    code_ref[...] = jnp.broadcast_to(code, (8, B)).astype(jnp.int32)
    up = gy % 2 == 0
    low, high = all_ref[2, 0], all_ref[3, 3]
    ya_ref[0, 0], yb_ref[0, 0] = jnp.where(up, high, low), jnp.where(up, low, high)
    low = contribs(diag_ref[fines[0]], [fine_ref[2, 0]], [low])[0]
    high = contribs(diag_ref[6 + fines[3]], [fine_ref[3, 3]], [high])[0]
    ya_ref[1, 0], yb_ref[1, 0] = jnp.where(up, high, low), jnp.where(up, low, high)


def contribs(a, faces, interps):
    found = []
    for s in range(0, len(faces), 2):
        pair = interps[s:s + 2]
        face = jnp.concatenate(faces[s:s + 2], axis=1)
        hi, lo = halves(mm(a, jnp.concatenate(pair, axis=1)) + face.astype(F32))
        for t, interp in enumerate(pair):
            lanes = slice(B * t, B * t + B)
            turned = jnp.transpose(interp)
            both = jnp.concatenate([turned, turned], axis=1)
            mixed = jnp.concatenate([hi[:, lanes], lo[:, lanes]], axis=0)
            found.append(mm(both, mixed).astype(BF16))
    return found


def near_kernel(
    split_ref, diag_ref, face_ref, fine_ref, all_ref, ha, hb, sum_ref, interp_ref, far_ref,
    zero_ref, sems,
):
    flags = split_ref[...][0, 0]
    fines = [fine_of(flags, c) for c in range(4)]
    zero_ref[...] = jnp.zeros((6, B, B), BF16)
    copies = []
    for c in range(4):
        e = 2 * c + fines[c]
        for block, to in ((all_ref.at[:, c], e), (zero_ref, 4 * c + 1 - e)):
            copies.append(pltpu.make_async_copy(block, interp_ref.at[:, to], sems.at[len(copies)]))
    for copy in copies[::2] + copies[1::2]:
        copy.start()
    parts = [[] for _ in range(4)]
    for c in range(4):
        z = fines[c]
        here = [(c, 1 - z, 4 + z, 5 - z, all_ref[5 - z, c])]
        if c > 0:
            here.append((c - 1, z, 3, 2, all_ref[2, c]))
        if c < 3:
            here.append((c + 1, z, 2, 3, all_ref[3, c]))
        found = contribs(
            diag_ref[2 * c + z], [fine_ref[d, c] for _, _, _, d, _ in here], [p for *_, p in here]
        )
        for (to, depth, back, _, interp), contrib in zip(here, found):
            product = mm(face_ref[back, 2 * to + depth], interp)
            parts[to].append((depth, contrib.astype(F32) + product))
    for c in range(4):
        for k in range(2):
            total = diag_ref[2 * c + k].astype(F32)
            for z, part in parts[c]:
                total = total + jnp.where(z == k, part, 0.0)
            sum_ref[2 * c + k] = total
    for c in range(4):
        far_ref[0, c], far_ref[1, c] = unfolded(ha, c), unfolded(hb, c)
    for copy in copies:
        copy.wait()


def bit_at(code, place):
    return lax.shift_right_logical(code, place) & 1


def computed(z, d, theirs, face, interp):
    return z, d, interp, contribs(theirs, [face], [interp])[0]


def from_four(z, d, sent, interp, c):
    theirs, face = sent[pl.ds(B * c, B), :], sent[pl.ds(B * (4 + c), B), :]
    return computed(z, d, theirs, face, interp[c])


def from_x(z, d, theirs, sent, interp, c):
    return computed(z, d, theirs, sent[pl.ds(FACES + B * c, B), :], interp[c])


def added(c, arrived, sum_ref, face_ref):
    totals = [sum_ref[2 * c], sum_ref[2 * c + 1]]
    for z, d, interp, contrib in arrived:
        part = contrib.astype(F32) + mm(face_ref[d, 2 * c + z], interp)
        totals = [total + jnp.where(z == k, part, 0.0) for k, total in enumerate(totals)]
    return totals


def middle_kernel(code_ref, sum_ref, face_ref, far_ref, ha, hz, xa_ref, z_ref, total_ref):
    gx, gz = lax.axis_index("gx"), lax.axis_index("gz")
    code = code_ref[...][0, 0]
    for c in range(4):
        arrived = [
            from_four(1 - gz, 5 - gz, hz, z_ref, c),
            from_x(bit_at(code, c), 1 - gx % 2, far_ref[0, c], ha, xa_ref, c),
        ]
        totals = added(c, arrived, sum_ref, face_ref)
        total_ref[2 * c], total_ref[2 * c + 1] = totals


def late_kernel(code_ref, sum_ref, face_ref, far_ref, hb, xb_ref, total_ref):
    gx = lax.axis_index("gx")
    code = code_ref[...][0, 0]
    for c in range(4):
        arrived = [from_x(bit_at(code, 4 + c), gx % 2, far_ref[1, c], hb, xb_ref, c)]
        totals = added(c, arrived, sum_ref, face_ref)
        total_ref[2 * c], total_ref[2 * c + 1] = totals


def coarse_kernel(
    split_ref, code_ref, sum_ref, face_ref, ya_ref, yb_ref, coarse_ref, total_ref, sems
):
    gy = lax.axis_index("gy")
    code = code_ref[...][0, 0]
    up = gy % 2 == 0
    flags = split_ref[...][0, 0]
    copies = []
    for c in (1, 2, 0, 3):
        arrived = []
        if c in (0, 3):
            first = up if c == 3 else jnp.logical_not(up)
            edge = 0 if c == 3 else 3
            z = jnp.where(first, bit_at(code, 8 + edge), bit_at(code, 12 + edge))
            pair = [jnp.where(first, ya_ref[k, 0], yb_ref[k, 0]) for k in range(2)]
            arrived.append((z, 3 if c == 3 else 2, *pair))
        totals = added(c, arrived, sum_ref, face_ref)
        for k in range(2):
            keep = split_at(flags, c, k) == 1
            total_ref[2 * c + k] = jnp.where(keep, totals[k], 0.0)
        pair = pl.ds(2 * c, 2)
        copies.append(
            pltpu.make_async_copy(total_ref.at[pair], coarse_ref.at[pair], sems.at[c])
        )
        copies[-1].start()
    for copy in copies:
        copy.wait()


def matching(size, start):
    pairs = [(i, i + 1) for i in range(start, size - 1, 2)]
    return pairs + [(b, a) for a, b in pairs]


def swap(x, axis, start):
    return lax.ppermute(x, axis, matching(lax.axis_size(axis), start))


def call(body, out_shape, in_specs, out_specs, scratch, flops):
    return pl.pallas_call(
        body,
        out_shape=out_shape,
        in_specs=in_specs,
        out_specs=out_specs,
        scratch_shapes=scratch,
        compiler_params=pltpu.CompilerParams(vmem_limit_bytes=LIMIT),
        cost_estimate=pl.CostEstimate(flops=flops, bytes_accessed=2 << 20, transcendentals=0),
    )


def on_device(diag_blocks, face_blocks, split):
    diag = diag_blocks.reshape(8, B, B)
    face = face_blocks.reshape(6, 8, B, B)
    split = jnp.transpose(split, (0, 2, 1))
    sds = jax.ShapeDtypeStruct
    dma = pltpu.SemaphoreType.DMA
    in_hbm = lambda x: pltpu.with_memory_space_constraint(x, pltpu.HBM)
    blocks = lambda *lead: sds(lead + (B, B), BF16)
    packed = lambda rows: sds((rows, B), BF16)
    facts, flags, diag, pa, pb, pz = call(
        facts_kernel,
        (
            sds((16, B), F32), sds((8, B), jnp.int32), blocks(8),
            packed(FACTS + 32), packed(FACTS + 32), packed(8 * B + 32),
        ),
        [HBM] * 3, (VMEM,) * 6,
        [
            pltpu.VMEM((16, B), F32), pltpu.SMEM((1, 2, 4), jnp.int32),
            pltpu.VMEM((2, 8, B, B), BF16), dma((8,)),
        ],
        1 << 20,
    )(in_hbm(split), in_hbm(diag), in_hbm(face))
    ha, hb = swap(pa, "gx", 0), swap(pb, "gx", 1)
    hc, hd = swap(facts, "gy", 0), swap(facts, "gy", 1)
    hz = swap(pz, "gz", 0)
    solved, fnorm, fine = call(
        inverse_kernel, (sds((6, 4, B, B), F32), sds((48, B), F32), blocks(6, 4)),
        [VMEM, VMEM, HBM], (VMEM, VMEM, VMEM),
        [
            pltpu.VMEM((3, 4, B, B), BF16), pltpu.VMEM((48, B), F32), pltpu.VMEM((2, B, B), F32),
            dma((4,)),
        ],
        1 << 30,
    )(flags, diag, in_hbm(face))
    code, xa, xb, ya, yb, z, both = call(
        interp_kernel,
        (
            sds((8, B), jnp.int32), blocks(4), blocks(4), blocks(2, 1), blocks(2, 1), blocks(4),
            blocks(6, 4),
        ),
        [VMEM] * 11, (VMEM,) * 7, [pltpu.VMEM((6, 8, B), F32)], 1 << 30,
    )(flags, diag, fine, solved, fnorm, facts, ha, hb, hc, hd, hz)
    xa, xb = swap(xa, "gx", 0), swap(xb, "gx", 1)
    ya, yb = swap(ya, "gy", 0), swap(yb, "gy", 1)
    z = swap(z, "gz", 0)
    total, interp, far = call(
        near_kernel, (sds((8, B, B), F32), blocks(6, 8), blocks(2, 4)), [VMEM] * 7,
        (VMEM, HBM, VMEM), [pltpu.VMEM((6, B, B), BF16), dma((8,))], 1 << 30,
    )(flags, diag, face, fine, both, ha, hb)
    total = call(
        middle_kernel, sds((8, B, B), F32), [VMEM] * 8, VMEM, [], 1 << 30,
    )(code, total, face, far, ha, hz, xa, z)
    total = call(
        late_kernel, sds((8, B, B), F32), [VMEM] * 6, VMEM, [], 1 << 30,
    )(code, total, face, far, hb, xb)
    coarse = call(
        coarse_kernel, sds((8, B, B), F32), [VMEM] * 6, HBM,
        [pltpu.VMEM((8, B, B), F32), dma((4,))], 1 << 30,
    )(flags, code, total, face, ya, yb)
    return interp.reshape(face_blocks.shape), coarse.reshape(diag_blocks.shape)


def solution(mesh):
    in_specs = (
        P("gx", "gy", "gz", None, None),
        P(None, "gx", "gy", "gz", None, None),
        P("gx", "gy", "gz"),
    )
    out_specs = (P(None, "gx", "gy", "gz", None, None), P("gx", "gy", "gz", None, None))
    return jax.shard_map(
        on_device, mesh=mesh, in_specs=in_specs, out_specs=out_specs, check_vma=False
    )
```
